32 devices in a mesh: dp: 8 (over z, x), tensor: 4 (over y, core).
Axes of the slice: x: 2, y: 2, z: 4, core: 2. Of those that a mesh axis runs over, the one named last changes fastest.
Arguments:
- layer_in: bfloat16 [16384, 1024], P(('dp', 'tensor')), may hold values from -6 to 6
- cotangent: bfloat16 [16384, 1024], P(('dp', 'tensor')), may hold values from -6 to 6
- lengths: int32 [8], P('dp'), may hold values from 256 to 2048, as said below
- languages: int32 [8], P('dp'), may hold values from 0 to 45
- lang_weight: float32 [46], replicated, may hold values from 0.3 to 3
- ln1_gain: float32 [1024], replicated, may hold values from 0.5 to 1.5
- ln1_bias: float32 [1024], replicated, may hold values from -2.5 to 2.5
- w_qkv: bfloat16 [1024, 3072], P(None, 'tensor'), may hold values from -0.1875 to 0.1875
- b_qv: float32 [2048], P('tensor'), may hold values from -2.5 to 2.5
- w_out: bfloat16 [1024, 1024], P('tensor'), may hold values from -1.5 to 1.5
- b_out: float32 [1024], replicated, may hold values from -2.5 to 2.5
- ln2_gain: float32 [1024], replicated, may hold values from 0.5 to 1.5
- ln2_bias: float32 [1024], replicated, may hold values from -2.5 to 2.5
- w_up: bfloat16 [1024, 4096], P(None, 'tensor'), may hold values from -0.1875 to 0.1875
- b_up: float32 [4096], P('tensor'), may hold values from -2.5 to 2.5
- w_down: bfloat16 [4096, 1024], P('tensor'), may hold values from -0.09375 to 0.09375
- b_down: float32 [1024], replicated, may hold values from -2.5 to 2.5
Outputs:
- output: bfloat16 [16384, 1024], P(('dp', 'tensor'))
- grad_x: bfloat16 [16384, 1024], P(('dp', 'tensor'))
- g_ln1_gain: float32 [1024], replicated
- g_ln1_bias: float32 [1024], replicated
- g_w_qkv: float32 [1024, 3072], P(None, 'tensor')
- g_b_qv: float32 [2048], P('tensor')
- g_w_out: float32 [1024, 1024], P('tensor')
- g_b_out: float32 [1024], replicated
- g_ln2_gain: float32 [1024], replicated
- g_ln2_bias: float32 [1024], replicated
- g_w_up: float32 [1024, 4096], P(None, 'tensor')
- g_b_up: float32 [4096], P('tensor')
- g_w_down: float32 [4096, 1024], P('tensor')
- g_b_down: float32 [1024], replicated
The draws below stay inside these ranges and needn't reach their ends.
Inputs may be any that keep to these rules, and one draw needn't show every extreme that they name: `lengths`: rows of languages 0 to 7 have all 2048 tokens; some row has 2048 tokens and some row 256.
All inputs are finite; a program needn't handle non-finite values.
Results may differ from the reference program's by a relative error of at most 0.019.
Values may be sent and summed in bfloat16 or wider, within the bound.
No kernel may reach another device: no remote copies, remote signals or barrier semaphores. Data moves between devices by JAX's collectives and lax.ppermute only.
A program may use at most 192 MiB of HBM per device.

```python
import math
import jax
import jax.numpy as jnp
from jax import lax

D = 1024
HEADS = 16
HD = 64
FF = 4096
LANGS = 46
LEN = 2048
SEQS = 8
TOKENS = 16384
N_TENSOR = 4


def row_plan(key):
    base_key = jax.random.fold_in(key, 7)
    key_lang, key_len, key_pick = jax.random.split(base_key, 3)
    language_ids = jax.random.randint(key_lang, (SEQS,), 0, LANGS)
    row_spans = jax.random.randint(key_len, (SEQS,), LEN // 8, LEN + 1)
    chosen = jax.random.randint(key_pick, (), 0, SEQS)
    second = (chosen + SEQS // 2) % SEQS
    places = jnp.arange(SEQS)
    language_ids = jnp.where(places == chosen, 0, language_ids)
    language_ids = jnp.where(places == second, LANGS - 1, language_ids)
    row_spans = jnp.where(language_ids < 8, LEN, row_spans)
    row_spans = jnp.where(places == second, LEN // 8, row_spans)
    return (language_ids.astype(jnp.int32), row_spans.astype(jnp.int32))


def draw_lengths(key, part):
    return row_plan(key)[1]


def draw_languages(key, part):
    return row_plan(key)[0]


def level_of(stream_key, dims, cuts, smallest, largest):
    level, own = 1.0, jax.random.fold_in(stream_key, 6)
    for dim, blocks in cuts:
        draws = jnp.exp(jax.random.uniform(jax.random.fold_in(own, dim), (blocks,), jnp.float32, smallest / len(cuts), largest / len(cuts)))
        level = level * jnp.repeat(draws, dims[dim] // blocks).reshape([-1 if axis == dim else 1 for axis in range(len(dims))])
    return level


def centred(stream_key, extent, scale, reach, cuts=(), kind=jnp.bfloat16):
    array = scale * jax.random.normal(stream_key, extent, jnp.float32)
    if cuts:
        array = array * level_of(stream_key, extent, cuts, -0.22, 0.18)
    return jnp.clip(array, -reach, reach).astype(kind)


def setup_inputs(seed: int = 0) -> dict:
    key_of = jax.random.split(jax.random.key(seed), 18)
    return {
        "layer_in": centred(key_of[0], (TOKENS, D), 1.0, 6.0, ((0, 32),)),
        "cotangent": centred(key_of[1], (TOKENS, D), 1.0, 6.0, ((0, 32),)),
        "lengths": draw_lengths(jax.random.fold_in(key_of[17], 71), 0),
        "languages": draw_languages(jax.random.fold_in(key_of[17], 71), 0),
        "lang_weight": jnp.clip(jnp.exp(jax.random.uniform(key_of[4], (LANGS,), jnp.float32, math.log(0.3), math.log(3.0))), 0.3, 3.0),
        "ln1_gain": jnp.clip(1.0 + 0.1 * jax.random.normal(key_of[5], (D,), jnp.float32), 0.5, 1.5),
        "ln1_bias": centred(key_of[6], (D,), 0.3, 2.5, (), jnp.float32),
        "w_qkv": centred(key_of[7], (D, 3 * D), D ** -0.5, 0.1875, ((1, 4),)),
        "b_qv": centred(key_of[8], (2 * D,), 0.3, 2.5, ((0, 4),), jnp.float32),
        "w_out": centred(key_of[9], (D, D), 16 ** -0.5, 1.5, ((0, 4),)),
        "b_out": centred(key_of[10], (D,), 0.2, 2.5, (), jnp.float32),
        "ln2_gain": jnp.clip(1.0 + 0.1 * jax.random.normal(key_of[11], (D,), jnp.float32), 0.5, 1.5),
        "ln2_bias": centred(key_of[12], (D,), 0.3, 2.5, (), jnp.float32),
        "w_up": centred(key_of[13], (D, FF), D ** -0.5, 0.1875, ((1, 4),)),
        "b_up": centred(key_of[14], (FF,), 0.3, 2.5, ((0, 4),), jnp.float32),
        "w_down": centred(key_of[15], (FF, D), FF ** -0.5, 0.09375, ((0, 4),)),
        "b_down": centred(key_of[16], (D,), 0.2, 2.5, (), jnp.float32),
    }


@jax.custom_vjp
def low(v):
    return lax.optimization_barrier(v.astype(jnp.bfloat16)).astype(jnp.float32)

@jax.custom_vjp
def low_back(v):
    return v

def low_keep(v):
    return (low(v), None)

def low_pass(kept, grad):
    return (grad,)

def back_keep(v):
    return (v, None)

def back_low(kept, grad):
    return (low(grad),)
low.defvjp(low_keep, low_pass)
low_back.defvjp(back_keep, back_low)
highest = lax.Precision.HIGHEST
eps = 1e-05

def normalize(values, gain, bias):
    centre = lax.optimization_barrier(jnp.mean(values, axis=-1, keepdims=True))
    shifted = values - centre
    spread = lax.optimization_barrier(jnp.mean(shifted * shifted, axis=-1, keepdims=True))
    return shifted * lax.rsqrt(spread + eps) * gain + bias

def attend(query, keys, values, length):
    block = 512 if LEN % 512 == 0 else LEN
    starts = (jnp.arange(LEN // block) * block).astype(jnp.int32)
    head_ids = jnp.arange(HEADS).astype(jnp.float32)
    slopes = jnp.exp2(-8.0 * (head_ids + 1.0) / HEADS)
    key_pos = jnp.arange(LEN).astype(jnp.int32)
    scale = HD ** (-0.5)

    def one_block(start):
        query_block = lax.dynamic_slice_in_dim(query, start, block, 1)
        query_pos = start + jnp.arange(block).astype(jnp.int32)
        scores = jnp.einsum('hqe,hke->hqk', query_block, keys, precision=highest) * scale
        offsets = (key_pos[None, :] - query_pos[:, None]).astype(jnp.float32)
        scores = scores + slopes[:, None, None] * offsets[None]
        allowed = (key_pos[None, :] <= query_pos[:, None]) & (key_pos[None, :] < length)
        scores = low_back(jnp.where(allowed[None], scores, -jnp.inf))
        probs = low(jax.nn.softmax(scores, axis=-1))
        return jnp.einsum('hqk,hke->hqe', probs, values, precision=highest)
    blocks = lax.map(jax.checkpoint(one_block), starts)
    return blocks.transpose(1, 0, 2, 3).reshape(HEADS, LEN, HD)

def forward(rows, length, params):
    ln1_gain, ln1_bias, w_qkv, b_qv, w_out, b_out, ln2_gain, ln2_bias, w_up, b_up, w_down, b_down = params
    local_heads = HEADS // N_TENSOR
    width = FF // N_TENSOR
    normed = low(normalize(rows, ln1_gain, ln1_bias))
    shared = low_back(jnp.broadcast_to(normed, (N_TENSOR, LEN, D)))
    mixed = jnp.einsum('gtd,dgc->gtc', shared, w_qkv.reshape(D, N_TENSOR, local_heads * 3 * HD), precision=highest)
    mixed = mixed.reshape(N_TENSOR, LEN, local_heads, 3, HD).transpose(0, 2, 1, 3, 4).reshape(HEADS, LEN, 3, HD)
    pair = b_qv.reshape(HEADS, 2, HD)
    bias_three = jnp.stack([pair[:, 0], jnp.zeros_like(pair[:, 0]), pair[:, 1]], axis=1)
    mixed = low(low_back(mixed + bias_three[:, None]))
    heads_out = attend(mixed[:, :, 0], mixed[:, :, 1], mixed[:, :, 2], length)
    heads_out = low(low_back(heads_out))
    grouped = heads_out.reshape(N_TENSOR, local_heads, LEN, HD).transpose(0, 2, 1, 3).reshape(N_TENSOR, LEN, local_heads * HD)
    attn_parts = jnp.einsum('gtc,gcd->gtd', grouped, w_out.reshape(N_TENSOR, local_heads * HD, D), precision=highest)
    middle = rows + low_back(lax.optimization_barrier(jnp.sum(low(attn_parts), axis=0))) + b_out
    normed_mid = low(normalize(middle, ln2_gain, ln2_bias))
    shared_mid = low_back(jnp.broadcast_to(normed_mid, (N_TENSOR, LEN, D)))
    pre_act = jnp.einsum('gtd,dgf->gtf', shared_mid, w_up.reshape(D, N_TENSOR, width), precision=highest)
    pre_act = low_back(pre_act + b_up.reshape(N_TENSOR, 1, width))
    active = low(jax.nn.gelu(pre_act, approximate=True))
    mlp_parts = jnp.einsum('gtf,gfd->gtd', active, w_down.reshape(N_TENSOR, width, D), precision=highest)
    return middle + low_back(lax.optimization_barrier(jnp.sum(low(mlp_parts), axis=0))) + b_down

def reference(layer_in, cotangent, lengths, languages, lang_weight, ln1_gain, ln1_bias, w_qkv, b_qv, w_out, b_out, ln2_gain, ln2_bias, w_up, b_up, w_down, b_down):
    params = tuple((item.astype(jnp.float32) for item in (ln1_gain, ln1_bias, w_qkv, b_qv, w_out, b_out, ln2_gain, ln2_bias, w_up, b_up, w_down, b_down)))
    inputs = layer_in.astype(jnp.float32).reshape(SEQS, LEN, D)
    grads_top = cotangent.astype(jnp.float32).reshape(SEQS, LEN, D)

    def one_sequence(totals, item):
        rows, grad_rows, length, language = item
        weight = jnp.sum(jnp.where(jnp.arange(LANGS) == language, lang_weight, 0.0))
        live = jnp.where(jnp.arange(LEN) < length, weight, 0.0)
        result, pull_back = jax.vjp(lambda values, weights: forward(values, length, weights), rows, params)
        grad_input, grad_params = pull_back(grad_rows * live[:, None])
        totals = jax.tree.map(lambda first, second: first + second, totals, grad_params)
        return (totals, (result.astype(jnp.bfloat16), grad_input.astype(jnp.bfloat16)))
    zeros = tuple((jnp.zeros(item.shape, jnp.float32) for item in params))
    totals, (results, grad_inputs) = lax.scan(one_sequence, zeros, (inputs, grads_top, lengths, languages))
    return (results.reshape(TOKENS, D), grad_inputs.reshape(TOKENS, D), totals[0], totals[1], totals[2], totals[3], totals[4], totals[5], totals[6], totals[7], totals[8], totals[9], totals[10], totals[11])
```

```python
import functools
import jax
import jax.numpy as jnp
from jax import lax
from jax.sharding import PartitionSpec as P
from jax.experimental import pallas as pl
from jax.experimental.pallas import tpu as pltpu

HEADS = 16
HD = 64
LANES = 128
F32 = jnp.float32
BF16 = jnp.bfloat16


def split3(x):
    hi = x.astype(BF16)
    rest = x - hi.astype(F32)
    mid = rest.astype(BF16)
    low = (rest - mid.astype(F32)).astype(BF16)
    return hi.astype(F32), mid.astype(F32), low.astype(F32)


def nt(a, b):
    return lax.dot_general(a, b, (((1,), (1,)), ((), ())), preferred_element_type=F32)


def nn(a, b):
    return jnp.dot(a, b, preferred_element_type=F32)


def at_lanes(lane, base, pairs):
    out = base
    for where, value in pairs:
        out = jnp.where(lane == where, value, out)
    return out


def key_side(span, length):
    pos = lax.broadcasted_iota(jnp.int32, (span, LANES), 0)
    lane = lax.broadcasted_iota(jnp.int32, (span, LANES), 1)
    low = (pos & 255).astype(F32)
    high = (pos - (pos & 255)).astype(F32)
    is_high = (lane == 64) | (lane == 66) | (lane == 68)
    is_low = (lane == 65) | (lane == 67) | (lane == 69)
    gone = jnp.where(pos < length, 0.0, -1e30)
    out = jnp.where(is_high, high, jnp.where(is_low, low, 0.0))
    out = jnp.where(lane == 70, gone, out)
    return jnp.where((lane >= 71) & (lane <= 73), 1.0, out)


def slope_side(lane, slope_parts):
    s1, s2, s3 = slope_parts
    out = jnp.where(lane < 66, s1, jnp.where(lane < 68, s2, s3))
    out = jnp.where(lane == 70, 1.0, out)
    return jnp.where((lane >= 64) & (lane <= 70), out, 0.0)


def wide(x):
    return jnp.concatenate([x, jnp.zeros_like(x)], axis=1)


def fwd_kernel(bq, length_ref, slope_ref, mixed_ref, heads_ref, qa_ref, ka_ref, va_ref, o_ref):
    span = mixed_ref.shape[0]
    heads = heads_ref.shape[1] // HD
    lane = lax.broadcasted_iota(jnp.int32, (1, LANES), 1)
    keys = key_side(span, length_ref[0])
    for h in range(heads):
        base = h * 3 * HD
        q = mixed_ref[:, base : base + HD].astype(F32) * (HD ** -0.5)
        k = mixed_ref[:, base + HD : base + 2 * HD].astype(F32)
        v = mixed_ref[:, base + 2 * HD : base + 3 * HD].astype(F32)
        parts = [slope_ref[h, n] for n in range(3)]
        qa_ref[h] = (wide(q) + slope_side(lane, parts)).astype(BF16)
        ka_ref[h] = (wide(k) + keys).astype(BF16)
        va_ref[h] = (wide(v) + jnp.where((lane >= 64) & (lane <= 66), 1.0, 0.0)).astype(BF16)

    def one_head(h, carry):
        for i in range(span // bq):
            rows = slice(i * bq, (i + 1) * bq)
            ext = (i + 1) * bq
            q = qa_ref[h, rows, :]
            s = nt(q, ka_ref[h, :ext, :])
            tq = lax.broadcasted_iota(jnp.int32, (bq, bq), 0)
            tk = lax.broadcasted_iota(jnp.int32, (bq, bq), 1)
            diag = jnp.where(tk <= tq, s[:, i * bq :], -3e38)
            s = jnp.concatenate([s[:, : i * bq], diag], axis=1) if i else diag
            m = jnp.max(s, axis=1, keepdims=True)
            p = jnp.exp(s - m).astype(BF16)
            o = nn(p, va_ref[h, :ext, :])
            total = o[:, HD : HD + 1]
            out = o / total
            lse = -(m + jnp.log(total))
            l1, l2, l3 = split3(lse)
            o_ref[h, rows, :] = out.astype(BF16)
            qa_ref[h, rows, :] = at_lanes(lane, q.astype(F32), ((71, l1), (72, l2), (73, l3))).astype(BF16)
        return carry

    lax.fori_loop(0, heads, one_head, 0)
    heads_ref[...] = jnp.concatenate([o_ref[h][:, :HD] for h in range(heads)], axis=1)


def attend_forward(mixed, length, slope_parts, bq=256):
    span = mixed.shape[0]
    heads = mixed.shape[1] // (3 * HD)
    vm = pl.BlockSpec(memory_space=pltpu.VMEM)
    sm = pl.BlockSpec(memory_space=pltpu.SMEM)
    aug = jax.ShapeDtypeStruct((heads, span, LANES), BF16)
    return pl.pallas_call(
        functools.partial(fwd_kernel, bq),
        out_shape=(jax.ShapeDtypeStruct((span, heads * HD), BF16), aug, aug, aug),
        in_specs=[sm, sm, vm],
        out_specs=(vm, vm, vm, vm),
        scratch_shapes=[pltpu.VMEM((heads, span, LANES), BF16)],
        compiler_params=pltpu.CompilerParams(vmem_limit_bytes=60 << 20),
        cost_estimate=pl.CostEstimate(
            flops=4 * heads * span * span * LANES // 2, transcendentals=heads * span * span // 2,
            bytes_accessed=heads * span * LANES * 10,
        ),
        name="attend_forward",
    )(length, slope_parts, mixed)


def bwd_kernel(bk, bq, qa_ref, ka_ref, va_ref, heads_ref, grad_ref, out_ref, da_ref, dqt_ref, dk_ref, dv_ref):
    heads, span, _ = qa_ref.shape
    lane = lax.broadcasted_iota(jnp.int32, (1, LANES), 1)
    for h in range(heads):
        o = heads_ref[:, h * HD : (h + 1) * HD].astype(F32)
        g = grad_ref[:, h * HD : (h + 1) * HD].astype(F32)
        d1, d2, d3 = split3(-jnp.sum(o * g, axis=1, keepdims=True))
        da_ref[h] = at_lanes(lane, wide(g), ((64, d1), (65, d2), (66, d3))).astype(BF16)

    def one_head(h, carry):
        for j in range(span // bk):
            cols = slice(j * bk, (j + 1) * bk)
            k = ka_ref[h, cols, :]
            v = va_ref[h, cols, :]
            kt = k[:, :HD].T
            start = j * bk
            dk = jnp.zeros((bk, LANES), F32)
            dv = jnp.zeros((bk, LANES), F32)
            while start < span:
                stop = min(span, (start // bq + 1) * bq)
                q = qa_ref[h, start:stop, :]
                d = da_ref[h, start:stop, :]
                p = jnp.exp(nt(k, q))
                if start == j * bk:
                    tk = lax.broadcasted_iota(jnp.int32, (bk, stop - start), 0)
                    tq = lax.broadcasted_iota(jnp.int32, (bk, stop - start), 1)
                    p = jnp.where(tk <= tq, p, 0.0)
                dp = nt(v, d)
                ds = (p * dp).astype(BF16)
                dv = dv + nn(p.astype(BF16), d)
                dk = dk + nn(ds, q)
                part = nn(kt, ds)
                if j == 0:
                    dqt_ref[h, :, start:stop] = part
                else:
                    dqt_ref[h, :, start:stop] += part
                start = stop
            dk_ref[h, cols, :] = dk
            dv_ref[h, cols, :] = dv
        return carry

    lax.fori_loop(0, heads, one_head, 0)
    pieces = []
    for h in range(heads):
        pieces += [dqt_ref[h].T * (HD ** -0.5), dk_ref[h][:, :HD], dv_ref[h][:, :HD]]
    out_ref[...] = jnp.concatenate(pieces, axis=1).astype(BF16)


def attend_backward(qa, ka, va, heads_b, grad_heads, bk=256, bq=1024):
    heads, span, _ = qa.shape
    vm = pl.BlockSpec(memory_space=pltpu.VMEM)
    return pl.pallas_call(
        functools.partial(bwd_kernel, bk, bq),
        out_shape=jax.ShapeDtypeStruct((span, heads * 3 * HD), BF16),
        in_specs=[vm] * 5,
        out_specs=vm,
        scratch_shapes=[
            pltpu.VMEM((heads, span, LANES), BF16),
            pltpu.VMEM((heads, HD, span), F32),
            pltpu.VMEM((heads, span, LANES), F32),
            pltpu.VMEM((heads, span, LANES), F32),
        ],
        compiler_params=pltpu.CompilerParams(vmem_limit_bytes=60 << 20),
        cost_estimate=pl.CostEstimate(
            flops=10 * heads * span * span * LANES // 2, transcendentals=heads * span * span // 2,
            bytes_accessed=heads * span * LANES * 12,
        ),
        name="attend_backward",
    )(qa, ka, va, heads_b, grad_heads)


def slope_table(first, count, total):
    ids = (first + jnp.arange(count, dtype=jnp.int32)).astype(F32)
    slopes = jnp.exp2(-8.0 * (ids + 1.0) / total)
    return jnp.stack(split3(slopes), axis=1)


eps = 1e-05


def layer_norm(values, gain, bias):
    centre = jnp.mean(values, axis=-1, keepdims=True)
    shifted = values - centre
    spread = jnp.mean(shifted * shifted, axis=-1, keepdims=True)
    factor = lax.rsqrt(spread + eps)
    unit_rows = shifted * factor
    return (unit_rows * gain + bias, unit_rows, factor)


def norm_back(grad_rows, unit_rows, factor, gain):
    scaled = grad_rows * gain
    inner = jnp.mean(scaled * unit_rows, axis=-1, keepdims=True)
    return factor * (scaled - jnp.mean(scaled, axis=-1, keepdims=True) - unit_rows * inner)


def cross_rows(left, right):
    return lax.dot_general(
        left, right, (((0,), (0,)), ((), ())), preferred_element_type=jnp.float32
    )


def times_trans(left, right):
    return lax.dot_general(
        left, right, (((1,), (1,)), ((), ())), preferred_element_type=jnp.float32
    )


def qkv_bias(pairs):
    return jnp.stack([pairs[:, 0], jnp.zeros_like(pairs[:, 0]), pairs[:, 1]], axis=1)


def body(
    layer_in,
    cotangent,
    lengths,
    languages,
    lang_weight,
    ln1_gain,
    ln1_bias,
    w_qkv,
    b_qv,
    w_out,
    b_out,
    ln2_gain,
    ln2_bias,
    w_up,
    b_up,
    w_down,
    b_down,
):
    groups = lax.axis_size("tensor")
    place = lax.axis_index("tensor")
    own_rows = layer_in.shape[0]
    all_rows = own_rows * groups
    seq_count = lengths.shape[0]
    seq_len = all_rows // seq_count
    head_dim = HD
    local_heads = w_out.shape[0] // head_dim
    in_float = layer_in.astype(jnp.float32)
    normed1, unit1, factor1 = layer_norm(in_float, ln1_gain, ln1_bias)
    normed1_b = normed1.astype(jnp.bfloat16)
    mixed = jnp.dot(
        lax.all_gather(normed1_b, "tensor", axis=0, tiled=True),
        w_qkv,
        preferred_element_type=jnp.float32,
    )
    bias_three = qkv_bias(b_qv.reshape(local_heads, 2, head_dim))
    mixed_b = (mixed + bias_three.reshape(1, -1)).astype(jnp.bfloat16)
    slope_parts = slope_table(place * local_heads, local_heads, HEADS)
    heads_b, query_aug, key_aug, value_aug = attend_forward(mixed_b, lengths, slope_parts)
    attn_sum = lax.psum_scatter(
        jnp.dot(heads_b, w_out, preferred_element_type=jnp.float32).astype(jnp.bfloat16),
        "tensor",
        scatter_dimension=0,
        tiled=True,
    ).astype(jnp.float32)
    middle = in_float + attn_sum + b_out
    normed2, unit2, factor2 = layer_norm(middle, ln2_gain, ln2_bias)
    normed2_b = normed2.astype(jnp.bfloat16)
    pre_act = (
        jnp.dot(
            lax.all_gather(normed2_b, "tensor", axis=0, tiled=True),
            w_up,
            preferred_element_type=jnp.float32,
        )
        + b_up
    )
    gelu_out, gelu_pull = jax.vjp(lambda inputs: jax.nn.gelu(inputs, approximate=True), pre_act)
    active_b = gelu_out.astype(jnp.bfloat16)
    output = (
        middle
        + lax.psum_scatter(
            jnp.dot(active_b, w_down, preferred_element_type=jnp.float32).astype(jnp.bfloat16),
            "tensor",
            scatter_dimension=0,
            tiled=True,
        ).astype(jnp.float32)
        + b_down
    )
    row_ids = place * own_rows + jnp.arange(own_rows, dtype=jnp.int32)
    seq_ids = row_ids // seq_len
    positions = row_ids - seq_ids * seq_len
    seq_hit = seq_ids[:, None] == jnp.arange(seq_count, dtype=jnp.int32)[None, :]
    row_length = jnp.sum(jnp.where(seq_hit, lengths[None, :], 0), axis=1)
    row_lang = jnp.sum(jnp.where(seq_hit, languages[None, :], 0), axis=1)
    lang_hit = row_lang[:, None] == jnp.arange(lang_weight.shape[0], dtype=jnp.int32)[None, :]
    row_weight = jnp.sum(jnp.where(lang_hit, lang_weight[None, :], 0.0), axis=1)
    live = jnp.where(positions < row_length, row_weight, 0.0)
    grad_top = cotangent.astype(jnp.float32) * live[:, None]
    g_b_down = jnp.sum(grad_top, axis=0)
    grad_full = lax.all_gather(grad_top.astype(jnp.bfloat16), "tensor", axis=0, tiled=True)
    g_w_down = cross_rows(active_b, grad_full)
    grad_active = times_trans(grad_full, w_down)
    grad_pre_b = gelu_pull(grad_active)[0].astype(jnp.bfloat16)
    g_b_up = jnp.sum(grad_pre_b.astype(jnp.float32), axis=0)
    rows_here = grad_pre_b
    g_w_up = cross_rows(lax.all_gather(normed2_b, "tensor", axis=0, tiled=True), rows_here)
    grad_norm2 = lax.psum_scatter(
        times_trans(grad_pre_b, w_up).astype(jnp.bfloat16),
        "tensor",
        scatter_dimension=0,
        tiled=True,
    ).astype(jnp.float32)
    g_ln2_gain = jnp.sum(grad_norm2 * unit2, axis=0)
    g_ln2_bias = jnp.sum(grad_norm2, axis=0)
    grad_middle = grad_top + norm_back(grad_norm2, unit2, factor2, ln2_gain)
    g_b_out = jnp.sum(grad_middle, axis=0)
    grad_mid_b = grad_middle.astype(jnp.bfloat16)
    grad_mid_full = lax.all_gather(grad_mid_b, "tensor", axis=0, tiled=True)
    g_w_out = cross_rows(heads_b, grad_mid_full)
    grad_heads_b = times_trans(grad_mid_full, w_out).astype(jnp.bfloat16)
    grad_mixed_b = attend_backward(query_aug, key_aug, value_aug, heads_b, grad_heads_b)
    column_sums = jnp.sum(grad_mixed_b.astype(jnp.float32), axis=0).reshape(
        local_heads, 3, head_dim
    )
    g_b_qv = jnp.stack([column_sums[:, 0], column_sums[:, 2]], axis=1).reshape(-1)
    rows_here = grad_mixed_b
    g_w_qkv = cross_rows(lax.all_gather(normed1_b, "tensor", axis=0, tiled=True), rows_here)
    grad_norm1 = lax.psum_scatter(
        times_trans(grad_mixed_b, w_qkv).astype(jnp.bfloat16),
        "tensor",
        scatter_dimension=0,
        tiled=True,
    ).astype(jnp.float32)
    g_ln1_gain = jnp.sum(grad_norm1 * unit1, axis=0)
    g_ln1_bias = jnp.sum(grad_norm1, axis=0)
    grad_input = grad_middle + norm_back(grad_norm1, unit1, factor1, ln1_gain)
    weights = (
        lax.psum(g_w_qkv.astype(jnp.bfloat16), "dp").astype(jnp.float32),
        lax.psum(g_b_qv.astype(jnp.bfloat16), "dp").astype(jnp.float32),
        lax.psum(g_w_out.astype(jnp.bfloat16), "dp").astype(jnp.float32),
        lax.psum(g_w_up.astype(jnp.bfloat16), "dp").astype(jnp.float32),
        lax.psum(g_b_up.astype(jnp.bfloat16), "dp").astype(jnp.float32),
        lax.psum(g_w_down.astype(jnp.bfloat16), "dp").astype(jnp.float32),
    )
    shared = lax.psum(
        (g_ln1_gain, g_ln1_bias, g_b_out, g_ln2_gain, g_ln2_bias, g_b_down), ("dp", "tensor")
    )
    return (
        output.astype(jnp.bfloat16),
        grad_input.astype(jnp.bfloat16),
        shared[0],
        shared[1],
        weights[0],
        weights[1],
        weights[2],
        shared[2],
        shared[3],
        shared[4],
        weights[3],
        weights[4],
        weights[5],
        shared[5],
    )


def solution(mesh):
    in_specs = (
        P(("dp", "tensor"), None),
        P(("dp", "tensor"), None),
        P("dp"),
        P("dp"),
        P(),
        P(),
        P(),
        P(None, "tensor"),
        P("tensor"),
        P("tensor", None),
        P(),
        P(),
        P(),
        P(None, "tensor"),
        P("tensor"),
        P("tensor", None),
        P(),
    )
    out_specs = (
        P(("dp", "tensor"), None),
        P(("dp", "tensor"), None),
        P(),
        P(),
        P(None, "tensor"),
        P("tensor"),
        P("tensor", None),
        P(),
        P(),
        P(),
        P(None, "tensor"),
        P("tensor"),
        P("tensor", None),
        P(),
    )
    return jax.shard_map(body, mesh=mesh, in_specs=in_specs, out_specs=out_specs, check_vma=False)
```

```python
import functools
import jax
import jax.numpy as jnp
from jax import lax
from jax.sharding import PartitionSpec as P
from jax.experimental import pallas as pl
from jax.experimental.pallas import tpu as pltpu

HEADS = 16
HD = 64
LANES = 128
F32 = jnp.float32
BF16 = jnp.bfloat16


def split3(x):
    hi = x.astype(BF16)
    rest = x - hi.astype(F32)
    mid = rest.astype(BF16)
    low = (rest - mid.astype(F32)).astype(BF16)
    return hi.astype(F32), mid.astype(F32), low.astype(F32)


def nt(a, b):
    return lax.dot_general(a, b, (((1,), (1,)), ((), ())), preferred_element_type=F32)


def nn(a, b):
    return jnp.dot(a, b, preferred_element_type=F32)


def at_lanes(lane, base, pairs):
    out = base
    for where, value in pairs:
        out = jnp.where(lane == where, value, out)
    return out


def key_side(span, first, length):
    pos = first + lax.broadcasted_iota(jnp.int32, (span, LANES), 0)
    lane = lax.broadcasted_iota(jnp.int32, (span, LANES), 1)
    low = (pos & 255).astype(F32)
    high = (pos - (pos & 255)).astype(F32)
    is_high = (lane == 64) | (lane == 66) | (lane == 68)
    is_low = (lane == 65) | (lane == 67) | (lane == 69)
    gone = jnp.where(pos < length, 0.0, -1e30)
    out = jnp.where(is_high, high, jnp.where(is_low, low, 0.0))
    out = jnp.where(lane == 70, gone, out)
    return jnp.where((lane >= 71) & (lane <= 73), 1.0, out)


def slope_side(lane, slope_parts):
    s1, s2, s3 = slope_parts
    out = jnp.where(lane < 66, s1, jnp.where(lane < 68, s2, s3))
    out = jnp.where(lane == 70, 1.0, out)
    return jnp.where((lane >= 64) & (lane <= 70), out, 0.0)


def wide(x):
    return jnp.concatenate([x, jnp.zeros_like(x)], axis=1)


def fwd_kernel(count, bq, place_ref, length_ref, slope_ref, *refs):
    mixed_refs, heads_refs = refs[:count], refs[count : 2 * count]
    qa_ref, ka_ref, va_ref, o_ref = refs[2 * count :]
    own = mixed_refs[0].shape[0]
    heads, span, _ = qa_ref.shape
    lane = lax.broadcasted_iota(jnp.int32, (1, LANES), 1)
    ones = jnp.where((lane >= 64) & (lane <= 66), 1.0, 0.0)
    for j in range(count):
        first = pl.multiple_of((place_ref[0] ^ j) * own, own)
        keys = key_side(own, first, length_ref[0])
        for h in range(heads):
            base = h * 3 * HD
            q = mixed_refs[j][:, base : base + HD].astype(F32) * (HD ** -0.5)
            k = mixed_refs[j][:, base + HD : base + 2 * HD].astype(F32)
            v = mixed_refs[j][:, base + 2 * HD : base + 3 * HD].astype(F32)
            parts = [slope_ref[h, n] for n in range(3)]
            rows = pl.ds(first, own)
            qa_ref[h, rows, :] = (wide(q) + slope_side(lane, parts)).astype(BF16)
            ka_ref[h, rows, :] = (wide(k) + keys).astype(BF16)
            va_ref[h, rows, :] = (wide(v) + ones).astype(BF16)

    def one_head(h, carry):
        for i in range(span // bq):
            rows = slice(i * bq, (i + 1) * bq)
            ext = (i + 1) * bq
            q = qa_ref[h, rows, :]
            s = nt(q, ka_ref[h, :ext, :])
            tq = lax.broadcasted_iota(jnp.int32, (bq, bq), 0)
            tk = lax.broadcasted_iota(jnp.int32, (bq, bq), 1)
            diag = jnp.where(tk <= tq, s[:, i * bq :], -3e38)
            s = jnp.concatenate([s[:, : i * bq], diag], axis=1) if i else diag
            m = jnp.max(s, axis=1, keepdims=True)
            p = jnp.exp(s - m).astype(BF16)
            o = nn(p, va_ref[h, :ext, :])
            total = o[:, HD : HD + 1]
            out = o / total
            l1, l2, l3 = split3(-(m + jnp.log(total)))
            o_ref[h, rows, :] = out.astype(BF16)
            logs = at_lanes(lane, q.astype(F32), ((71, l1), (72, l2), (73, l3)))
            qa_ref[h, rows, :] = logs.astype(BF16)
        return carry

    lax.fori_loop(0, heads, one_head, 0)
    for j in range(count):
        rows = pl.ds(pl.multiple_of((place_ref[0] ^ j) * own, own), own)
        heads_refs[j][...] = jnp.concatenate([o_ref[h, rows, :][:, :HD] for h in range(heads)], axis=1)


def attend_forward(mixed, place, length, slope_parts, bq=256):
    count = len(mixed)
    own = mixed[0].shape[0]
    span = own * count
    heads = mixed[0].shape[1] // (3 * HD)
    vm = pl.BlockSpec(memory_space=pltpu.VMEM)
    sm = pl.BlockSpec(memory_space=pltpu.SMEM)
    aug = jax.ShapeDtypeStruct((heads, span, LANES), BF16)
    res = pl.pallas_call(
        functools.partial(fwd_kernel, count, bq),
        out_shape=(jax.ShapeDtypeStruct((own, heads * HD), BF16),) * count + (aug, aug, aug),
        in_specs=[sm, sm, sm] + [vm] * count,
        out_specs=(vm,) * (count + 3),
        scratch_shapes=[pltpu.VMEM((heads, span, LANES), BF16)],
        compiler_params=pltpu.CompilerParams(vmem_limit_bytes=60 << 20),
        cost_estimate=pl.CostEstimate(
            flops=4 * heads * span * span * LANES // 2, transcendentals=heads * span * span // 2,
            bytes_accessed=heads * span * LANES * 10,
        ),
        name="attend_forward",
    )(place, length, slope_parts, *mixed)
    return res[:count], res[count:]


def bwd_kernel(count, bk, bq, place_ref, qa_ref, ka_ref, va_ref, *refs):
    heads_refs, grad_refs, out_refs = refs[:count], refs[count : 2 * count], refs[2 * count : 3 * count]
    da_ref, dqt_ref, dk_ref, dv_ref = refs[3 * count :]
    own = heads_refs[0].shape[0]
    heads, span, _ = qa_ref.shape
    lane = lax.broadcasted_iota(jnp.int32, (1, LANES), 1)
    for j in range(count):
        rows = pl.ds(pl.multiple_of((place_ref[0] ^ j) * own, own), own)
        for h in range(heads):
            o = heads_refs[j][:, h * HD : (h + 1) * HD].astype(F32)
            g = grad_refs[j][:, h * HD : (h + 1) * HD].astype(F32)
            d1, d2, d3 = split3(-jnp.sum(o * g, axis=1, keepdims=True))
            da_ref[h, rows, :] = at_lanes(lane, wide(g), ((64, d1), (65, d2), (66, d3))).astype(BF16)

    def one_head(h, carry):
        for j in range(span // bk):
            cols = slice(j * bk, (j + 1) * bk)
            k = ka_ref[h, cols, :]
            v = va_ref[h, cols, :]
            kt = k[:, :HD].T
            start = j * bk
            dk = jnp.zeros((bk, LANES), F32)
            dv = jnp.zeros((bk, LANES), F32)
            while start < span:
                stop = min(span, (start // bq + 1) * bq)
                q = qa_ref[h, start:stop, :]
                d = da_ref[h, start:stop, :]
                p = jnp.exp(nt(k, q))
                if start == j * bk:
                    tk = lax.broadcasted_iota(jnp.int32, (bk, stop - start), 0)
                    tq = lax.broadcasted_iota(jnp.int32, (bk, stop - start), 1)
                    p = jnp.where(tk <= tq, p, 0.0)
                dp = nt(v, d)
                ds = (p * dp).astype(BF16)
                dv = dv + nn(p.astype(BF16), d)
                dk = dk + nn(ds, q)
                part = nn(kt, ds)
                if j == 0:
                    dqt_ref[h, :, start:stop] = part
                else:
                    dqt_ref[h, :, start:stop] += part
                start = stop
            dk_ref[h, cols, :] = dk
            dv_ref[h, cols, :] = dv
        return carry

    lax.fori_loop(0, heads, one_head, 0)
    for j in range(count):
        first = pl.multiple_of((place_ref[0] ^ j) * own, own)
        rows = pl.ds(first, own)
        pieces = []
        for h in range(heads):
            pieces += [dqt_ref[h, :, rows].T * (HD ** -0.5), dk_ref[h, rows, :HD], dv_ref[h, rows, :HD]]
        out_refs[j][...] = jnp.concatenate(pieces, axis=1).astype(BF16)


def attend_backward(saved, heads_b, grad_heads, place, bk=256, bq=2048):
    heads, span, _ = saved[0].shape
    count = len(heads_b)
    own = span // count
    vm = pl.BlockSpec(memory_space=pltpu.VMEM)
    sm = pl.BlockSpec(memory_space=pltpu.SMEM)
    return pl.pallas_call(
        functools.partial(bwd_kernel, count, bk, bq),
        out_shape=(jax.ShapeDtypeStruct((own, heads * 3 * HD), BF16),) * count,
        in_specs=[sm] + [vm] * (3 + 2 * count),
        out_specs=(vm,) * count,
        scratch_shapes=[
            pltpu.VMEM((heads, span, LANES), BF16),
            pltpu.VMEM((heads, HD, span), F32),
            pltpu.VMEM((heads, span, LANES), F32),
            pltpu.VMEM((heads, span, LANES), F32),
        ],
        compiler_params=pltpu.CompilerParams(vmem_limit_bytes=60 << 20),
        cost_estimate=pl.CostEstimate(
            flops=10 * heads * span * span * LANES // 2, transcendentals=heads * span * span // 2,
            bytes_accessed=heads * span * LANES * 12,
        ),
        name="attend_backward",
    )(place, *saved, *heads_b, *grad_heads)


def slope_table(first, count, total):
    ids = (first + jnp.arange(count, dtype=jnp.int32)).astype(F32)
    slopes = jnp.exp2(-8.0 * (ids + 1.0) / total)
    return jnp.stack(split3(slopes), axis=1)


eps = 1e-05


def layer_norm(values, gain, bias):
    centre = jnp.mean(values, axis=-1, keepdims=True)
    shifted = values - centre
    spread = jnp.mean(shifted * shifted, axis=-1, keepdims=True)
    factor = lax.rsqrt(spread + eps)
    unit_rows = shifted * factor
    return (unit_rows * gain + bias, unit_rows, factor)


def norm_back(grad_rows, unit_rows, factor, gain):
    scaled = grad_rows * gain
    inner = jnp.mean(scaled * unit_rows, axis=-1, keepdims=True)
    return factor * (scaled - jnp.mean(scaled, axis=-1, keepdims=True) - unit_rows * inner)


def tn(a, b):
    return lax.dot_general(a, b, (((0,), (0,)), ((), ())), preferred_element_type=F32)


def swap(x, axis, bit):
    return lax.ppermute(x, axis, [(i, i ^ bit) for i in range(lax.axis_size(axis))])


def bits_of(axis):
    return [1 << n for n in range(lax.axis_size(axis).bit_length() - 1)]


def gather_blocks(x, axis):
    blocks = {0: x}
    for bit in bits_of(axis)[1:]:
        blocks.update({j ^ bit: swap(b, axis, bit) for j, b in list(blocks.items())})
    blocks.update({j ^ 1: swap(b, axis, 1) for j, b in list(blocks.items())})
    return [blocks[j] for j in range(len(blocks))]


def sum_blocks(parts, axis):
    parts = dict(enumerate(parts))
    for bit in bits_of(axis):
        kept = {}
        for j in sorted(parts, reverse=True):
            if not j & bit:
                kept[j] = parts[j].astype(F32) + swap(parts[j | bit].astype(BF16), axis, bit).astype(F32)
        parts = kept
    return parts[0]


def total_of(x, axis):
    for bit in bits_of(axis):
        x = x + swap(x, axis, bit)
    return x


def body(
    layer_in,
    cotangent,
    lengths,
    languages,
    lang_weight,
    ln1_gain,
    ln1_bias,
    w_qkv,
    b_qv,
    w_out,
    b_out,
    ln2_gain,
    ln2_bias,
    w_up,
    b_up,
    w_down,
    b_down,
):
    groups = lax.axis_size("tensor")
    place = lax.axis_index("tensor")
    place_one = place.astype(jnp.int32).reshape(1)
    own_rows = layer_in.shape[0]
    local_heads = w_out.shape[0] // HD

    in_float = layer_in.astype(F32)
    normed1, unit1, factor1 = layer_norm(in_float, ln1_gain, ln1_bias)
    n1 = gather_blocks(normed1.astype(BF16), "tensor")

    positions = place * own_rows + jnp.arange(own_rows, dtype=jnp.int32)
    weight = jnp.sum(jnp.where(jnp.arange(lang_weight.shape[0]) == languages[0], lang_weight, 0.0))
    live = jnp.where(positions < lengths[0], weight, 0.0)
    grad_top = cotangent.astype(F32) * live[:, None]
    g_b_down = jnp.sum(grad_top, axis=0)

    pairs = b_qv.reshape(local_heads, 2, HD)
    bias_three = jnp.stack([pairs[:, 0], jnp.zeros_like(pairs[:, 0]), pairs[:, 1]], axis=1).reshape(1, -1)
    mixed = [(nn(x, w_qkv) + bias_three).astype(BF16) for x in n1]
    slope_parts = slope_table(place * local_heads, local_heads, HEADS)
    heads_b, saved = attend_forward(mixed, place_one, lengths, slope_parts)

    top_gate, mixed_gate = lax.optimization_barrier((grad_top.astype(BF16), mixed[-1]))
    top = gather_blocks(top_gate, "tensor")

    attn_sum = sum_blocks([nn(x, w_out).astype(BF16) for x in heads_b], "tensor")
    middle = in_float + attn_sum + b_out
    normed2, unit2, factor2 = layer_norm(middle, ln2_gain, ln2_bias)
    n2 = gather_blocks(normed2.astype(BF16), "tensor")

    active, grad_pre = [], []
    for j in range(groups):
        pre = nn(n2[j], w_up) + b_up
        out, pull = jax.vjp(lambda v: jax.nn.gelu(v, approximate=True), pre)
        active.append(out.astype(BF16))
        grad_pre.append(pull(nt(top[j], w_down))[0].astype(BF16))
    grad_norm2 = sum_blocks([nt(x, w_up).astype(BF16) for x in grad_pre], "tensor")
    mlp_sum = sum_blocks([nn(x, w_down).astype(BF16) for x in active], "tensor")
    output = middle + mlp_sum + b_down

    def weight_grad(lefts, rights):
        return tn(jnp.concatenate(lefts, axis=0), jnp.concatenate(rights, axis=0))

    g_w_down = weight_grad(active, top)
    g_w_up = weight_grad(n2, grad_pre)
    g_b_up = sum(jnp.sum(x.astype(F32), axis=0) for x in grad_pre)

    g_ln2_gain = jnp.sum(grad_norm2 * unit2, axis=0)
    g_ln2_bias = jnp.sum(grad_norm2, axis=0)
    grad_middle = grad_top + norm_back(grad_norm2, unit2, factor2, ln2_gain)
    g_b_out = jnp.sum(grad_middle, axis=0)
    gm = gather_blocks(grad_middle.astype(BF16), "tensor")
    grad_heads = [nt(x, w_out).astype(BF16) for x in gm]
    grad_mixed = attend_backward(saved, heads_b, grad_heads, place_one)
    g_w_out = weight_grad(heads_b, gm)
    column_sums = sum(jnp.sum(x.astype(F32), axis=0) for x in grad_mixed).reshape(local_heads, 3, HD)
    g_b_qv = jnp.stack([column_sums[:, 0], column_sums[:, 2]], axis=1).reshape(-1)
    g_w_qkv = weight_grad(n1, grad_mixed)
    grad_norm1 = sum_blocks([nt(x, w_qkv).astype(BF16) for x in grad_mixed], "tensor")
    g_ln1_gain = jnp.sum(grad_norm1 * unit1, axis=0)
    g_ln1_bias = jnp.sum(grad_norm1, axis=0)
    grad_input = grad_middle + norm_back(grad_norm1, unit1, factor1, ln1_gain)

    up, down = lax.psum((g_w_up.astype(BF16), g_w_down.astype(BF16)), "dp")
    w_rest, up, down = lax.optimization_barrier(((g_w_qkv.astype(BF16), g_w_out.astype(BF16)), up, down))
    qkv, out = lax.psum(w_rest, "dp")

    width = ln1_gain.shape[0]
    early = total_of(jnp.concatenate([g_b_down, g_b_out, g_ln2_gain, g_ln2_bias]), "tensor")
    early = total_of(jnp.concatenate([early, g_b_up]), "dp")
    late = total_of(jnp.concatenate([g_ln1_gain, g_ln1_bias]), "tensor")
    late = total_of(jnp.concatenate([late, g_b_qv]), "dp")
    shared = [early[n * width : (n + 1) * width] for n in range(4)]
    g_b_up = early[4 * width :]
    return (
        output.astype(BF16),
        grad_input.astype(BF16),
        late[:width],
        late[width : 2 * width],
        qkv.astype(F32),
        late[2 * width :],
        out.astype(F32),
        shared[1],
        shared[2],
        shared[3],
        up.astype(F32),
        g_b_up,
        down.astype(F32),
        shared[0],
    )


def solution(mesh):
    rows, columns, flat = P("tensor", None), P(None, "tensor"), P("tensor")
    tokens = P(("dp", "tensor"), None)
    in_specs = (tokens, tokens, P("dp"), P("dp"), P(), P(), P(), columns, flat, rows, P(), P(), P(), columns, flat, rows, P())
    out_specs = (tokens, tokens, P(), P(), columns, flat, rows, P(), P(), P(), columns, flat, rows, P())
    return jax.shard_map(body, mesh=mesh, in_specs=in_specs, out_specs=out_specs, check_vma=False)
```

```python
import functools
import math
import jax
import jax.numpy as jnp
from jax import lax
from jax.sharding import PartitionSpec as P
from jax.experimental import pallas as pl
from jax.experimental.pallas import tpu as pltpu

HEADS = 16
HD = 64
LANES = 128
F32 = jnp.float32
BF16 = jnp.bfloat16
COST = pl.CostEstimate(flops=1000, transcendentals=0, bytes_accessed=1000)


def split3(x):
    hi = x.astype(BF16)
    rest = x - hi.astype(F32)
    mid = rest.astype(BF16)
    low = (rest - mid.astype(F32)).astype(BF16)
    return hi.astype(F32), mid.astype(F32), low.astype(F32)


def nt(a, b):
    return lax.dot_general(a, b, (((1,), (1,)), ((), ())), preferred_element_type=F32)


def nn(a, b):
    return jnp.dot(a, b, preferred_element_type=F32)


def at_lanes(lane, base, pairs):
    out = base
    for where, value in pairs:
        out = jnp.where(lane == where, value, out)
    return out


def key_side(span, first, length):
    pos = first + lax.broadcasted_iota(jnp.int32, (span, LANES), 0)
    lane = lax.broadcasted_iota(jnp.int32, (span, LANES), 1)
    low = (pos & 255).astype(F32)
    high = (pos - (pos & 255)).astype(F32)
    is_high = (lane == 64) | (lane == 66) | (lane == 68)
    is_low = (lane == 65) | (lane == 67) | (lane == 69)
    gone = jnp.where(pos < length, 0.0, -1e30)
    out = jnp.where(is_high, high, jnp.where(is_low, low, 0.0))
    out = jnp.where(lane == 70, gone, out)
    return jnp.where((lane >= 71) & (lane <= 73), 1.0, out)


def slope_side(lane, slope_parts):
    s1, s2, s3 = slope_parts
    out = jnp.where(lane < 66, s1, jnp.where(lane < 68, s2, s3))
    out = jnp.where(lane == 70, 1.0, out)
    return jnp.where((lane >= 64) & (lane <= 70), out, 0.0)


def wide(x):
    return jnp.concatenate([x, jnp.zeros_like(x)], axis=1)


def fwd_kernel(count, bq, place_ref, length_ref, slope_ref, *refs):
    mixed_refs, heads_refs = refs[:count], refs[count : 2 * count]
    qa_ref, ka_ref, va_ref, o_ref = refs[2 * count :]
    own = mixed_refs[0].shape[0]
    heads, span, _ = qa_ref.shape
    lane = lax.broadcasted_iota(jnp.int32, (1, LANES), 1)
    ones = jnp.where((lane >= 64) & (lane <= 66), 1.0, 0.0)
    for j in range(count):
        first = pl.multiple_of((place_ref[0] ^ j) * own, own)
        keys = key_side(own, first, length_ref[0])
        for h in range(heads):
            base = h * 3 * HD
            q = mixed_refs[j][:, base : base + HD].astype(F32) * (HD ** -0.5)
            k = mixed_refs[j][:, base + HD : base + 2 * HD].astype(F32)
            v = mixed_refs[j][:, base + 2 * HD : base + 3 * HD].astype(F32)
            parts = [slope_ref[h, n] for n in range(3)]
            rows = pl.ds(first, own)
            qa_ref[h, rows, :] = (wide(q) + slope_side(lane, parts)).astype(BF16)
            ka_ref[h, rows, :] = (wide(k) + keys).astype(BF16)
            va_ref[h, rows, :] = (wide(v) + ones).astype(BF16)

    def one_head(h, carry):
        for i in range(span // bq):
            rows = slice(i * bq, (i + 1) * bq)
            ext = (i + 1) * bq
            q = qa_ref[h, rows, :]
            s = nt(q, ka_ref[h, :ext, :])
            tq = lax.broadcasted_iota(jnp.int32, (bq, bq), 0)
            tk = lax.broadcasted_iota(jnp.int32, (bq, bq), 1)
            diag = jnp.where(tk <= tq, s[:, i * bq :], -3e38)
            s = jnp.concatenate([s[:, : i * bq], diag], axis=1) if i else diag
            m = jnp.max(s, axis=1, keepdims=True)
            p = jnp.exp(s - m).astype(BF16)
            o = nn(p, va_ref[h, :ext, :])
            total = o[:, HD : HD + 1]
            out = o / total
            l1, l2, l3 = split3(-(m + jnp.log(total)))
            o_ref[h, rows, :] = out.astype(BF16)
            logs = at_lanes(lane, q.astype(F32), ((71, l1), (72, l2), (73, l3)))
            qa_ref[h, rows, :] = logs.astype(BF16)
        return carry

    lax.fori_loop(0, heads, one_head, 0)
    for j in range(count):
        rows = pl.ds(pl.multiple_of((place_ref[0] ^ j) * own, own), own)
        heads_refs[j][...] = jnp.concatenate([o_ref[h, rows, :][:, :HD] for h in range(heads)], axis=1)


def attend_forward(mixed, place, length, slope_parts, bq=256):
    count = len(mixed)
    own = mixed[0].shape[0]
    span = own * count
    heads = mixed[0].shape[1] // (3 * HD)
    vm = pl.BlockSpec(memory_space=pltpu.VMEM)
    sm = pl.BlockSpec(memory_space=pltpu.SMEM)
    aug = jax.ShapeDtypeStruct((heads, span, LANES), BF16)
    res = pl.pallas_call(
        functools.partial(fwd_kernel, count, bq),
        out_shape=(jax.ShapeDtypeStruct((own, heads * HD), BF16),) * count + (aug, aug, aug),
        in_specs=[sm, sm, sm] + [vm] * count,
        out_specs=(vm,) * (count + 3),
        scratch_shapes=[pltpu.VMEM((heads, span, LANES), BF16)],
        compiler_params=pltpu.CompilerParams(vmem_limit_bytes=60 << 20),
        cost_estimate=COST,
        name="attend_forward",
    )(place, length, slope_parts, *mixed)
    return res[:count], res[count:]


def bwd_kernel(count, bk, bq, place_ref, qa_ref, ka_ref, va_ref, *refs):
    heads_refs, grad_refs, out_refs = refs[:count], refs[count : 2 * count], refs[2 * count : 3 * count]
    sums_ref, da_ref, dqt_ref, dk_ref, dv_ref = refs[3 * count :]
    own = heads_refs[0].shape[0]
    heads, span, _ = qa_ref.shape
    lane = lax.broadcasted_iota(jnp.int32, (1, LANES), 1)
    for j in range(count):
        rows = pl.ds(pl.multiple_of((place_ref[0] ^ j) * own, own), own)
        for h in range(heads):
            o = heads_refs[j][:, h * HD : (h + 1) * HD].astype(F32)
            g = grad_refs[j][:, h * HD : (h + 1) * HD].astype(F32)
            d1, d2, d3 = split3(-jnp.sum(o * g, axis=1, keepdims=True))
            da_ref[h, rows, :] = at_lanes(lane, wide(g), ((64, d1), (65, d2), (66, d3))).astype(BF16)

    def one_head(h, carry):
        for j in range(span // bk):
            cols = slice(j * bk, (j + 1) * bk)
            k = ka_ref[h, cols, :]
            v = va_ref[h, cols, :]
            kt = k[:, :HD].T
            start = j * bk
            dk = jnp.zeros((bk, LANES), F32)
            dv = jnp.zeros((bk, LANES), F32)
            while start < span:
                stop = min(span, (start // bq + 1) * bq)
                q = qa_ref[h, start:stop, :]
                d = da_ref[h, start:stop, :]
                p = jnp.exp(nt(k, q))
                if start == j * bk:
                    tk = lax.broadcasted_iota(jnp.int32, (bk, stop - start), 0)
                    tq = lax.broadcasted_iota(jnp.int32, (bk, stop - start), 1)
                    p = jnp.where(tk <= tq, p, 0.0)
                dp = nt(v, d)
                ds = (p * dp).astype(BF16)
                dv = dv + nn(p.astype(BF16), d)
                dk = dk + nn(ds, q)
                part = nn(kt, ds)
                if j == 0:
                    dqt_ref[h, :, start:stop] = part
                else:
                    dqt_ref[h, :, start:stop] += part
                start = stop
            dk_ref[h, cols, :] = dk
            dv_ref[h, cols, :] = dv
        return carry

    lax.fori_loop(0, heads, one_head, 0)
    for j in range(count):
        first = pl.multiple_of((place_ref[0] ^ j) * own, own)
        rows = pl.ds(first, own)
        pieces = []
        for h in range(heads):
            pieces += [dqt_ref[h, :, rows].T * (HD ** -0.5), dk_ref[h, rows, :HD], dv_ref[h, rows, :HD]]
        rounded = jnp.concatenate(pieces, axis=1).astype(BF16)
        out_refs[j][...] = rounded
        sums = jnp.sum(rounded.astype(F32), axis=0, keepdims=True)
        sums_ref[...] = sums if j == 0 else sums_ref[...] + sums


def attend_backward(saved, heads_b, grad_heads, place, part, parts, bk=256, bq=2048):
    heads, span, _ = saved[0].shape
    heads = heads // parts
    count = len(heads_b)
    own = span // count
    vm = pl.BlockSpec(memory_space=pltpu.VMEM)
    sm = pl.BlockSpec(memory_space=pltpu.SMEM)
    aug = pl.BlockSpec((heads, span, LANES), lambda i: (part, 0, 0))
    flat = pl.BlockSpec((own, heads * HD), lambda i: (0, part))
    out = pl.BlockSpec((own, heads * 3 * HD), lambda i: (0, 0))
    return pl.pallas_call(
        functools.partial(bwd_kernel, count, bk, bq),
        grid=(1,),
        out_shape=(jax.ShapeDtypeStruct((own, heads * 3 * HD), BF16),) * count
        + (jax.ShapeDtypeStruct((1, heads * 3 * HD), F32),),
        in_specs=[sm] + [aug] * 3 + [flat] * (2 * count),
        out_specs=(out,) * count + (pl.BlockSpec((1, heads * 3 * HD), lambda i: (0, 0)),),
        scratch_shapes=[
            pltpu.VMEM((heads, span, LANES), BF16),
            pltpu.VMEM((heads, HD, span), F32),
            pltpu.VMEM((heads, span, LANES), F32),
            pltpu.VMEM((heads, span, LANES), F32),
        ],
        compiler_params=pltpu.CompilerParams(vmem_limit_bytes=60 << 20),
        cost_estimate=COST,
        name="attend_backward",
    )(place, *saved, *heads_b, *grad_heads)


def slope_table(first, count, total):
    ids = (first + jnp.arange(count, dtype=jnp.int32)).astype(F32)
    slopes = jnp.exp2(-8.0 * (ids + 1.0) / total)
    return jnp.stack(split3(slopes), axis=1)


eps = 1e-05


def whole_call(kernel, outs, ins, name, smem=0):
    vm = pl.BlockSpec(memory_space=pltpu.VMEM)
    sm = pl.BlockSpec(memory_space=pltpu.SMEM)
    return pl.pallas_call(
        kernel,
        out_shape=tuple(jax.ShapeDtypeStruct(shape, kind) for shape, kind in outs),
        in_specs=[sm] * smem + [vm] * (len(ins) - smem),
        out_specs=(vm,) * len(outs),
        compiler_params=pltpu.CompilerParams(vmem_limit_bytes=60 << 20),
        cost_estimate=COST,
        name=name,
    )(*ins)


def tn(a, b):
    return lax.dot_general(a, b, (((0,), (0,)), ((), ())), preferred_element_type=F32)


def weight_kernel(count, spots, based, *refs):
    out_ref = refs[-1]
    for n, (row, column) in enumerate(spots):
        lefts, rights = [refs[m * count : (m + 1) * count] for m in (2 * n, 2 * n + 1)]
        rows, width = lefts[0].shape[1], rights[0].shape[1]
        for top in range(0, rows, 256):
            size = min(256, rows - top)
            total = tn(lefts[0][:, top : top + size], rights[0][...])
            for left, right in zip(lefts[1:], rights[1:]):
                total = total + tn(left[:, top : top + size], right[...])
            spot = (slice(row + top, row + top + size), slice(column, column + width))
            if based:
                total = total + refs[-2][spot]
            out_ref[spot] = total.astype(out_ref.dtype)


def weight_grads(*groups, base=None, kind=BF16, stack=False):
    count = len(groups[0][0])
    ins = [x for lefts, rights in groups for x in list(lefts) + list(rights)]
    spots, row, column = [], 0, 0
    for lefts, rights in groups:
        spots.append((row, column))
        row, column = (row + lefts[0].shape[1], 0) if stack else (0, column + rights[0].shape[1])
    last = groups[-1]
    shape = (spots[-1][0] + last[0][0].shape[1], spots[-1][1] + last[1][0].shape[1])
    if base is not None:
        ins.append(base)
    kernel = functools.partial(weight_kernel, count, spots, base is not None)
    return whole_call(kernel, [(shape, kind)], ins, "weight_grads")[0]


def through_kernel(count, parts, w_ref, *refs):
    outs = refs[count * parts :]
    width = w_ref.shape[1] // parts
    for j in range(count):
        total = nt(refs[j * parts][...], w_ref[:, :width])
        for p in range(1, parts):
            total = total + nt(refs[j * parts + p][...], w_ref[:, p * width : (p + 1) * width])
        outs[j][...] = total.astype(BF16)


def through(blocks, w):
    count, parts = len(blocks), len(blocks[0])
    shape = (blocks[0][0].shape[0], w.shape[0])
    ins = [w] + [x for block in blocks for x in block]
    return list(whole_call(functools.partial(through_kernel, count, parts), [(shape, BF16)] * count, ins, "through"))


def unit_of(values):
    centre = jnp.mean(values, axis=-1, keepdims=True)
    shifted = values - centre
    factor = lax.rsqrt(jnp.mean(shifted * shifted, axis=-1, keepdims=True) + eps)
    return shifted * factor, factor


def norm_in_kernel(x_ref, gain_ref, bias_ref, out_ref):
    unit, _ = unit_of(x_ref[...].astype(F32))
    out_ref[...] = (unit * gain_ref[...] + bias_ref[...]).astype(BF16)


def norm_mid_kernel(x_ref, near_ref, far_ref, b_ref, gain_ref, bias_ref, mid_ref, out_ref):
    mid = x_ref[...].astype(F32) + (near_ref[...].astype(F32) + far_ref[...].astype(F32)) + b_ref[...]
    mid_ref[...] = mid
    unit, _ = unit_of(mid)
    out_ref[...] = (unit * gain_ref[...] + bias_ref[...]).astype(BF16)


def back_of(grad, values, gain):
    unit, factor = unit_of(values)
    d = grad * gain
    inner = jnp.mean(d * unit, axis=-1, keepdims=True)
    sums = [jnp.sum(grad * unit, axis=0, keepdims=True), jnp.sum(grad, axis=0, keepdims=True)]
    return factor * (d - jnp.mean(d, axis=-1, keepdims=True) - unit * inner), sums


def norm_mid_back_kernel(mid_ref, near_ref, far_ref, top_ref, live_ref, gain_ref, grad_ref, rounded_ref, sums_ref):
    grad = near_ref[...].astype(F32) + far_ref[...].astype(F32)
    back, sums = back_of(grad, mid_ref[...], gain_ref[...])
    top = top_ref[...].astype(F32) * live_ref[...]
    grad_mid = top + back
    grad_ref[...] = grad_mid
    rounded_ref[...] = grad_mid.astype(BF16)
    rows = [jnp.sum(top, axis=0, keepdims=True), jnp.sum(grad_mid, axis=0, keepdims=True)] + sums
    sums_ref[...] = jnp.concatenate(rows, axis=0)


def norm_in_back_kernel(x_ref, near_ref, far_ref, mid_ref, gain_ref, grad_ref, sums_ref):
    grad = near_ref[...].astype(F32) + far_ref[...].astype(F32)
    back, sums = back_of(grad, x_ref[...].astype(F32), gain_ref[...])
    grad_ref[...] = (mid_ref[...] + back).astype(BF16)
    sums_ref[...] = jnp.concatenate(sums, axis=0)


def mlp_kernel(count, tile, w_up_ref, w_down_ref, b_up_ref, *refs):
    n2_refs, top_refs, act_refs, pre_refs, back_refs = [refs[n * count : (n + 1) * count] for n in range(5)]
    sums_ref = refs[-1]
    sums_ref[...] = jnp.zeros_like(sums_ref)
    root = (2.0 / math.pi) ** 0.5

    for j in range(count):

        def step(i, carry):
            rows = pl.ds(pl.multiple_of(i * tile, tile), tile)
            pre = nn(n2_refs[j][rows, :], w_up_ref[...]) + b_up_ref[...]
            grad = nt(top_refs[j][rows, :], w_down_ref[...])
            square = pre * pre
            tanh = jnp.tanh(pre * (root + (root * 0.044715) * square))
            half = 0.5 + 0.5 * tanh
            act_refs[j][rows, :] = (pre * half).astype(BF16)
            slope = half + (0.5 * pre) * (1.0 - tanh * tanh) * (root + (root * 0.134145) * square)
            inner = (grad * slope).astype(BF16)
            pre_refs[j][rows, :] = inner
            sums_ref[...] += jnp.sum(inner.astype(F32), axis=0, keepdims=True)
            back_refs[j][rows, :] = nt(inner, w_up_ref[...]).astype(BF16)
            return carry

        lax.fori_loop(0, n2_refs[j].shape[0] // tile, step, 0)


def mlp_both(n2, top, w_up, w_down, b_up):
    count = len(n2)
    own, width = n2[0].shape
    hidden = w_up.shape[1]
    vm = pl.BlockSpec(memory_space=pltpu.VMEM)
    inner = jax.ShapeDtypeStruct((own, hidden), BF16)
    outer = jax.ShapeDtypeStruct((own, width), BF16)
    res = pl.pallas_call(
        functools.partial(mlp_kernel, count, min(own, 256)),
        out_shape=(inner,) * (2 * count) + (outer,) * count + (jax.ShapeDtypeStruct((1, hidden), F32),),
        in_specs=[vm] * (3 + 2 * count),
        out_specs=(vm,) * (3 * count + 1),
        compiler_params=pltpu.CompilerParams(vmem_limit_bytes=60 << 20),
        cost_estimate=COST,
        name="mlp_both",
    )(w_up, w_down, b_up.reshape(1, -1), *n2, *top)
    return list(res[:count]), list(res[count : 2 * count]), list(res[2 * count : -1]), res[-1][0]


def swap(x, axis, bit):
    return lax.ppermute(x, axis, [(i, i ^ bit) for i in range(lax.axis_size(axis))])


def bits_of(axis):
    return [1 << n for n in range(lax.axis_size(axis).bit_length() - 1)]


def gather_ring(x, axis):
    blocks = {0: x}
    for bit in bits_of(axis)[1:]:
        blocks.update({j ^ bit: swap(b, axis, bit) for j, b in list(blocks.items())})
    return [blocks[j] for j in sorted(blocks) if j]


def gather_chip(blocks, axis):
    return [x for b in blocks for x in (b, swap(b, axis, 1))]


def sum_chip(parts, axis):
    return [
        (parts[j].astype(F32) + swap(parts[j + 1], axis, 1).astype(F32)).astype(BF16)
        for j in range(0, len(parts), 2)
    ]


def sum_ring(parts, axis):
    parts = {2 * (n + 1): x for n, x in enumerate(parts)}
    for bit in bits_of(axis)[1:]:
        kept = {}
        for j in sorted({j & ~bit for j in parts}):
            got = swap(parts[j | bit].astype(BF16), axis, bit).astype(F32)
            kept[j] = got + parts[j].astype(F32) if j in parts else got
        parts = kept
    return parts[0]


def total_of(x, axis):
    for bit in bits_of(axis):
        x = x + swap(x, axis, bit)
    return x


def gate(*values):
    return lax.optimization_barrier(values)


def half_of(x, upper):
    rows = x.shape[0] // 2
    return lax.dynamic_slice_in_dim(x, jnp.where(upper, rows, 0), rows, 0)


class DpSum:
    def __init__(self, x, order, place):
        self.value, self.got, self.later = x, None, [(True, b) for b in order] + [(False, b) for b in order[::-1]]
        self.advance(place)

    def advance(self, place):
        if self.got is not None:
            halving, bit = self.later.pop(0)
            upper = (place & bit) != 0
            x, got = self.value, self.got
            if halving:
                x = half_of(x, upper) + got.astype(F32)
                if not self.later[0][0]:
                    x = x.astype(BF16)
            else:
                x = jnp.concatenate([jnp.where(upper, got, x), jnp.where(upper, x, got)], axis=0)
            self.value, self.got = x, None
        if self.later:
            halving, bit = self.later[0]
            send = half_of(self.value, (place & bit) == 0).astype(BF16) if halving else self.value
            self.got = swap(send, "dp", bit)

    def result(self, place):
        while self.later:
            self.advance(place)
        return self.value.astype(F32)


def body(
    layer_in,
    cotangent,
    lengths,
    languages,
    lang_weight,
    ln1_gain,
    ln1_bias,
    w_qkv,
    b_qv,
    w_out,
    b_out,
    ln2_gain,
    ln2_bias,
    w_up,
    b_up,
    w_down,
    b_down,
):
    groups = lax.axis_size("tensor")
    place = lax.axis_index("tensor")
    place_one = place.astype(jnp.int32).reshape(1)
    own_rows = layer_in.shape[0]
    local_heads = w_out.shape[0] // HD
    dp_place = lax.axis_index("dp")
    order_a = bits_of("dp")
    order_b = order_a[1:] + order_a[:1]

    width = layer_in.shape[1]

    def row(x):
        return x.reshape(1, -1)

    def tokens_of(kernel, kinds, ins, name, sums=0):
        outs = [((own_rows, width), kind) for kind in kinds] + [((n, width), F32) for n in ([sums] if sums else [])]
        return whole_call(kernel, outs, ins, name)

    (n1_own,) = tokens_of(norm_in_kernel, [BF16], (layer_in, row(ln1_gain), row(ln1_bias)), "norm_in")
    n1_far = gather_ring(n1_own, "tensor")
    n1 = gather_chip([n1_own], "tensor")
    near = len(n1)

    positions = place * own_rows + jnp.arange(own_rows, dtype=jnp.int32)
    weight = jnp.sum(jnp.where(jnp.arange(lang_weight.shape[0]) == languages[0], lang_weight, 0.0))
    live = jnp.where(positions < lengths[0], weight, 0.0)[:, None]
    top_own = (cotangent.astype(F32) * live).astype(BF16)

    pairs = b_qv.reshape(local_heads, 2, HD)
    bias_three = jnp.stack([pairs[:, 0], jnp.zeros_like(pairs[:, 0]), pairs[:, 1]], axis=1).reshape(1, -1)

    def project(x):
        return (nn(x, w_qkv) + bias_three).astype(BF16)

    mixed = [project(x) for x in n1]
    top_own, *rest = gate(top_own, *mixed, *n1_far)
    mixed, n1_far = rest[:near], rest[near:]
    top_far = gather_ring(top_own, "tensor")
    n1 += gather_chip(n1_far, "tensor")
    mixed += [project(x) for x in n1[near:]]
    slope_parts = slope_table(place * local_heads, local_heads, HEADS)
    heads_b, saved = attend_forward(mixed, place_one, lengths, slope_parts)
    rest = gate(*heads_b, *top_far)
    heads_b, top_far = list(rest[:groups]), list(rest[groups:])

    parts = [nn(x, w_out).astype(BF16) for x in heads_b[near:]]
    far_sum = sum_chip(parts, "tensor")
    rest = gate(*heads_b[:near], *far_sum)
    heads_b[:near], far_sum = rest[:near], rest[near:]
    attn_far = sum_ring(far_sum, "tensor")
    parts = [nn(x, w_out).astype(BF16) for x in heads_b[:near]]
    attn_near = sum_chip(parts, "tensor")[0]
    top = gather_chip([top_own] + top_far, "tensor")
    middle, n2_own = tokens_of(
        norm_mid_kernel, [F32, BF16], (layer_in, attn_near, attn_far, row(b_out), row(ln2_gain), row(ln2_bias)), "norm_mid"
    )
    n2_far = gather_ring(n2_own, "tensor")
    n2 = gather_chip([n2_own], "tensor")

    active, grad_pre, back, up_sums = mlp_both(n2, top[:near], w_up, w_down, b_up)
    square = w_up.shape[0] == w_up.shape[1]

    def mlp_weight_grads(lows, highs, **more):
        if square:
            return [weight_grads(lows, highs, stack=True, **more)]
        return [weight_grads(lows, **more), weight_grads(highs, **more)]

    near_sums = mlp_weight_grads((active, top[:near]), (n2, grad_pre), kind=F32)
    rest = gate(*back, *n2_far, *near_sums)
    back, n2_far, near_sums = list(rest[:near]), list(rest[near : -len(near_sums)]), rest[-len(near_sums) :]
    n2 += gather_chip(n2_far, "tensor")
    far_active, far_pre, far_back, far_sums = mlp_both(n2[near:], top[near:], w_up, w_down, b_up)
    g_b_up = up_sums + far_sums
    far_sum = sum_chip(far_back, "tensor")
    rest = gate(*far_sum, *far_active, *far_pre, *back, *active)
    far_sum, rest = list(rest[: len(far_sum)]), list(rest[len(far_sum) :])
    count = groups - near
    far_active, far_pre, back, active = rest[:count], rest[count : 2 * count], rest[2 * count : -near], rest[-near:]
    norm2_far = sum_ring(far_sum, "tensor")
    groups_of_far = (far_active, top[near:]), (n2[near:], far_pre)
    if square:
        mlp_grads = [weight_grads(*groups_of_far, base=near_sums[0], stack=True)]
    else:
        mlp_grads = [weight_grads(g, base=base) for g, base in zip(groups_of_far, near_sums)]
    *mlp_grads, back[0] = gate(*mlp_grads, back[0])
    mlp_grads = [lax.psum_scatter(x, "dp", scatter_dimension=0, tiled=True) for x in mlp_grads]
    active += far_active
    norm2_near = sum_chip(back, "tensor")[0]

    grad_middle, gm_own, mid_sums = tokens_of(
        norm_mid_back_kernel,
        [F32, BF16],
        (middle, norm2_near, norm2_far, cotangent, live, row(ln2_gain)),
        "norm_mid_back",
        4,
    )
    *active, gm_own, dp_place = gate(*active, gm_own, dp_place)
    gm_far = gather_ring(gm_own, "tensor")
    gm = gather_chip([gm_own], "tensor")

    mlp_sums = sum_chip([nn(x, w_down).astype(BF16) for x in active], "tensor")
    grad_heads = through([[x] for x in gm], w_out)
    rest = gate(*gm_far, *grad_heads, *mlp_sums, dp_place)
    dp_place = rest[-1]
    count = len(gm_far)
    gm_far, grad_heads, mlp_sums = list(rest[:count]), list(rest[count : count + near]), rest[count + near : -1]
    gm += gather_chip(gm_far, "tensor")
    grad_heads += through([[x] for x in gm[near:]], w_out)
    mlp_far = sum_ring(mlp_sums[1:], "tensor")

    parts = 2 if local_heads % 4 == 0 else 1
    grad_mixed, w_sums, columns, w_cols = [], [], [], w_qkv.shape[1] // parts
    for part in range(parts):
        *piece, sums = attend_backward(saved, heads_b, grad_heads, place_one, part, parts)
        *grad_heads, piece[0], dp_place = gate(*grad_heads, piece[0], dp_place)
        columns.append(sums[0])
        if w_sums:
            w_sums[-1].advance(dp_place)
            w_sums[-1].value, mlp_far, piece[near] = gate(w_sums[-1].value, mlp_far, piece[near])
        grad_mixed.append(piece)
        if part == 0:
            dp_place, *mlp_grads = gate(dp_place, *mlp_grads)
            mlp_grads = [lax.all_gather(x, "dp", axis=0, tiled=True) for x in mlp_grads]
        if part < parts - 1:
            w_part = weight_grads((n1, piece), (gm, heads_b))
            *grad_heads, w_part, dp_place = gate(*grad_heads, w_part, dp_place)
            w_sums.append(DpSum(w_part, order_a, dp_place))
    blocks = [[piece[j] for piece in grad_mixed] for j in range(groups)]
    far_sum = sum_chip(through(blocks[near:], w_qkv), "tensor")
    *far_sum, n1[0], blocks[0][0], dp_place = gate(*far_sum, n1[0], blocks[0][0], dp_place)
    norm1_far = sum_ring(far_sum, "tensor")
    last = [(n1, grad_mixed[-1])] + ([(gm, heads_b)] if parts == 1 else [])
    w_part = weight_grads(*last)
    blocks[0][0], w_part = gate(blocks[0][0], w_part)
    w_sums.append(DpSum(w_part, order_a, dp_place))
    norm1_near = sum_chip(through(blocks[:near], w_qkv), "tensor")[0]
    for _ in range(2):
        norm1_near, dp_place = gate(norm1_near, dp_place)
        for item in w_sums:
            item.advance(dp_place)
        rest = gate(norm1_near, *[item.value for item in w_sums])
        norm1_near = rest[0]
        for item, value in zip(w_sums, rest[1:]):
            item.value = value
    norm1_near, dp_place, *mlp_grads = gate(norm1_near, dp_place, *mlp_grads)
    down, up = (mlp_grads[0][: w_down.shape[0]], mlp_grads[0][w_down.shape[0] :]) if square else mlp_grads
    w_parts = [item.result(dp_place) for item in w_sums]
    out = w_parts[0][:, w_cols:].T
    qkv = jnp.concatenate([w_parts[0][:, :w_cols]] + w_parts[1:], axis=1)
    column_sums = jnp.concatenate(columns).reshape(local_heads, 3, HD)
    g_b_qv = jnp.stack([column_sums[:, 0], column_sums[:, 2]], axis=1).reshape(-1)
    grad_input, in_sums = tokens_of(
        norm_in_back_kernel, [BF16], (layer_in, norm1_near, norm1_far, grad_middle, row(ln1_gain)), "norm_in_back", 2
    )
    down, up = down.astype(F32), up.astype(F32)
    output = middle + (mlp_sums[0].astype(F32) + mlp_far) + b_down

    total = total_of(jnp.concatenate([mid_sums.reshape(-1), in_sums.reshape(-1)]), "tensor")
    total = total_of(jnp.concatenate([total, g_b_up, g_b_qv]), "dp")
    shared = [total[n * width : (n + 1) * width] for n in range(6)]
    hidden = b_up.shape[0]
    g_b_up, g_b_qv = total[6 * width : 6 * width + hidden], total[6 * width + hidden :]
    return (
        output.astype(BF16),
        grad_input,
        shared[4],
        shared[5],
        qkv,
        g_b_qv,
        out,
        shared[1],
        shared[2],
        shared[3],
        up,
        g_b_up,
        down,
        shared[0],
    )


def solution(mesh):
    rows, columns, flat = P("tensor", None), P(None, "tensor"), P("tensor")
    tokens = P(("dp", "tensor"), None)
    in_specs = (tokens, tokens, P("dp"), P("dp"), P(), P(), P(), columns, flat, rows, P(), P(), P(), columns, flat, rows, P())
    out_specs = (tokens, tokens, P(), P(), columns, flat, rows, P(), P(), P(), columns, flat, rows, P())
    return jax.shard_map(body, mesh=mesh, in_specs=in_specs, out_specs=out_specs, check_vma=False)
```

```python
import functools
import math
import jax
import jax.numpy as jnp
from jax import lax
from jax.sharding import PartitionSpec as P
from jax.experimental import pallas as pl
from jax.experimental.pallas import tpu as pltpu

HEADS = 16
HD = 64
LANES = 128
F32 = jnp.float32
BF16 = jnp.bfloat16
COST = pl.CostEstimate(flops=1000, transcendentals=0, bytes_accessed=1000)


def split3(x):
    hi = x.astype(BF16)
    rest = x - hi.astype(F32)
    mid = rest.astype(BF16)
    low = (rest - mid.astype(F32)).astype(BF16)
    return hi.astype(F32), mid.astype(F32), low.astype(F32)


def nt(a, b):
    return lax.dot_general(a, b, (((1,), (1,)), ((), ())), preferred_element_type=F32)


def nn(a, b):
    return jnp.dot(a, b, preferred_element_type=F32)


def at_lanes(lane, base, pairs):
    out = base
    for where, value in pairs:
        out = jnp.where(lane == where, value, out)
    return out


def key_side(span, first, length):
    pos = first + lax.broadcasted_iota(jnp.int32, (span, LANES), 0)
    lane = lax.broadcasted_iota(jnp.int32, (span, LANES), 1)
    low = (pos & 255).astype(F32)
    high = (pos - (pos & 255)).astype(F32)
    is_high = (lane == 64) | (lane == 66) | (lane == 68)
    is_low = (lane == 65) | (lane == 67) | (lane == 69)
    gone = jnp.where(pos < length, 0.0, -1e30)
    out = jnp.where(is_high, high, jnp.where(is_low, low, 0.0))
    out = jnp.where(lane == 70, gone, out)
    return jnp.where((lane >= 71) & (lane <= 73), 1.0, out)


def slope_side(lane, slope_parts):
    s1, s2, s3 = slope_parts
    out = jnp.where(lane < 66, s1, jnp.where(lane < 68, s2, s3))
    out = jnp.where(lane == 70, 1.0, out)
    return jnp.where((lane >= 64) & (lane <= 70), out, 0.0)


def wide(x):
    return jnp.concatenate([x, jnp.zeros_like(x)], axis=1)


def fwd_kernel(count, bq, place_ref, length_ref, slope_ref, *refs):
    mixed_refs, heads_refs = refs[:count], refs[count : 2 * count]
    qa_ref, ka_ref, va_ref, o_ref = refs[2 * count :]
    own = mixed_refs[0].shape[0]
    heads, span, _ = qa_ref.shape
    lane = lax.broadcasted_iota(jnp.int32, (1, LANES), 1)
    ones = jnp.where((lane >= 64) & (lane <= 66), 1.0, 0.0)
    for j in range(count):
        first = pl.multiple_of((place_ref[0] ^ j) * own, own)
        keys = key_side(own, first, length_ref[0])
        for h in range(heads):
            base = h * 3 * HD
            q = mixed_refs[j][:, base : base + HD].astype(F32) * (HD ** -0.5)
            k = mixed_refs[j][:, base + HD : base + 2 * HD].astype(F32)
            v = mixed_refs[j][:, base + 2 * HD : base + 3 * HD].astype(F32)
            parts = [slope_ref[h, n] for n in range(3)]
            rows = pl.ds(first, own)
            qa_ref[h, rows, :] = (wide(q) + slope_side(lane, parts)).astype(BF16)
            ka_ref[h, rows, :] = (wide(k) + keys).astype(BF16)
            va_ref[h, rows, :] = (wide(v) + ones).astype(BF16)

    def one_head(h, carry):
        for i in range(span // bq):
            rows = slice(i * bq, (i + 1) * bq)
            ext = (i + 1) * bq
            q = qa_ref[h, rows, :]
            s = nt(q, ka_ref[h, :ext, :])
            tq = lax.broadcasted_iota(jnp.int32, (bq, bq), 0)
            tk = lax.broadcasted_iota(jnp.int32, (bq, bq), 1)
            diag = jnp.where(tk <= tq, s[:, i * bq :], -3e38)
            s = jnp.concatenate([s[:, : i * bq], diag], axis=1) if i else diag
            m = jnp.max(s, axis=1, keepdims=True)
            p = jnp.exp(s - m).astype(BF16)
            o = nn(p, va_ref[h, :ext, :])
            total = o[:, HD : HD + 1]
            out = o / total
            l1, l2, l3 = split3(-(m + jnp.log(total)))
            o_ref[h, rows, :] = out.astype(BF16)
            logs = at_lanes(lane, q.astype(F32), ((71, l1), (72, l2), (73, l3)))
            qa_ref[h, rows, :] = logs.astype(BF16)
        return carry

    lax.fori_loop(0, heads, one_head, 0)
    for j in range(count):
        rows = pl.ds(pl.multiple_of((place_ref[0] ^ j) * own, own), own)
        heads_refs[j][...] = jnp.concatenate([o_ref[h, rows, :][:, :HD] for h in range(heads)], axis=1)


def attend_forward(mixed, place, length, slope_parts, bq=256):
    count = len(mixed)
    own = mixed[0].shape[0]
    span = own * count
    heads = mixed[0].shape[1] // (3 * HD)
    vm = pl.BlockSpec(memory_space=pltpu.VMEM)
    sm = pl.BlockSpec(memory_space=pltpu.SMEM)
    aug = jax.ShapeDtypeStruct((heads, span, LANES), BF16)
    res = pl.pallas_call(
        functools.partial(fwd_kernel, count, bq),
        out_shape=(jax.ShapeDtypeStruct((own, heads * HD), BF16),) * count + (aug, aug, aug),
        in_specs=[sm, sm, sm] + [vm] * count,
        out_specs=(vm,) * (count + 3),
        scratch_shapes=[pltpu.VMEM((heads, span, LANES), BF16)],
        compiler_params=pltpu.CompilerParams(vmem_limit_bytes=60 << 20),
        cost_estimate=COST,
        name="attend_forward",
    )(place, length, slope_parts, *mixed)
    return res[:count], res[count:]


def bwd_kernel(count, bk, bq, place_ref, qa_ref, ka_ref, va_ref, *refs):
    heads_refs, grad_refs, out_refs = refs[:count], refs[count : 2 * count], refs[2 * count : 3 * count]
    sums_ref, da_ref, dqt_ref, dk_ref, dv_ref = refs[3 * count :]
    own = heads_refs[0].shape[0]
    heads, span, _ = qa_ref.shape
    lane = lax.broadcasted_iota(jnp.int32, (1, LANES), 1)
    for j in range(count):
        rows = pl.ds(pl.multiple_of((place_ref[0] ^ j) * own, own), own)
        for h in range(heads):
            o = heads_refs[j][:, h * HD : (h + 1) * HD].astype(F32)
            g = grad_refs[j][:, h * HD : (h + 1) * HD].astype(F32)
            d1, d2, d3 = split3(-jnp.sum(o * g, axis=1, keepdims=True))
            da_ref[h, rows, :] = at_lanes(lane, wide(g), ((64, d1), (65, d2), (66, d3))).astype(BF16)

    def one_head(h, carry):
        for j in range(span // bk):
            cols = slice(j * bk, (j + 1) * bk)
            k = ka_ref[h, cols, :]
            v = va_ref[h, cols, :]
            kt = k[:, :HD].T
            start = j * bk
            dk = jnp.zeros((bk, LANES), F32)
            dv = jnp.zeros((bk, LANES), F32)
            while start < span:
                stop = min(span, (start // bq + 1) * bq)
                q = qa_ref[h, start:stop, :]
                d = da_ref[h, start:stop, :]
                p = jnp.exp(nt(k, q))
                if start == j * bk:
                    tk = lax.broadcasted_iota(jnp.int32, (bk, stop - start), 0)
                    tq = lax.broadcasted_iota(jnp.int32, (bk, stop - start), 1)
                    p = jnp.where(tk <= tq, p, 0.0)
                dp = nt(v, d)
                ds = (p * dp).astype(BF16)
                dv = dv + nn(p.astype(BF16), d)
                dk = dk + nn(ds, q)
                part = nn(kt, ds)
                if j == 0:
                    dqt_ref[h, :, start:stop] = part
                else:
                    dqt_ref[h, :, start:stop] += part
                start = stop
            dk_ref[h, cols, :] = dk
            dv_ref[h, cols, :] = dv
        return carry

    lax.fori_loop(0, heads, one_head, 0)
    for j in range(count):
        first = pl.multiple_of((place_ref[0] ^ j) * own, own)
        rows = pl.ds(first, own)
        pieces = []
        for h in range(heads):
            pieces += [dqt_ref[h, :, rows].T * (HD ** -0.5), dk_ref[h, rows, :HD], dv_ref[h, rows, :HD]]
        rounded = jnp.concatenate(pieces, axis=1).astype(BF16)
        out_refs[j][...] = rounded
        sums = jnp.sum(rounded.astype(F32), axis=0, keepdims=True)
        sums_ref[...] = sums if j == 0 else sums_ref[...] + sums


def attend_backward(saved, heads_b, grad_heads, place, part, parts, bk=256, bq=2048):
    heads, span, _ = saved[0].shape
    heads = heads // parts
    count = len(heads_b)
    own = span // count
    vm = pl.BlockSpec(memory_space=pltpu.VMEM)
    sm = pl.BlockSpec(memory_space=pltpu.SMEM)
    aug = pl.BlockSpec((heads, span, LANES), lambda i: (part, 0, 0))
    flat = pl.BlockSpec((own, heads * HD), lambda i: (0, part))
    out = pl.BlockSpec((own, heads * 3 * HD), lambda i: (0, 0))
    return pl.pallas_call(
        functools.partial(bwd_kernel, count, bk, bq),
        grid=(1,),
        out_shape=(jax.ShapeDtypeStruct((own, heads * 3 * HD), BF16),) * count
        + (jax.ShapeDtypeStruct((1, heads * 3 * HD), F32),),
        in_specs=[sm] + [aug] * 3 + [flat] * (2 * count),
        out_specs=(out,) * count + (pl.BlockSpec((1, heads * 3 * HD), lambda i: (0, 0)),),
        scratch_shapes=[
            pltpu.VMEM((heads, span, LANES), BF16),
            pltpu.VMEM((heads, HD, span), F32),
            pltpu.VMEM((heads, span, LANES), F32),
            pltpu.VMEM((heads, span, LANES), F32),
        ],
        compiler_params=pltpu.CompilerParams(vmem_limit_bytes=60 << 20),
        cost_estimate=COST,
        name="attend_backward",
    )(place, *saved, *heads_b, *grad_heads)


def slope_table(first, count, total):
    ids = (first + jnp.arange(count, dtype=jnp.int32)).astype(F32)
    slopes = jnp.exp2(-8.0 * (ids + 1.0) / total)
    return jnp.stack(split3(slopes), axis=1)


eps = 1e-05


def whole_call(kernel, outs, ins, name, smem=0):
    vm = pl.BlockSpec(memory_space=pltpu.VMEM)
    sm = pl.BlockSpec(memory_space=pltpu.SMEM)
    return pl.pallas_call(
        kernel,
        out_shape=tuple(jax.ShapeDtypeStruct(shape, kind) for shape, kind in outs),
        in_specs=[sm] * smem + [vm] * (len(ins) - smem),
        out_specs=(vm,) * len(outs),
        compiler_params=pltpu.CompilerParams(vmem_limit_bytes=60 << 20),
        cost_estimate=COST,
        name=name,
    )(*ins)


def tn(a, b):
    return lax.dot_general(a, b, (((0,), (0,)), ((), ())), preferred_element_type=F32)


def weight_kernel(count, spots, based, *refs):
    out_ref = refs[-1]
    for n, (row, column) in enumerate(spots):
        lefts, rights = [refs[m * count : (m + 1) * count] for m in (2 * n, 2 * n + 1)]
        rows, width = lefts[0].shape[1], rights[0].shape[1]
        for top in range(0, rows, 256):
            size = min(256, rows - top)
            total = tn(lefts[0][:, top : top + size], rights[0][...])
            for left, right in zip(lefts[1:], rights[1:]):
                total = total + tn(left[:, top : top + size], right[...])
            spot = (slice(row + top, row + top + size), slice(column, column + width))
            if based:
                total = total + refs[-2][spot]
            out_ref[spot] = total.astype(out_ref.dtype)


def weight_grads(*groups, base=None, kind=BF16, stack=False):
    count = len(groups[0][0])
    ins = [x for lefts, rights in groups for x in list(lefts) + list(rights)]
    spots, row, column = [], 0, 0
    for lefts, rights in groups:
        spots.append((row, column))
        row, column = (row + lefts[0].shape[1], 0) if stack else (0, column + rights[0].shape[1])
    last = groups[-1]
    shape = (spots[-1][0] + last[0][0].shape[1], spots[-1][1] + last[1][0].shape[1])
    if base is not None:
        ins.append(base)
    kernel = functools.partial(weight_kernel, count, spots, base is not None)
    return whole_call(kernel, [(shape, kind)], ins, "weight_grads")[0]


def through_kernel(count, parts, w_ref, *refs):
    outs = refs[count * parts :]
    width = w_ref.shape[1] // parts
    for j in range(count):
        total = nt(refs[j * parts][...], w_ref[:, :width])
        for p in range(1, parts):
            total = total + nt(refs[j * parts + p][...], w_ref[:, p * width : (p + 1) * width])
        outs[j][...] = total.astype(BF16)


def through(blocks, w):
    count, parts = len(blocks), len(blocks[0])
    shape = (blocks[0][0].shape[0], w.shape[0])
    ins = [w] + [x for block in blocks for x in block]
    return list(whole_call(functools.partial(through_kernel, count, parts), [(shape, BF16)] * count, ins, "through"))


def unit_of(values):
    centre = jnp.mean(values, axis=-1, keepdims=True)
    shifted = values - centre
    factor = lax.rsqrt(jnp.mean(shifted * shifted, axis=-1, keepdims=True) + eps)
    return shifted * factor, factor


def rows_call(kernel, scalars, rows_in, whole_in, kinds, sums, name, tile=256):
    own, width = rows_in[0].shape
    tile = min(tile, own)

    def spec(x):
        return pl.BlockSpec((tile, x.shape[1]), lambda i: (i, 0))

    whole = [pl.BlockSpec(x.shape, lambda i: (0, 0)) for x in whole_in]
    outs = [jax.ShapeDtypeStruct((own, width), kind) for kind in kinds]
    out_specs = [pl.BlockSpec((tile, width), lambda i: (i, 0)) for _ in kinds]
    if sums:
        outs.append(jax.ShapeDtypeStruct((sums, width), F32))
        out_specs.append(pl.BlockSpec((sums, width), lambda i: (0, 0)))
    return pl.pallas_call(
        kernel,
        grid=(own // tile,),
        out_shape=tuple(outs),
        in_specs=[pl.BlockSpec(memory_space=pltpu.SMEM)] * len(scalars) + [spec(x) for x in rows_in] + whole,
        out_specs=tuple(out_specs),
        compiler_params=pltpu.CompilerParams(vmem_limit_bytes=60 << 20),
        cost_estimate=COST,
        name=name,
    )(*scalars, *rows_in, *whole_in)


def add_rows(sums_ref, rows):
    new = jnp.concatenate(rows, axis=0)
    first = pl.program_id(0) == 0
    sums_ref[...] = jnp.where(first, new, sums_ref[...] + new)


def norm_in_kernel(x_ref, gain_ref, bias_ref, out_ref):
    unit, _ = unit_of(x_ref[...].astype(F32))
    out_ref[...] = (unit * gain_ref[...] + bias_ref[...]).astype(BF16)


def three(a_ref, b_ref, far_ref):
    return (a_ref[...].astype(F32) + b_ref[...].astype(F32)) + far_ref[...].astype(F32)


def norm_mid_kernel(x_ref, a_ref, b_ref, far_ref, bo_ref, gain_ref, bias_ref, mid_ref, out_ref):
    mid = x_ref[...].astype(F32) + three(a_ref, b_ref, far_ref) + bo_ref[...]
    mid_ref[...] = mid
    unit, _ = unit_of(mid)
    out_ref[...] = (unit * gain_ref[...] + bias_ref[...]).astype(BF16)


def back_of(grad, values, gain):
    unit, factor = unit_of(values)
    d = grad * gain
    inner = jnp.mean(d * unit, axis=-1, keepdims=True)
    sums = [jnp.sum(grad * unit, axis=0, keepdims=True), jnp.sum(grad, axis=0, keepdims=True)]
    return factor * (d - jnp.mean(d, axis=-1, keepdims=True) - unit * inner), sums


def norm_mid_back_kernel(
    first_ref, length_ref, weight_ref, mid_ref, a_ref, b_ref, far_ref, top_ref, gain_ref, grad_ref, rounded_ref, sums_ref
):
    back, sums = back_of(three(a_ref, b_ref, far_ref), mid_ref[...], gain_ref[...])
    rows = top_ref.shape[0]
    pos = first_ref[0] + pl.program_id(0) * rows + lax.broadcasted_iota(jnp.int32, (rows, 1), 0)
    top = top_ref[...].astype(F32) * jnp.where(pos < length_ref[0], weight_ref[0], 0.0)
    grad_mid = top + back
    grad_ref[...] = grad_mid
    rounded_ref[...] = grad_mid.astype(BF16)
    add_rows(sums_ref, [jnp.sum(top, axis=0, keepdims=True), jnp.sum(grad_mid, axis=0, keepdims=True)] + sums)


def norm_in_back_kernel(x_ref, a_ref, b_ref, far_ref, mid_ref, gain_ref, grad_ref, sums_ref):
    back, sums = back_of(three(a_ref, b_ref, far_ref), x_ref[...].astype(F32), gain_ref[...])
    grad_ref[...] = (mid_ref[...] + back).astype(BF16)
    add_rows(sums_ref, sums)


def unpack_kernel(cols, heads_cols, upper_ref, *refs):
    qkv_ref, out_ref = refs[-2:]
    for p in range(len(refs) // 2 - 1):
        sent, got = refs[2 * p][...].astype(F32), refs[2 * p + 1][...].astype(F32)
        rows = sent.shape[0]
        upper = upper_ref[p] != 0
        for n, x in enumerate((jnp.where(upper, got, sent), jnp.where(upper, sent, got))):
            spot = slice(n * rows, (n + 1) * rows)
            qkv_ref[spot, p * cols : (p + 1) * cols] = x[:, :cols]
            if p == 0:
                out_ref[:, spot] = x[:, cols : cols + heads_cols].T


def mlp_kernel(count, tile, w_up_ref, w_down_ref, b_up_ref, *refs):
    n2_refs, top_refs, act_refs, pre_refs, back_refs = [refs[n * count : (n + 1) * count] for n in range(5)]
    sums_ref = refs[-1]
    sums_ref[...] = jnp.zeros_like(sums_ref)
    root = (2.0 / math.pi) ** 0.5

    for j in range(count):

        def step(i, carry):
            rows = pl.ds(pl.multiple_of(i * tile, tile), tile)
            pre = nn(n2_refs[j][rows, :], w_up_ref[...]) + b_up_ref[...]
            grad = nt(top_refs[j][rows, :], w_down_ref[...])
            square = pre * pre
            tanh = jnp.tanh(pre * (root + (root * 0.044715) * square))
            half = 0.5 + 0.5 * tanh
            act_refs[j][rows, :] = (pre * half).astype(BF16)
            slope = half + (0.5 * pre) * (1.0 - tanh * tanh) * (root + (root * 0.134145) * square)
            inner = (grad * slope).astype(BF16)
            pre_refs[j][rows, :] = inner
            sums_ref[...] += jnp.sum(inner.astype(F32), axis=0, keepdims=True)
            back_refs[j][rows, :] = nt(inner, w_up_ref[...]).astype(BF16)
            return carry

        lax.fori_loop(0, n2_refs[j].shape[0] // tile, step, 0)


def mlp_both(n2, top, w_up, w_down, b_up):
    count = len(n2)
    own, width = n2[0].shape
    hidden = w_up.shape[1]
    vm = pl.BlockSpec(memory_space=pltpu.VMEM)
    inner = jax.ShapeDtypeStruct((own, hidden), BF16)
    outer = jax.ShapeDtypeStruct((own, width), BF16)
    res = pl.pallas_call(
        functools.partial(mlp_kernel, count, min(own, 256)),
        out_shape=(inner,) * (2 * count) + (outer,) * count + (jax.ShapeDtypeStruct((1, hidden), F32),),
        in_specs=[vm] * (3 + 2 * count),
        out_specs=(vm,) * (3 * count + 1),
        compiler_params=pltpu.CompilerParams(vmem_limit_bytes=60 << 20),
        cost_estimate=COST,
        name="mlp_both",
    )(w_up, w_down, b_up.reshape(1, -1), *n2, *top)
    return list(res[:count]), list(res[count : 2 * count]), list(res[2 * count : -1]), res[-1][0]


def swap(x, axis, bit):
    return lax.ppermute(x, axis, [(i, i ^ bit) for i in range(lax.axis_size(axis))])


def bits_of(axis):
    return [1 << n for n in range(lax.axis_size(axis).bit_length() - 1)]


def gather_ring(x, axis):
    blocks = {0: x}
    for bit in bits_of(axis)[1:]:
        blocks.update({j ^ bit: swap(b, axis, bit) for j, b in list(blocks.items())})
    return [blocks[j] for j in sorted(blocks) if j]


def gather_chip(blocks, axis):
    return [x for b in blocks for x in (b, swap(b, axis, 1))]


def sum_chip(parts, axis):
    return [
        (parts[j].astype(F32) + swap(parts[j + 1], axis, 1).astype(F32)).astype(BF16)
        for j in range(0, len(parts), 2)
    ]


def sum_ring(parts, axis):
    parts = {2 * (n + 1): x for n, x in enumerate(parts)}
    for bit in bits_of(axis)[1:]:
        kept = {}
        for j in sorted({j & ~bit for j in parts}):
            got = swap(parts[j | bit].astype(BF16), axis, bit)
            kept[j] = got.astype(F32) + parts[j].astype(F32) if j in parts else got
        parts = kept
    return parts[0]


def total_of(x, axis):
    for bit in bits_of(axis):
        x = x + swap(x, axis, bit)
    return x


def gate(*values):
    return lax.optimization_barrier(values)


def half_of(x, upper):
    rows = x.shape[0] // 2
    return lax.dynamic_slice_in_dim(x, jnp.where(upper, rows, 0), rows, 0)


class DpSum:
    def __init__(self, x, order, place):
        self.value, self.got, self.later = x, None, [(True, b) for b in order] + [(False, b) for b in order[::-1]]
        self.send(place)

    def send(self, place):
        halving, bit = self.later[0]
        send = half_of(self.value, (place & bit) == 0).astype(BF16) if halving else self.value
        self.got = swap(send, "dp", bit)

    def take(self, place):
        halving, bit = self.later.pop(0)
        upper = (place & bit) != 0
        x, got = self.value, self.got
        if halving:
            x = half_of(x, upper).astype(F32) + got.astype(F32)
            if not self.later[0][0]:
                x = x.astype(BF16)
        else:
            x = jnp.concatenate([jnp.where(upper, got, x), jnp.where(upper, x, got)], axis=0)
        self.value = x


def body(
    layer_in,
    cotangent,
    lengths,
    languages,
    lang_weight,
    ln1_gain,
    ln1_bias,
    w_qkv,
    b_qv,
    w_out,
    b_out,
    ln2_gain,
    ln2_bias,
    w_up,
    b_up,
    w_down,
    b_down,
):
    groups = lax.axis_size("tensor")
    place = lax.axis_index("tensor")
    place_one = place.astype(jnp.int32).reshape(1)
    own_rows = layer_in.shape[0]
    local_heads = w_out.shape[0] // HD
    dp_place = lax.axis_index("dp")
    order_a = bits_of("dp")
    order_b = order_a[1:] + order_a[:1]

    width = layer_in.shape[1]

    def row(x):
        return x.reshape(1, -1)

    (n1_own,) = rows_call(norm_in_kernel, [], [layer_in], [row(ln1_gain), row(ln1_bias)], [BF16], 0, "norm_in")
    n1_far = gather_ring(n1_own, "tensor")
    n1 = gather_chip([n1_own], "tensor")
    near = len(n1)

    positions = place * own_rows + jnp.arange(own_rows, dtype=jnp.int32)
    weight = jnp.sum(jnp.where(jnp.arange(lang_weight.shape[0]) == languages[0], lang_weight, 0.0))
    live = jnp.where(positions < lengths[0], weight, 0.0)
    top_own = (cotangent.astype(F32) * live[:, None]).astype(BF16)

    pairs = b_qv.reshape(local_heads, 2, HD)
    bias_three = jnp.stack([pairs[:, 0], jnp.zeros_like(pairs[:, 0]), pairs[:, 1]], axis=1).reshape(1, -1)

    def project(x):
        return (nn(x, w_qkv) + bias_three).astype(BF16)

    mixed = [project(x) for x in n1]
    top_own, *rest = gate(top_own, *mixed, *n1_far)
    mixed, n1_far = rest[:near], rest[near:]
    top_far = gather_ring(top_own, "tensor")
    n1 += gather_chip(n1_far, "tensor")
    mixed += [project(x) for x in n1[near:]]
    slope_parts = slope_table(place * local_heads, local_heads, HEADS)
    heads_b, saved = attend_forward(mixed, place_one, lengths, slope_parts)
    rest = gate(*heads_b, *top_far)
    heads_b, top_far = list(rest[:groups]), list(rest[groups:])

    parts = [nn(x, w_out).astype(BF16) for x in heads_b[near:]]
    far_sum = sum_chip(parts, "tensor")
    rest = gate(*heads_b[:near], *far_sum)
    heads_b[:near], far_sum = rest[:near], rest[near:]
    attn_far = sum_ring(far_sum, "tensor")
    attn_near = [nn(x, w_out).astype(BF16) for x in heads_b[:near]]
    attn_near[1] = swap(attn_near[1], "tensor", 1)
    top = gather_chip([top_own] + top_far, "tensor")
    middle, n2_own = rows_call(
        norm_mid_kernel,
        [],
        [layer_in, *attn_near, attn_far],
        [row(b_out), row(ln2_gain), row(ln2_bias)],
        [F32, BF16],
        0,
        "norm_mid",
    )
    n2_far = gather_ring(n2_own, "tensor")
    n2 = gather_chip([n2_own], "tensor")

    active, grad_pre, back, up_sums = mlp_both(n2, top[:near], w_up, w_down, b_up)
    square = w_up.shape[0] == w_up.shape[1]

    def mlp_weight_grads(lows, highs, **more):
        if square:
            return [weight_grads(lows, highs, stack=True, **more)]
        return [weight_grads(lows, **more), weight_grads(highs, **more)]

    near_sums = mlp_weight_grads((active, top[:near]), (n2, grad_pre), kind=F32)
    rest = gate(*back, *n2_far, *near_sums)
    back, n2_far, near_sums = list(rest[:near]), list(rest[near : -len(near_sums)]), rest[-len(near_sums) :]
    n2 += gather_chip(n2_far, "tensor")
    far_active, far_pre, far_back, far_sums = mlp_both(n2[near:], top[near:], w_up, w_down, b_up)
    g_b_up = up_sums + far_sums
    far_sum = sum_chip(far_back, "tensor")
    rest = gate(*far_sum, *far_active, *far_pre, *back, *active)
    far_sum, rest = list(rest[: len(far_sum)]), list(rest[len(far_sum) :])
    count = groups - near
    far_active, far_pre, back, active = rest[:count], rest[count : 2 * count], rest[2 * count : -near], rest[-near:]
    norm2_far = sum_ring(far_sum, "tensor")
    groups_of_far = (far_active, top[near:]), (n2[near:], far_pre)
    if square:
        mlp_grads = [weight_grads(*groups_of_far, base=near_sums[0], stack=True)]
    else:
        mlp_grads = [weight_grads(g, base=base) for g, base in zip(groups_of_far, near_sums)]
    *mlp_grads, back[0] = gate(*mlp_grads, back[0])
    mlp_grads = [lax.psum_scatter(x, "dp", scatter_dimension=0, tiled=True) for x in mlp_grads]
    active += far_active
    back[1] = swap(back[1], "tensor", 1)
    grad_middle, gm_own, mid_sums = rows_call(
        norm_mid_back_kernel,
        [(place * own_rows).astype(jnp.int32).reshape(1), lengths, weight.reshape(1)],
        [middle, *back, norm2_far, cotangent],
        [row(ln2_gain)],
        [F32, BF16],
        4,
        "norm_mid_back",
    )
    *active, gm_own, dp_place = gate(*active, gm_own, dp_place)
    gm_far = gather_ring(gm_own, "tensor")
    gm = gather_chip([gm_own], "tensor")

    mlp_sums = sum_chip([nn(x, w_down).astype(BF16) for x in active], "tensor")
    grad_heads = through([[x] for x in gm], w_out)
    rest = gate(*gm_far, *grad_heads, *mlp_sums, dp_place)
    dp_place = rest[-1]
    count = len(gm_far)
    gm_far, grad_heads, mlp_sums = list(rest[:count]), list(rest[count : count + near]), rest[count + near : -1]
    gm += gather_chip(gm_far, "tensor")
    grad_heads += through([[x] for x in gm[near:]], w_out)
    mlp_far = sum_ring(mlp_sums[1:], "tensor")

    parts = 2 if local_heads % 4 == 0 else 1
    grad_mixed, w_sums, columns, w_cols = [], [], [], w_qkv.shape[1] // parts
    for part in range(parts):
        *piece, sums = attend_backward(saved, heads_b, grad_heads, place_one, part, parts)
        *grad_heads, piece[0], dp_place = gate(*grad_heads, piece[0], dp_place)
        columns.append(sums[0])
        if w_sums:
            w_sums[-1].take(dp_place)
            w_sums[-1].send(dp_place)
            w_sums[-1].value, mlp_far, piece[near] = gate(w_sums[-1].value, mlp_far, piece[near])
        grad_mixed.append(piece)
        if part == 0:
            dp_place, *mlp_grads = gate(dp_place, *mlp_grads)
            mlp_grads = [lax.all_gather(x, "dp", axis=0, tiled=True) for x in mlp_grads]
        if part < parts - 1:
            w_part = weight_grads((n1, piece), (gm, heads_b))
            *grad_heads, w_part, dp_place = gate(*grad_heads, w_part, dp_place)
            w_sums.append(DpSum(w_part, order_a, dp_place))
    blocks = [[piece[j] for piece in grad_mixed] for j in range(groups)]
    far_sum = sum_chip(through(blocks[near:], w_qkv), "tensor")
    *far_sum, n1[0], blocks[0][0], dp_place = gate(*far_sum, n1[0], blocks[0][0], dp_place)
    norm1_far = sum_ring(far_sum, "tensor")
    last = [(n1, grad_mixed[-1])] + ([(gm, heads_b)] if parts == 1 else [])
    w_part = weight_grads(*last)
    blocks[0][0], w_part = gate(blocks[0][0], w_part)
    w_sums.append(DpSum(w_part, order_b if parts > 1 else order_a, dp_place))
    norm1_near = through(blocks[:near], w_qkv)
    norm1_near[1] = swap(norm1_near[1], "tensor", 1)
    output = (middle + (mlp_sums[0].astype(F32) + mlp_far.astype(F32)) + b_down).astype(BF16)
    norm1_near[0], output, dp_place = gate(norm1_near[0], output, dp_place)
    if parts > 1:
        for item in w_sums:
            item.take(dp_place)
            item.send(dp_place)
        norm1_near[0], *values = gate(norm1_near[0], *[item.value for item in w_sums])
        for item, value in zip(w_sums, values):
            item.value = value
    grad_input, in_sums = rows_call(
        norm_in_back_kernel,
        [],
        [layer_in, *norm1_near, norm1_far, grad_middle],
        [row(ln1_gain)],
        [BF16],
        2,
        "norm_in_back",
    )
    in_sums, dp_place, *mlp_grads = gate(in_sums, dp_place, *mlp_grads)
    down, up = (mlp_grads[0][: w_down.shape[0]], mlp_grads[0][w_down.shape[0] :]) if square else mlp_grads
    down, up = down.astype(F32), up.astype(F32)
    for item in w_sums:
        item.take(dp_place)
        item.send(dp_place)
    down, up, *values = gate(down, up, *[item.value for item in w_sums])
    for item, value in zip(w_sums, values):
        item.value = value
    while max(len(item.later) for item in w_sums) > 1:
        for item in w_sums:
            if len(item.later) > 1:
                item.take(dp_place)
                item.send(dp_place)
    uppers = jnp.stack([(dp_place & item.later[0][1]).astype(jnp.int32) for item in w_sums])
    qkv, out = whole_call(
        functools.partial(unpack_kernel, w_cols, w_out.shape[0]),
        [(w_qkv.shape, F32), (w_out.shape, F32)],
        [uppers] + [x for item in w_sums for x in (item.value, item.got)],
        "unpack",
        smem=1,
    )
    column_sums = jnp.concatenate(columns).reshape(local_heads, 3, HD)
    g_b_qv = jnp.stack([column_sums[:, 0], column_sums[:, 2]], axis=1).reshape(-1)
    total = total_of(jnp.concatenate([mid_sums.reshape(-1), in_sums.reshape(-1)]), "tensor")
    total = total_of(jnp.concatenate([total, g_b_up, g_b_qv]), "dp")
    shared = [total[n * width : (n + 1) * width] for n in range(6)]
    hidden = b_up.shape[0]
    g_b_up, g_b_qv = total[6 * width : 6 * width + hidden], total[6 * width + hidden :]
    return (
        output,
        grad_input,
        shared[4],
        shared[5],
        qkv,
        g_b_qv,
        out,
        shared[1],
        shared[2],
        shared[3],
        up,
        g_b_up,
        down,
        shared[0],
    )


def solution(mesh):
    rows, columns, flat = P("tensor", None), P(None, "tensor"), P("tensor")
    tokens = P(("dp", "tensor"), None)
    in_specs = (tokens, tokens, P("dp"), P("dp"), P(), P(), P(), columns, flat, rows, P(), P(), P(), columns, flat, rows, P())
    out_specs = (tokens, tokens, P(), P(), columns, flat, rows, P(), P(), P(), columns, flat, rows, P())
    return jax.shard_map(body, mesh=mesh, in_specs=in_specs, out_specs=out_specs, check_vma=False)
```

```python
import functools
import math
import jax
import jax.numpy as jnp
from jax import lax
from jax.sharding import PartitionSpec as P
from jax.experimental import pallas as pl
from jax.experimental.pallas import tpu as pltpu

HEADS = 16
HD = 64
LANES = 128
F32 = jnp.float32
BF16 = jnp.bfloat16
COST = pl.CostEstimate(flops=1000, transcendentals=0, bytes_accessed=1000)


def split3(x):
    hi = x.astype(BF16)
    rest = x - hi.astype(F32)
    mid = rest.astype(BF16)
    low = (rest - mid.astype(F32)).astype(BF16)
    return hi.astype(F32), mid.astype(F32), low.astype(F32)


def nt(a, b):
    return lax.dot_general(a, b, (((1,), (1,)), ((), ())), preferred_element_type=F32)


def nn(a, b):
    return jnp.dot(a, b, preferred_element_type=F32)


def at_lanes(lane, base, pairs):
    out = base
    for where, value in pairs:
        out = jnp.where(lane == where, value, out)
    return out


def key_side(span, first, length):
    pos = first + lax.broadcasted_iota(jnp.int32, (span, HD), 0)
    lane = lax.broadcasted_iota(jnp.int32, (span, HD), 1)
    low = (pos & 255).astype(F32)
    high = (pos - (pos & 255)).astype(F32)
    out = jnp.where((lane == 1) | (lane == 3) | (lane == 5), low, 0.0)
    out = jnp.where((lane == 0) | (lane == 2) | (lane == 4), high, out)
    out = jnp.where(lane == 6, jnp.where(pos < length, 0.0, -1e30), out)
    return jnp.where((lane >= 7) & (lane <= 9), 1.0, out).astype(BF16)


def slope_side(rows, slope_parts):
    lane = lax.broadcasted_iota(jnp.int32, (rows, HD), 1)
    s1, s2, s3 = slope_parts
    out = jnp.where(lane < 2, s1, jnp.where(lane < 4, s2, s3))
    return jnp.where(lane < 6, out, jnp.where(lane == 6, 1.0, 0.0)).astype(BF16)


def beside(x, extra):
    return jnp.concatenate([x, extra], axis=1)


def fwd_kernel(count, bq, place_ref, length_ref, slope_ref, *refs):
    mixed_refs, heads_refs = refs[:count], refs[count : 2 * count]
    qa_ref, ka_ref, va_ref, o_ref, keys_ref = refs[2 * count :]
    own = mixed_refs[0].shape[0]
    heads, span, _ = o_ref.shape
    lane = lax.broadcasted_iota(jnp.int32, (1, LANES), 1)
    h = pl.program_id(0)

    def rows_of(j):
        return pl.ds(pl.multiple_of((place_ref[0] ^ j) * own, own), own)

    @pl.when(h == 0)
    def _():
        for j in range(count):
            keys_ref[rows_of(j), :] = key_side(own, (place_ref[0] ^ j) * own, length_ref[0])

    ones = (lax.broadcasted_iota(jnp.int32, (own, HD), 1) < 3).astype(F32).astype(BF16)
    slopes = slope_side(own, [slope_ref[h, n] for n in range(3)])
    for head in range(heads):

        @pl.when(h == head)
        def _(base=head * 3 * HD):
            for j in range(count):
                rows = rows_of(j)
                q = mixed_refs[j][:, base : base + HD] * jnp.asarray(HD ** -0.5, BF16)
                qa_ref[0, rows, :] = beside(q, slopes)
                ka_ref[0, rows, :] = beside(mixed_refs[j][:, base + HD : base + 2 * HD], keys_ref[rows, :])
                va_ref[0, rows, :] = beside(mixed_refs[j][:, base + 2 * HD : base + 3 * HD], ones)

    for i in range(span // bq):
        rows = slice(i * bq, (i + 1) * bq)
        ext = (i + 1) * bq
        q = qa_ref[0, rows, :]
        s = nt(q, ka_ref[0, :ext, :])
        tq = lax.broadcasted_iota(jnp.int32, (bq, bq), 0)
        tk = lax.broadcasted_iota(jnp.int32, (bq, bq), 1)
        diag = jnp.where(tk <= tq, s[:, i * bq :], -3e38)
        s = jnp.concatenate([s[:, : i * bq], diag], axis=1) if i else diag
        m = jnp.max(s, axis=1, keepdims=True)
        p = jnp.exp(s - m).astype(BF16)
        o = nn(p, va_ref[0, :ext, :])
        total = o[:, HD : HD + 1]
        out = o / total
        l1, l2, l3 = split3(-(m + jnp.log(total)))
        o_ref[h, rows, :] = out.astype(BF16)
        logs = at_lanes(lane, q.astype(F32), ((71, l1), (72, l2), (73, l3)))
        qa_ref[0, rows, :] = logs.astype(BF16)

    @pl.when(h == heads - 1)
    def _():
        for j in range(count):
            heads_refs[j][...] = jnp.concatenate([o_ref[n, rows_of(j), :][:, :HD] for n in range(heads)], axis=1)


def attend_forward(mixed, place, length, slope_parts, bq=256):
    count = len(mixed)
    own = mixed[0].shape[0]
    span = own * count
    heads = mixed[0].shape[1] // (3 * HD)
    vm = pl.BlockSpec(memory_space=pltpu.VMEM)
    sm = pl.BlockSpec(memory_space=pltpu.SMEM)
    aug = jax.ShapeDtypeStruct((heads, span, LANES), BF16)
    one = pl.BlockSpec((1, span, LANES), lambda i: (i, 0, 0))
    res = pl.pallas_call(
        functools.partial(fwd_kernel, count, bq),
        grid=(heads,),
        out_shape=(jax.ShapeDtypeStruct((own, heads * HD), BF16),) * count + (aug, aug, aug),
        in_specs=[sm, sm, sm] + [vm] * count,
        out_specs=(vm,) * count + (one, one, one),
        scratch_shapes=[pltpu.VMEM((heads, span, LANES), BF16), pltpu.VMEM((span, HD), BF16)],
        compiler_params=pltpu.CompilerParams(vmem_limit_bytes=60 << 20),
        cost_estimate=COST,
        name="attend_forward",
    )(place, length, slope_parts, *mixed)
    return res[:count], res[count:]


def bwd_kernel(count, bk, bq, place_ref, qa_ref, ka_ref, va_ref, *refs):
    heads_refs, grad_refs, out_refs = refs[:count], refs[count : 2 * count], refs[2 * count : 3 * count]
    sums_ref, da_ref, dqt_ref, dk_ref, dv_ref = refs[3 * count :]
    own = heads_refs[0].shape[0]
    heads, span, _ = da_ref.shape
    h = pl.program_id(0)

    def rows_of(j):
        return pl.ds(pl.multiple_of((place_ref[0] ^ j) * own, own), own)

    @pl.when(h == 0)
    def _():
        lane = lax.broadcasted_iota(jnp.int32, (1, HD), 1)
        for j in range(count):
            for n in range(heads):
                g = grad_refs[j][:, n * HD : (n + 1) * HD]
                o = heads_refs[j][:, n * HD : (n + 1) * HD].astype(F32)
                d1, d2, d3 = split3(-jnp.sum(o * g.astype(F32), axis=1, keepdims=True))
                extra = at_lanes(lane, jnp.zeros((own, HD), F32), ((0, d1), (1, d2), (2, d3)))
                da_ref[n, rows_of(j), :] = beside(g, extra.astype(BF16))

    for j in range(span // bk):
        cols = slice(j * bk, (j + 1) * bk)
        k = ka_ref[0, cols, :]
        v = va_ref[0, cols, :]
        kt = k[:, :HD].T
        start = j * bk
        dk = jnp.zeros((bk, LANES), F32)
        dv = jnp.zeros((bk, LANES), F32)
        while start < span:
            stop = min(span, (start // bq + 1) * bq)
            q = qa_ref[0, start:stop, :]
            d = da_ref[h, start:stop, :]
            p = jnp.exp(nt(k, q))
            if start == j * bk:
                tk = lax.broadcasted_iota(jnp.int32, (bk, stop - start), 0)
                tq = lax.broadcasted_iota(jnp.int32, (bk, stop - start), 1)
                p = jnp.where(tk <= tq, p, 0.0)
            dp = nt(v, d)
            ds = (p * dp).astype(BF16)
            dv = dv + nn(p.astype(BF16), d)
            dk = dk + nn(ds, q)
            part = nn(kt, ds)
            if j == 0:
                dqt_ref[h, :, start:stop] = part
            else:
                dqt_ref[h, :, start:stop] += part
            start = stop
        dk_ref[h, cols, :] = dk
        dv_ref[h, cols, :] = dv

    @pl.when(h == heads - 1)
    def _():
        for j in range(count):
            rows = rows_of(j)
            pieces = []
            for n in range(heads):
                pieces += [dqt_ref[n, :, rows].T * (HD ** -0.5), dk_ref[n, rows, :HD], dv_ref[n, rows, :HD]]
            rounded = jnp.concatenate(pieces, axis=1).astype(BF16)
            out_refs[j][...] = rounded
            sums = jnp.sum(rounded.astype(F32), axis=0, keepdims=True)
            sums_ref[...] = sums if j == 0 else sums_ref[...] + sums


def attend_backward(saved, heads_b, grad_heads, place, part, parts, bk=256, bq=2048):
    heads, span, _ = saved[0].shape
    heads = heads // parts
    count = len(heads_b)
    own = span // count
    vm = pl.BlockSpec(memory_space=pltpu.VMEM)
    sm = pl.BlockSpec(memory_space=pltpu.SMEM)
    aug = pl.BlockSpec((1, span, LANES), lambda i: (part * heads + i, 0, 0))
    flat = pl.BlockSpec((own, heads * HD), lambda i: (0, part))
    out = pl.BlockSpec((own, heads * 3 * HD), lambda i: (0, 0))
    return pl.pallas_call(
        functools.partial(bwd_kernel, count, bk, bq),
        grid=(heads,),
        out_shape=(jax.ShapeDtypeStruct((own, heads * 3 * HD), BF16),) * count
        + (jax.ShapeDtypeStruct((1, heads * 3 * HD), F32),),
        in_specs=[sm] + [aug] * 3 + [flat] * (2 * count),
        out_specs=(out,) * count + (pl.BlockSpec((1, heads * 3 * HD), lambda i: (0, 0)),),
        scratch_shapes=[
            pltpu.VMEM((heads, span, LANES), BF16),
            pltpu.VMEM((heads, HD, span), F32),
            pltpu.VMEM((heads, span, LANES), F32),
            pltpu.VMEM((heads, span, LANES), F32),
        ],
        compiler_params=pltpu.CompilerParams(vmem_limit_bytes=60 << 20),
        cost_estimate=COST,
        name="attend_backward",
    )(place, *saved, *heads_b, *grad_heads)


def slope_table(first, count, total):
    ids = (first + jnp.arange(count, dtype=jnp.int32)).astype(F32)
    slopes = jnp.exp2(-8.0 * (ids + 1.0) / total)
    return jnp.stack(split3(slopes), axis=1)


eps = 1e-05


def whole_call(kernel, outs, ins, name, smem=0):
    vm = pl.BlockSpec(memory_space=pltpu.VMEM)
    sm = pl.BlockSpec(memory_space=pltpu.SMEM)
    return pl.pallas_call(
        kernel,
        out_shape=tuple(jax.ShapeDtypeStruct(shape, kind) for shape, kind in outs),
        in_specs=[sm] * smem + [vm] * (len(ins) - smem),
        out_specs=(vm,) * len(outs),
        compiler_params=pltpu.CompilerParams(vmem_limit_bytes=60 << 20),
        cost_estimate=COST,
        name=name,
    )(*ins)


def tn(a, b):
    return lax.dot_general(a, b, (((0,), (0,)), ((), ())), preferred_element_type=F32)


def weight_kernel(count, spots, based, *refs):
    out_ref = refs[-1]
    for n, (row, column) in enumerate(spots):
        lefts, rights = [refs[m * count : (m + 1) * count] for m in (2 * n, 2 * n + 1)]
        rows, width = lefts[0].shape[1], rights[0].shape[1]
        for top in range(0, rows, 256):
            size = min(256, rows - top)
            total = tn(lefts[0][:, top : top + size], rights[0][...])
            for left, right in zip(lefts[1:], rights[1:]):
                total = total + tn(left[:, top : top + size], right[...])
            spot = (slice(row + top, row + top + size), slice(column, column + width))
            if based:
                total = total + refs[-2][spot]
            out_ref[spot] = total.astype(out_ref.dtype)


def weight_grads(*groups, base=None, kind=BF16, stack=False):
    count = len(groups[0][0])
    ins = [x for lefts, rights in groups for x in list(lefts) + list(rights)]
    spots, row, column = [], 0, 0
    for lefts, rights in groups:
        spots.append((row, column))
        row, column = (row + lefts[0].shape[1], 0) if stack else (0, column + rights[0].shape[1])
    last = groups[-1]
    shape = (spots[-1][0] + last[0][0].shape[1], spots[-1][1] + last[1][0].shape[1])
    if base is not None:
        ins.append(base)
    kernel = functools.partial(weight_kernel, count, spots, base is not None)
    return whole_call(kernel, [(shape, kind)], ins, "weight_grads")[0]


def through_kernel(count, parts, w_ref, *refs):
    outs = refs[count * parts :]
    width = w_ref.shape[1] // parts
    for j in range(count):
        total = nt(refs[j * parts][...], w_ref[:, :width])
        for p in range(1, parts):
            total = total + nt(refs[j * parts + p][...], w_ref[:, p * width : (p + 1) * width])
        outs[j][...] = total.astype(BF16)


def through(blocks, w):
    count, parts = len(blocks), len(blocks[0])
    shape = (blocks[0][0].shape[0], w.shape[0])
    ins = [w] + [x for block in blocks for x in block]
    return list(whole_call(functools.partial(through_kernel, count, parts), [(shape, BF16)] * count, ins, "through"))


def unit_of(values):
    centre = jnp.mean(values, axis=-1, keepdims=True)
    shifted = values - centre
    factor = lax.rsqrt(jnp.mean(shifted * shifted, axis=-1, keepdims=True) + eps)
    return shifted * factor, factor


def rows_call(kernel, scalars, rows_in, whole_in, kinds, sums, name, tile=256):
    own, width = rows_in[0].shape
    tile = min(tile, own)

    def spec(x):
        return pl.BlockSpec((tile, x.shape[1]), lambda i: (i, 0))

    whole = [pl.BlockSpec(x.shape, lambda i: (0, 0)) for x in whole_in]
    outs = [jax.ShapeDtypeStruct((own, width), kind) for kind in kinds]
    out_specs = [pl.BlockSpec((tile, width), lambda i: (i, 0)) for _ in kinds]
    if sums:
        outs.append(jax.ShapeDtypeStruct((sums, width), F32))
        out_specs.append(pl.BlockSpec((sums, width), lambda i: (0, 0)))
    return pl.pallas_call(
        kernel,
        grid=(own // tile,),
        out_shape=tuple(outs),
        in_specs=[pl.BlockSpec(memory_space=pltpu.SMEM)] * len(scalars) + [spec(x) for x in rows_in] + whole,
        out_specs=tuple(out_specs),
        compiler_params=pltpu.CompilerParams(vmem_limit_bytes=60 << 20),
        cost_estimate=COST,
        name=name,
    )(*scalars, *rows_in, *whole_in)


def add_rows(sums_ref, rows):
    new = jnp.concatenate(rows, axis=0)
    first = pl.program_id(0) == 0
    sums_ref[...] = jnp.where(first, new, sums_ref[...] + new)


def norm_in_kernel(x_ref, gain_ref, bias_ref, out_ref):
    unit, _ = unit_of(x_ref[...].astype(F32))
    out_ref[...] = (unit * gain_ref[...] + bias_ref[...]).astype(BF16)


def three(a_ref, b_ref, far_ref):
    return (a_ref[...].astype(F32) + b_ref[...].astype(F32)) + far_ref[...].astype(F32)


def norm_mid_kernel(x_ref, a_ref, b_ref, far_ref, bo_ref, gain_ref, bias_ref, mid_ref, out_ref):
    mid = x_ref[...].astype(F32) + three(a_ref, b_ref, far_ref) + bo_ref[...]
    mid_ref[...] = mid
    unit, _ = unit_of(mid)
    out_ref[...] = (unit * gain_ref[...] + bias_ref[...]).astype(BF16)


def back_of(grad, values, gain):
    unit, factor = unit_of(values)
    d = grad * gain
    inner = jnp.mean(d * unit, axis=-1, keepdims=True)
    sums = [jnp.sum(grad * unit, axis=0, keepdims=True), jnp.sum(grad, axis=0, keepdims=True)]
    return factor * (d - jnp.mean(d, axis=-1, keepdims=True) - unit * inner), sums


def norm_mid_back_kernel(
    first_ref, length_ref, weight_ref, mid_ref, a_ref, b_ref, far_ref, top_ref, gain_ref, grad_ref, rounded_ref, sums_ref
):
    back, sums = back_of(three(a_ref, b_ref, far_ref), mid_ref[...], gain_ref[...])
    rows = top_ref.shape[0]
    pos = first_ref[0] + pl.program_id(0) * rows + lax.broadcasted_iota(jnp.int32, (rows, 1), 0)
    top = top_ref[...].astype(F32) * jnp.where(pos < length_ref[0], weight_ref[0], 0.0)
    grad_mid = top + back
    grad_ref[...] = grad_mid
    rounded_ref[...] = grad_mid.astype(BF16)
    add_rows(sums_ref, [jnp.sum(top, axis=0, keepdims=True), jnp.sum(grad_mid, axis=0, keepdims=True)] + sums)


def norm_in_back_kernel(x_ref, a_ref, b_ref, far_ref, mid_ref, gain_ref, grad_ref, sums_ref):
    back, sums = back_of(three(a_ref, b_ref, far_ref), x_ref[...].astype(F32), gain_ref[...])
    grad_ref[...] = (mid_ref[...] + back).astype(BF16)
    add_rows(sums_ref, sums)


def unpack_kernel(cols, heads_cols, upper_ref, *refs):
    qkv_ref, out_ref = refs[-2:]
    for p in range(len(refs) // 2 - 1):
        sent, got = refs[2 * p][...].astype(F32), refs[2 * p + 1][...].astype(F32)
        rows = sent.shape[0]
        upper = upper_ref[p] != 0
        for n, x in enumerate((jnp.where(upper, got, sent), jnp.where(upper, sent, got))):
            spot = slice(n * rows, (n + 1) * rows)
            qkv_ref[spot, p * cols : (p + 1) * cols] = x[:, :cols]
            if p == 0:
                out_ref[:, spot] = x[:, cols : cols + heads_cols].T


def mlp_kernel(count, tile, w_up_ref, w_down_ref, b_up_ref, *refs):
    n2_refs, top_refs, act_refs, pre_refs, back_refs = [refs[n * count : (n + 1) * count] for n in range(5)]
    sums_ref = refs[-1]
    sums_ref[...] = jnp.zeros_like(sums_ref)
    root = (2.0 / math.pi) ** 0.5

    for j in range(count):

        def step(i, carry):
            rows = pl.ds(pl.multiple_of(i * tile, tile), tile)
            pre = nn(n2_refs[j][rows, :], w_up_ref[...]) + b_up_ref[...]
            grad = nt(top_refs[j][rows, :], w_down_ref[...])
            square = pre * pre
            tanh = jnp.tanh(pre * (root + (root * 0.044715) * square))
            half = 0.5 + 0.5 * tanh
            act_refs[j][rows, :] = (pre * half).astype(BF16)
            slope = half + (0.5 * pre) * (1.0 - tanh * tanh) * (root + (root * 0.134145) * square)
            inner = (grad * slope).astype(BF16)
            pre_refs[j][rows, :] = inner
            sums_ref[...] += jnp.sum(inner.astype(F32), axis=0, keepdims=True)
            back_refs[j][rows, :] = nt(inner, w_up_ref[...]).astype(BF16)
            return carry

        lax.fori_loop(0, n2_refs[j].shape[0] // tile, step, 0)


def mlp_both(n2, top, w_up, w_down, b_up):
    count = len(n2)
    own, width = n2[0].shape
    hidden = w_up.shape[1]
    vm = pl.BlockSpec(memory_space=pltpu.VMEM)
    inner = jax.ShapeDtypeStruct((own, hidden), BF16)
    outer = jax.ShapeDtypeStruct((own, width), BF16)
    res = pl.pallas_call(
        functools.partial(mlp_kernel, count, min(own, 256)),
        out_shape=(inner,) * (2 * count) + (outer,) * count + (jax.ShapeDtypeStruct((1, hidden), F32),),
        in_specs=[vm] * (3 + 2 * count),
        out_specs=(vm,) * (3 * count + 1),
        compiler_params=pltpu.CompilerParams(vmem_limit_bytes=60 << 20),
        cost_estimate=COST,
        name="mlp_both",
    )(w_up, w_down, b_up.reshape(1, -1), *n2, *top)
    return list(res[:count]), list(res[count : 2 * count]), list(res[2 * count : -1]), res[-1][0]


def swap(x, axis, bit):
    return lax.ppermute(x, axis, [(i, i ^ bit) for i in range(lax.axis_size(axis))])


def bits_of(axis):
    return [1 << n for n in range(lax.axis_size(axis).bit_length() - 1)]


def gather_ring(x, axis):
    blocks = {0: x}
    for bit in bits_of(axis)[1:]:
        blocks.update({j ^ bit: swap(b, axis, bit) for j, b in list(blocks.items())})
    return [blocks[j] for j in sorted(blocks) if j]


def gather_chip(blocks, axis):
    return [x for b in blocks for x in (b, swap(b, axis, 1))]


def sum_chip(parts, axis):
    return [
        (parts[j].astype(F32) + swap(parts[j + 1], axis, 1).astype(F32)).astype(BF16)
        for j in range(0, len(parts), 2)
    ]


def sum_ring(parts, axis):
    parts = {2 * (n + 1): x for n, x in enumerate(parts)}
    for bit in bits_of(axis)[1:]:
        kept = {}
        for j in sorted({j & ~bit for j in parts}):
            got = swap(parts[j | bit].astype(BF16), axis, bit)
            kept[j] = got.astype(F32) + parts[j].astype(F32) if j in parts else got
        parts = kept
    return parts[0]


def total_of(x, axis):
    for bit in bits_of(axis):
        x = x + swap(x, axis, bit)
    return x


def gate(*values):
    return lax.optimization_barrier(values)


def half_of(x, upper):
    rows = x.shape[0] // 2
    return lax.dynamic_slice_in_dim(x, jnp.where(upper, rows, 0), rows, 0)


class DpSum:
    def __init__(self, x, order, place):
        self.value, self.got, self.later = x, None, [(True, b) for b in order] + [(False, b) for b in order[::-1]]
        self.send(place)

    def send(self, place):
        halving, bit = self.later[0]
        send = half_of(self.value, (place & bit) == 0).astype(BF16) if halving else self.value
        self.got = swap(send, "dp", bit)

    def take(self, place):
        halving, bit = self.later.pop(0)
        upper = (place & bit) != 0
        x, got = self.value, self.got
        if halving:
            x = half_of(x, upper).astype(F32) + got.astype(F32)
            if not self.later[0][0]:
                x = x.astype(BF16)
        else:
            x = jnp.concatenate([jnp.where(upper, got, x), jnp.where(upper, x, got)], axis=0)
        self.value = x

    def result(self, place):
        while len(self.later) > 1:
            self.take(place)
            self.send(place)
        self.take(place)
        return self.value.astype(F32)


def step(items, place, critical):
    for item in items:
        item.take(place)
        item.send(place)
    critical, *values = gate(critical, *[item.value for item in items])
    for item, value in zip(items, values):
        item.value = value
    return critical


def body(
    layer_in,
    cotangent,
    lengths,
    languages,
    lang_weight,
    ln1_gain,
    ln1_bias,
    w_qkv,
    b_qv,
    w_out,
    b_out,
    ln2_gain,
    ln2_bias,
    w_up,
    b_up,
    w_down,
    b_down,
):
    groups = lax.axis_size("tensor")
    place = lax.axis_index("tensor")
    place_one = place.astype(jnp.int32).reshape(1)
    own_rows = layer_in.shape[0]
    local_heads = w_out.shape[0] // HD
    dp_place = lax.axis_index("dp")
    order_a = bits_of("dp")
    order_b = order_a[1:] + order_a[:1]

    width = layer_in.shape[1]

    def row(x):
        return x.reshape(1, -1)

    (n1_own,) = rows_call(norm_in_kernel, [], [layer_in], [row(ln1_gain), row(ln1_bias)], [BF16], 0, "norm_in")
    n1_far = gather_ring(n1_own, "tensor")
    n1 = gather_chip([n1_own], "tensor")
    near = len(n1)

    positions = place * own_rows + jnp.arange(own_rows, dtype=jnp.int32)
    weight = jnp.sum(jnp.where(jnp.arange(lang_weight.shape[0]) == languages[0], lang_weight, 0.0))
    live = jnp.where(positions < lengths[0], weight, 0.0)
    top_own = (cotangent.astype(F32) * live[:, None]).astype(BF16)

    pairs = b_qv.reshape(local_heads, 2, HD)
    bias_three = jnp.stack([pairs[:, 0], jnp.zeros_like(pairs[:, 0]), pairs[:, 1]], axis=1).reshape(1, -1)

    def project(x):
        return (nn(x, w_qkv) + bias_three).astype(BF16)

    mixed = [project(x) for x in n1]
    top_own, *rest = gate(top_own, *mixed, *n1_far)
    mixed, n1_far = rest[:near], rest[near:]
    top_far = gather_ring(top_own, "tensor")
    n1 += gather_chip(n1_far, "tensor")
    mixed += [project(x) for x in n1[near:]]
    slope_parts = slope_table(place * local_heads, local_heads, HEADS)
    heads_b, saved = attend_forward(mixed, place_one, lengths, slope_parts)
    rest = gate(*heads_b, *top_far)
    heads_b, top_far = list(rest[:groups]), list(rest[groups:])

    parts = [nn(x, w_out).astype(BF16) for x in heads_b[near:]]
    far_sum = sum_chip(parts, "tensor")
    rest = gate(*heads_b[:near], *far_sum)
    heads_b[:near], far_sum = rest[:near], rest[near:]
    attn_far = sum_ring(far_sum, "tensor")
    attn_near = [nn(x, w_out).astype(BF16) for x in heads_b[:near]]
    attn_near[1] = swap(attn_near[1], "tensor", 1)
    top = gather_chip([top_own] + top_far, "tensor")
    middle, n2_own = rows_call(
        norm_mid_kernel,
        [],
        [layer_in, *attn_near, attn_far],
        [row(b_out), row(ln2_gain), row(ln2_bias)],
        [F32, BF16],
        0,
        "norm_mid",
    )
    n2_far = gather_ring(n2_own, "tensor")
    n2 = gather_chip([n2_own], "tensor")

    active, grad_pre, back, up_sums = mlp_both(n2, top[:near], w_up, w_down, b_up)
    square = w_up.shape[0] == w_up.shape[1]

    def mlp_weight_grads(lows, highs, **more):
        if square:
            return [weight_grads(lows, highs, stack=True, **more)]
        return [weight_grads(lows, **more), weight_grads(highs, **more)]

    near_sums = mlp_weight_grads((active, top[:near]), (n2, grad_pre), kind=F32)
    rest = gate(*back, *n2_far, *near_sums)
    back, n2_far, near_sums = list(rest[:near]), list(rest[near : -len(near_sums)]), rest[-len(near_sums) :]
    n2 += gather_chip(n2_far, "tensor")
    far_active, far_pre, far_back, far_sums = mlp_both(n2[near:], top[near:], w_up, w_down, b_up)
    g_b_up = up_sums + far_sums
    far_sum = sum_chip(far_back, "tensor")
    rest = gate(*far_sum, *far_active, *far_pre, *back, *active)
    far_sum, rest = list(rest[: len(far_sum)]), list(rest[len(far_sum) :])
    count = groups - near
    far_active, far_pre, back, active = rest[:count], rest[count : 2 * count], rest[2 * count : -near], rest[-near:]
    norm2_far = sum_ring(far_sum, "tensor")
    groups_of_far = (far_active, top[near:]), (n2[near:], far_pre)
    if square:
        mlp_grads = [weight_grads(*groups_of_far, base=near_sums[0], stack=True)]
    else:
        mlp_grads = [weight_grads(g, base=base) for g, base in zip(groups_of_far, near_sums)]
    *mlp_grads, back[0] = gate(*mlp_grads, back[0])
    mlp_grads = [lax.psum_scatter(x, "dp", scatter_dimension=0, tiled=True) for x in mlp_grads]
    active += far_active
    back[1] = swap(back[1], "tensor", 1)
    grad_middle, gm_own, mid_sums = rows_call(
        norm_mid_back_kernel,
        [(place * own_rows).astype(jnp.int32).reshape(1), lengths, weight.reshape(1)],
        [middle, *back, norm2_far, cotangent],
        [row(ln2_gain)],
        [F32, BF16],
        4,
        "norm_mid_back",
    )
    *active, gm_own, dp_place = gate(*active, gm_own, dp_place)
    gm_far = gather_ring(gm_own, "tensor")
    gm = gather_chip([gm_own], "tensor")

    mlp_sums = sum_chip([nn(x, w_down).astype(BF16) for x in active], "tensor")
    grad_heads = through([[x] for x in gm], w_out)
    rest = gate(*gm_far, *grad_heads, *mlp_sums, dp_place)
    dp_place = rest[-1]
    count = len(gm_far)
    gm_far, grad_heads, mlp_sums = list(rest[:count]), list(rest[count : count + near]), rest[count + near : -1]
    gm += gather_chip(gm_far, "tensor")
    grad_heads += through([[x] for x in gm[near:]], w_out)
    mlp_far = sum_ring(mlp_sums[1:], "tensor")

    parts = 2 if local_heads % 4 == 0 else 1
    grad_mixed, w_sums, columns, w_cols = [], [], [], w_qkv.shape[1] // parts
    for part in range(parts):
        *piece, sums = attend_backward(saved, heads_b, grad_heads, place_one, part, parts)
        *grad_heads, piece[0], dp_place = gate(*grad_heads, piece[0], dp_place)
        columns.append(sums[0])
        if w_sums:
            w_sums[-1].take(dp_place)
            w_sums[-1].send(dp_place)
            w_sums[-1].value, mlp_far, piece[near] = gate(w_sums[-1].value, mlp_far, piece[near])
        grad_mixed.append(piece)
        if part == 0:
            dp_place, *mlp_grads = gate(dp_place, *mlp_grads)
            mlp_grads = [lax.all_gather(x, "dp", axis=0, tiled=True) for x in mlp_grads]
        if part < parts - 1:
            w_part = weight_grads((n1, piece), (gm, heads_b))
            *grad_heads, w_part, dp_place = gate(*grad_heads, w_part, dp_place)
            w_sums.append(DpSum(w_part, order_a, dp_place))
    blocks = [[piece[j] for piece in grad_mixed] for j in range(groups)]
    far_sum = sum_chip(through(blocks[near:], w_qkv), "tensor")
    *far_sum, n1[0], blocks[0][0], dp_place = gate(*far_sum, n1[0], blocks[0][0], dp_place)
    norm1_far = sum_ring(far_sum, "tensor")
    last = [(n1, grad_mixed[-1])] + ([(gm, heads_b)] if parts == 1 else [])
    w_part = weight_grads(*last)
    blocks[0][0], w_part = gate(blocks[0][0], w_part)
    w_sums.append(DpSum(w_part, order_a, dp_place))
    norm1_near = through(blocks[:near], w_qkv)
    norm1_near[1] = swap(norm1_near[1], "tensor", 1)
    output = (middle + (mlp_sums[0].astype(F32) + mlp_far.astype(F32)) + b_down).astype(BF16)
    norm1_near[0], output, dp_place = gate(norm1_near[0], output, dp_place)
    if parts > 1:
        norm1_near[0] = step(w_sums[:1], dp_place, norm1_near[0])
    grad_input, in_sums = rows_call(
        norm_in_back_kernel,
        [],
        [layer_in, *norm1_near, norm1_far, grad_middle],
        [row(ln1_gain)],
        [BF16],
        2,
        "norm_in_back",
    )
    in_sums, dp_place, *mlp_grads = gate(in_sums, dp_place, *mlp_grads)
    down, up = (mlp_grads[0][: w_down.shape[0]], mlp_grads[0][w_down.shape[0] :]) if square else mlp_grads
    down, up = down.astype(F32), up.astype(F32)
    in_sums = step(w_sums, dp_place, in_sums)
    down, up, w_sums[0].value = gate(down, up, w_sums[0].value)
    while max(len(item.later) for item in w_sums) > 1:
        for item in w_sums:
            if len(item.later) > 1:
                item.take(dp_place)
                item.send(dp_place)
    uppers = jnp.stack([(dp_place & item.later[0][1]).astype(jnp.int32) for item in w_sums])
    qkv, out = whole_call(
        functools.partial(unpack_kernel, w_cols, w_out.shape[0]),
        [(w_qkv.shape, F32), (w_out.shape, F32)],
        [uppers] + [x for item in w_sums for x in (item.value, item.got)],
        "unpack",
        smem=1,
    )
    column_sums = jnp.concatenate(columns).reshape(local_heads, 3, HD)
    g_b_qv = jnp.stack([column_sums[:, 0], column_sums[:, 2]], axis=1).reshape(-1)
    total = total_of(jnp.concatenate([mid_sums.reshape(-1), in_sums.reshape(-1)]), "tensor")
    total = total_of(jnp.concatenate([total, g_b_up, g_b_qv]), "dp")
    shared = [total[n * width : (n + 1) * width] for n in range(6)]
    hidden = b_up.shape[0]
    g_b_up, g_b_qv = total[6 * width : 6 * width + hidden], total[6 * width + hidden :]
    return (
        output,
        grad_input,
        shared[4],
        shared[5],
        qkv,
        g_b_qv,
        out,
        shared[1],
        shared[2],
        shared[3],
        up,
        g_b_up,
        down,
        shared[0],
    )


def solution(mesh):
    rows, columns, flat = P("tensor", None), P(None, "tensor"), P("tensor")
    tokens = P(("dp", "tensor"), None)
    in_specs = (tokens, tokens, P("dp"), P("dp"), P(), P(), P(), columns, flat, rows, P(), P(), P(), columns, flat, rows, P())
    out_specs = (tokens, tokens, P(), P(), columns, flat, rows, P(), P(), P(), columns, flat, rows, P())
    return jax.shard_map(body, mesh=mesh, in_specs=in_specs, out_specs=out_specs, check_vma=False)
```

```python
import functools
import math
import jax
import jax.numpy as jnp
from jax import lax
from jax.sharding import PartitionSpec as P
from jax.experimental import pallas as pl
from jax.experimental.pallas import tpu as pltpu

HEADS = 16
HD = 64
LANES = 128
F32 = jnp.float32
BF16 = jnp.bfloat16
COST = pl.CostEstimate(flops=1000, transcendentals=0, bytes_accessed=1000)


def split3(x):
    hi = x.astype(BF16)
    rest = x - hi.astype(F32)
    mid = rest.astype(BF16)
    low = (rest - mid.astype(F32)).astype(BF16)
    return hi.astype(F32), mid.astype(F32), low.astype(F32)


def nt(a, b):
    return lax.dot_general(a, b, (((1,), (1,)), ((), ())), preferred_element_type=F32)


def nn(a, b):
    return jnp.dot(a, b, preferred_element_type=F32)


def at_lanes(lane, base, pairs):
    out = base
    for where, value in pairs:
        out = jnp.where(lane == where, value, out)
    return out


def key_side(span, first, length):
    pos = first + lax.broadcasted_iota(jnp.int32, (span, HD), 0)
    lane = lax.broadcasted_iota(jnp.int32, (span, HD), 1)
    low = (pos & 255).astype(F32)
    high = (pos - (pos & 255)).astype(F32)
    out = jnp.where((lane == 1) | (lane == 3) | (lane == 5), low, 0.0)
    out = jnp.where((lane == 0) | (lane == 2) | (lane == 4), high, out)
    out = jnp.where(lane == 6, jnp.where(pos < length, 0.0, -1e30), out)
    return jnp.where((lane >= 7) & (lane <= 9), 1.0, out).astype(BF16)


def slope_side(rows, slope_parts):
    lane = lax.broadcasted_iota(jnp.int32, (rows, HD), 1)
    s1, s2, s3 = slope_parts
    out = jnp.where(lane < 2, s1, jnp.where(lane < 4, s2, s3))
    return jnp.where(lane < 6, out, jnp.where(lane == 6, 1.0, 0.0)).astype(BF16)


def beside(x, extra):
    return jnp.concatenate([x, extra], axis=1)


def fwd_kernel(count, bq, place_ref, length_ref, slope_ref, *refs):
    mixed_refs, heads_refs = refs[:count], refs[count : 2 * count]
    qa_ref, ka_ref, va_ref, o_ref, keys_ref = refs[2 * count :]
    own = mixed_refs[0].shape[0]
    heads, span, _ = o_ref.shape
    lane = lax.broadcasted_iota(jnp.int32, (1, LANES), 1)
    h = pl.program_id(0)

    def rows_of(j):
        return pl.ds(pl.multiple_of((place_ref[0] ^ j) * own, own), own)

    @pl.when(h == 0)
    def _():
        for j in range(count):
            keys_ref[rows_of(j), :] = key_side(own, (place_ref[0] ^ j) * own, length_ref[0])

    ones = (lax.broadcasted_iota(jnp.int32, (own, HD), 1) < 3).astype(F32).astype(BF16)
    slopes = slope_side(own, [slope_ref[h, n] for n in range(3)])
    for head in range(heads):

        @pl.when(h == head)
        def _(base=head * 3 * HD):
            for j in range(count):
                rows = rows_of(j)
                q = mixed_refs[j][:, base : base + HD] * jnp.asarray(HD ** -0.5, BF16)
                qa_ref[0, rows, :] = beside(q, slopes)
                ka_ref[0, rows, :] = beside(mixed_refs[j][:, base + HD : base + 2 * HD], keys_ref[rows, :])
                va_ref[0, rows, :] = beside(mixed_refs[j][:, base + 2 * HD : base + 3 * HD], ones)

    for i in range(span // bq):
        rows = slice(i * bq, (i + 1) * bq)
        ext = (i + 1) * bq
        q = qa_ref[0, rows, :]
        s = nt(q, ka_ref[0, :ext, :])
        tq = lax.broadcasted_iota(jnp.int32, (bq, bq), 0)
        tk = lax.broadcasted_iota(jnp.int32, (bq, bq), 1)
        diag = jnp.where(tk <= tq, s[:, i * bq :], -3e38)
        s = jnp.concatenate([s[:, : i * bq], diag], axis=1) if i else diag
        m = jnp.max(s, axis=1, keepdims=True)
        p = jnp.exp(s - m).astype(BF16)
        o = nn(p, va_ref[0, :ext, :])
        total = o[:, HD : HD + 1]
        out = o / total
        l1, l2, l3 = split3(-(m + jnp.log(total)))
        o_ref[h, rows, :] = out.astype(BF16)
        logs = at_lanes(lane, q.astype(F32), ((71, l1), (72, l2), (73, l3)))
        qa_ref[0, rows, :] = logs.astype(BF16)

    @pl.when(h == heads - 1)
    def _():
        for j in range(count):
            heads_refs[j][...] = jnp.concatenate([o_ref[n, rows_of(j), :][:, :HD] for n in range(heads)], axis=1)


def attend_forward(mixed, place, length, slope_parts, bq=512):
    count = len(mixed)
    own = mixed[0].shape[0]
    span = own * count
    heads = mixed[0].shape[1] // (3 * HD)
    vm = pl.BlockSpec(memory_space=pltpu.VMEM)
    sm = pl.BlockSpec(memory_space=pltpu.SMEM)
    aug = jax.ShapeDtypeStruct((heads, span, LANES), BF16)
    one = pl.BlockSpec((1, span, LANES), lambda i: (i, 0, 0))
    res = pl.pallas_call(
        functools.partial(fwd_kernel, count, bq),
        grid=(heads,),
        out_shape=(jax.ShapeDtypeStruct((own, heads * HD), BF16),) * count + (aug, aug, aug),
        in_specs=[sm, sm, sm] + [vm] * count,
        out_specs=(vm,) * count + (one, one, one),
        scratch_shapes=[pltpu.VMEM((heads, span, LANES), BF16), pltpu.VMEM((span, HD), BF16)],
        compiler_params=pltpu.CompilerParams(vmem_limit_bytes=60 << 20),
        cost_estimate=COST,
        name="attend_forward",
    )(place, length, slope_parts, *mixed)
    return res[:count], res[count:]


def bwd_kernel(count, bk, bq, place_ref, qa_ref, ka_ref, va_ref, *refs):
    heads_refs, grad_refs, out_refs = refs[:count], refs[count : 2 * count], refs[2 * count : 3 * count]
    sums_ref, da_ref, dqt_ref, dk_ref, dv_ref = refs[3 * count :]
    own = heads_refs[0].shape[0]
    heads, span, _ = da_ref.shape
    h = pl.program_id(0)

    def rows_of(j):
        return pl.ds(pl.multiple_of((place_ref[0] ^ j) * own, own), own)

    @pl.when(h == 0)
    def _():
        lane = lax.broadcasted_iota(jnp.int32, (1, HD), 1)
        for j in range(count):
            for n in range(heads):
                g = grad_refs[j][:, n * HD : (n + 1) * HD]
                o = heads_refs[j][:, n * HD : (n + 1) * HD].astype(F32)
                d1, d2, d3 = split3(-jnp.sum(o * g.astype(F32), axis=1, keepdims=True))
                extra = at_lanes(lane, jnp.zeros((own, HD), F32), ((0, d1), (1, d2), (2, d3)))
                da_ref[n, rows_of(j), :] = beside(g, extra.astype(BF16))

    for j in range(span // bk):
        cols = slice(j * bk, (j + 1) * bk)
        k = ka_ref[0, cols, :]
        v = va_ref[0, cols, :]
        kt = k[:, :HD].T
        start = j * bk
        dk = jnp.zeros((bk, LANES), F32)
        dv = jnp.zeros((bk, LANES), F32)
        while start < span:
            stop = min(span, (start // bq + 1) * bq)
            q = qa_ref[0, start:stop, :]
            d = da_ref[h, start:stop, :]
            p = jnp.exp(nt(k, q))
            if start == j * bk:
                tk = lax.broadcasted_iota(jnp.int32, (bk, stop - start), 0)
                tq = lax.broadcasted_iota(jnp.int32, (bk, stop - start), 1)
                p = jnp.where(tk <= tq, p, 0.0)
            dp = nt(v, d)
            ds = (p * dp).astype(BF16)
            dv = dv + nn(p.astype(BF16), d)
            dk = dk + nn(ds, q)
            part = nn(kt, ds)
            if j == 0:
                dqt_ref[h, :, start:stop] = part
            else:
                dqt_ref[h, :, start:stop] += part
            start = stop
        dk_ref[h, cols, :] = dk
        dv_ref[h, cols, :] = dv

    @pl.when(h == heads - 1)
    def _():
        for j in range(count):
            rows = rows_of(j)
            pieces = []
            for n in range(heads):
                pieces += [dqt_ref[n, :, rows].T * (HD ** -0.5), dk_ref[n, rows, :HD], dv_ref[n, rows, :HD]]
            rounded = jnp.concatenate(pieces, axis=1).astype(BF16)
            out_refs[j][...] = rounded
            sums = jnp.sum(rounded.astype(F32), axis=0, keepdims=True)
            sums_ref[...] = sums if j == 0 else sums_ref[...] + sums


def attend_backward(saved, heads_b, grad_heads, place, part, parts, bk=256, bq=2048):
    heads, span, _ = saved[0].shape
    heads = heads // parts
    count = len(heads_b)
    own = span // count
    vm = pl.BlockSpec(memory_space=pltpu.VMEM)
    sm = pl.BlockSpec(memory_space=pltpu.SMEM)
    aug = pl.BlockSpec((1, span, LANES), lambda i: (part * heads + i, 0, 0))
    flat = pl.BlockSpec((own, heads * HD), lambda i: (0, part))
    out = pl.BlockSpec((own, heads * 3 * HD), lambda i: (0, 0))
    return pl.pallas_call(
        functools.partial(bwd_kernel, count, bk, bq),
        grid=(heads,),
        out_shape=(jax.ShapeDtypeStruct((own, heads * 3 * HD), BF16),) * count
        + (jax.ShapeDtypeStruct((1, heads * 3 * HD), F32),),
        in_specs=[sm] + [aug] * 3 + [flat] * (2 * count),
        out_specs=(out,) * count + (pl.BlockSpec((1, heads * 3 * HD), lambda i: (0, 0)),),
        scratch_shapes=[
            pltpu.VMEM((heads, span, LANES), BF16),
            pltpu.VMEM((heads, HD, span), F32),
            pltpu.VMEM((heads, span, LANES), F32),
            pltpu.VMEM((heads, span, LANES), F32),
        ],
        compiler_params=pltpu.CompilerParams(vmem_limit_bytes=60 << 20),
        cost_estimate=COST,
        name="attend_backward",
    )(place, *saved, *heads_b, *grad_heads)


def slope_table(first, count, total):
    ids = (first + jnp.arange(count, dtype=jnp.int32)).astype(F32)
    slopes = jnp.exp2(-8.0 * (ids + 1.0) / total)
    return jnp.stack(split3(slopes), axis=1)


eps = 1e-05


def whole_call(kernel, outs, ins, name, smem=0):
    vm = pl.BlockSpec(memory_space=pltpu.VMEM)
    sm = pl.BlockSpec(memory_space=pltpu.SMEM)
    return pl.pallas_call(
        kernel,
        out_shape=tuple(jax.ShapeDtypeStruct(shape, kind) for shape, kind in outs),
        in_specs=[sm] * smem + [vm] * (len(ins) - smem),
        out_specs=(vm,) * len(outs),
        compiler_params=pltpu.CompilerParams(vmem_limit_bytes=60 << 20),
        cost_estimate=COST,
        name=name,
    )(*ins)


def tn(a, b):
    return lax.dot_general(a, b, (((0,), (0,)), ((), ())), preferred_element_type=F32)


def weight_kernel(count, spots, based, *refs):
    out_ref = refs[-1]
    for n, (row, column) in enumerate(spots):
        lefts, rights = [refs[m * count : (m + 1) * count] for m in (2 * n, 2 * n + 1)]
        rows, width = lefts[0].shape[1], rights[0].shape[1]
        for top in range(0, rows, 256):
            size = min(256, rows - top)
            total = tn(lefts[0][:, top : top + size], rights[0][...])
            for left, right in zip(lefts[1:], rights[1:]):
                total = total + tn(left[:, top : top + size], right[...])
            spot = (slice(row + top, row + top + size), slice(column, column + width))
            if based:
                total = total + refs[-2][spot]
            out_ref[spot] = total.astype(out_ref.dtype)


def weight_grads(*groups, base=None, kind=BF16, stack=False):
    count = len(groups[0][0])
    ins = [x for lefts, rights in groups for x in list(lefts) + list(rights)]
    spots, row, column = [], 0, 0
    for lefts, rights in groups:
        spots.append((row, column))
        row, column = (row + lefts[0].shape[1], 0) if stack else (0, column + rights[0].shape[1])
    last = groups[-1]
    shape = (spots[-1][0] + last[0][0].shape[1], spots[-1][1] + last[1][0].shape[1])
    if base is not None:
        ins.append(base)
    kernel = functools.partial(weight_kernel, count, spots, base is not None)
    return whole_call(kernel, [(shape, kind)], ins, "weight_grads")[0]


def through_kernel(count, parts, w_ref, *refs):
    outs = refs[count * parts :]
    width = w_ref.shape[1] // parts
    for j in range(count):
        total = nt(refs[j * parts][...], w_ref[:, :width])
        for p in range(1, parts):
            total = total + nt(refs[j * parts + p][...], w_ref[:, p * width : (p + 1) * width])
        outs[j][...] = total.astype(BF16)


def through(blocks, w):
    count, parts = len(blocks), len(blocks[0])
    shape = (blocks[0][0].shape[0], w.shape[0])
    ins = [w] + [x for block in blocks for x in block]
    return list(whole_call(functools.partial(through_kernel, count, parts), [(shape, BF16)] * count, ins, "through"))


def unit_of(values):
    centre = jnp.mean(values, axis=-1, keepdims=True)
    shifted = values - centre
    factor = lax.rsqrt(jnp.mean(shifted * shifted, axis=-1, keepdims=True) + eps)
    return shifted * factor, factor


def rows_call(kernel, scalars, rows_in, whole_in, kinds, sums, name, tile=256):
    own, width = rows_in[0].shape
    tile = min(tile, own)

    def spec(x):
        return pl.BlockSpec((tile, x.shape[1]), lambda i: (i, 0))

    whole = [pl.BlockSpec(x.shape, lambda i: (0, 0)) for x in whole_in]
    outs = [jax.ShapeDtypeStruct((own, width), kind) for kind in kinds]
    out_specs = [pl.BlockSpec((tile, width), lambda i: (i, 0)) for _ in kinds]
    if sums:
        outs.append(jax.ShapeDtypeStruct((sums, width), F32))
        out_specs.append(pl.BlockSpec((sums, width), lambda i: (0, 0)))
    return pl.pallas_call(
        kernel,
        grid=(own // tile,),
        out_shape=tuple(outs),
        in_specs=[pl.BlockSpec(memory_space=pltpu.SMEM)] * len(scalars) + [spec(x) for x in rows_in] + whole,
        out_specs=tuple(out_specs),
        compiler_params=pltpu.CompilerParams(vmem_limit_bytes=60 << 20),
        cost_estimate=COST,
        name=name,
    )(*scalars, *rows_in, *whole_in)


def add_rows(sums_ref, rows):
    new = jnp.concatenate(rows, axis=0)
    first = pl.program_id(0) == 0
    sums_ref[...] = jnp.where(first, new, sums_ref[...] + new)


def norm_in_kernel(x_ref, gain_ref, bias_ref, out_ref):
    unit, _ = unit_of(x_ref[...].astype(F32))
    out_ref[...] = (unit * gain_ref[...] + bias_ref[...]).astype(BF16)


def three(a_ref, b_ref, far_ref):
    return (a_ref[...].astype(F32) + b_ref[...].astype(F32)) + far_ref[...].astype(F32)


def pair_sums_kernel(*refs):
    ins, outs = refs[: 2 * (len(refs) // 3)], refs[2 * (len(refs) // 3) :]
    for n, out_ref in enumerate(outs):
        out_ref[...] = (ins[2 * n][...].astype(F32) + ins[2 * n + 1][...].astype(F32)).astype(BF16)


def norm_mid_kernel(x_ref, a_ref, b_ref, far_ref, bo_ref, gain_ref, bias_ref, mid_ref, out_ref):
    mid = x_ref[...].astype(F32) + three(a_ref, b_ref, far_ref) + bo_ref[...]
    mid_ref[...] = mid
    unit, _ = unit_of(mid)
    out_ref[...] = (unit * gain_ref[...] + bias_ref[...]).astype(BF16)


def back_of(grad, values, gain):
    unit, factor = unit_of(values)
    d = grad * gain
    inner = jnp.mean(d * unit, axis=-1, keepdims=True)
    sums = [jnp.sum(grad * unit, axis=0, keepdims=True), jnp.sum(grad, axis=0, keepdims=True)]
    return factor * (d - jnp.mean(d, axis=-1, keepdims=True) - unit * inner), sums


def norm_mid_back_kernel(
    first_ref, length_ref, weight_ref, mid_ref, a_ref, b_ref, far_ref, top_ref, gain_ref, grad_ref, rounded_ref, sums_ref
):
    back, sums = back_of(three(a_ref, b_ref, far_ref), mid_ref[...], gain_ref[...])
    rows = top_ref.shape[0]
    pos = first_ref[0] + pl.program_id(0) * rows + lax.broadcasted_iota(jnp.int32, (rows, 1), 0)
    top = top_ref[...].astype(F32) * jnp.where(pos < length_ref[0], weight_ref[0], 0.0)
    grad_mid = top + back
    grad_ref[...] = grad_mid
    rounded_ref[...] = grad_mid.astype(BF16)
    add_rows(sums_ref, [jnp.sum(top, axis=0, keepdims=True), jnp.sum(grad_mid, axis=0, keepdims=True)] + sums)


def norm_in_back_kernel(x_ref, a_ref, b_ref, far_ref, mid_ref, gain_ref, grad_ref, sums_ref):
    back, sums = back_of(three(a_ref, b_ref, far_ref), x_ref[...].astype(F32), gain_ref[...])
    grad_ref[...] = (mid_ref[...] + back).astype(BF16)
    add_rows(sums_ref, sums)


def unpack_kernel(cols, heads_cols, upper_ref, *refs):
    qkv_ref, out_ref = refs[-2:]
    for p in range(len(refs) // 2 - 1):
        sent, got = refs[2 * p][...].astype(F32), refs[2 * p + 1][...].astype(F32)
        rows = sent.shape[0]
        upper = upper_ref[p] != 0
        for n, x in enumerate((jnp.where(upper, got, sent), jnp.where(upper, sent, got))):
            spot = slice(n * rows, (n + 1) * rows)
            qkv_ref[spot, p * cols : (p + 1) * cols] = x[:, :cols]
            if p == 0:
                out_ref[:, spot] = x[:, cols : cols + heads_cols].T


def mlp_kernel(count, tile, w_up_ref, w_down_ref, b_up_ref, *refs):
    n2_refs, top_refs, act_refs, pre_refs, back_refs = [refs[n * count : (n + 1) * count] for n in range(5)]
    sums_ref = refs[-1]
    sums_ref[...] = jnp.zeros_like(sums_ref)
    root = (2.0 / math.pi) ** 0.5

    for j in range(count):

        def step(i, carry):
            rows = pl.ds(pl.multiple_of(i * tile, tile), tile)
            pre = nn(n2_refs[j][rows, :], w_up_ref[...]) + b_up_ref[...]
            grad = nt(top_refs[j][rows, :], w_down_ref[...])
            square = pre * pre
            tanh = jnp.tanh(pre * (root + (root * 0.044715) * square))
            half = 0.5 + 0.5 * tanh
            act_refs[j][rows, :] = (pre * half).astype(BF16)
            slope = half + (0.5 * pre) * (1.0 - tanh * tanh) * (root + (root * 0.134145) * square)
            inner = (grad * slope).astype(BF16)
            pre_refs[j][rows, :] = inner
            sums_ref[...] += jnp.sum(inner.astype(F32), axis=0, keepdims=True)
            back_refs[j][rows, :] = nt(inner, w_up_ref[...]).astype(BF16)
            return carry

        lax.fori_loop(0, n2_refs[j].shape[0] // tile, step, 0)


def mlp_both(n2, top, w_up, w_down, b_up):
    count = len(n2)
    own, width = n2[0].shape
    hidden = w_up.shape[1]
    vm = pl.BlockSpec(memory_space=pltpu.VMEM)
    inner = jax.ShapeDtypeStruct((own, hidden), BF16)
    outer = jax.ShapeDtypeStruct((own, width), BF16)
    res = pl.pallas_call(
        functools.partial(mlp_kernel, count, min(own, 256)),
        out_shape=(inner,) * (2 * count) + (outer,) * count + (jax.ShapeDtypeStruct((1, hidden), F32),),
        in_specs=[vm] * (3 + 2 * count),
        out_specs=(vm,) * (3 * count + 1),
        compiler_params=pltpu.CompilerParams(vmem_limit_bytes=60 << 20),
        cost_estimate=COST,
        name="mlp_both",
    )(w_up, w_down, b_up.reshape(1, -1), *n2, *top)
    return list(res[:count]), list(res[count : 2 * count]), list(res[2 * count : -1]), res[-1][0]


def swap(x, axis, bit):
    return lax.ppermute(x, axis, [(i, i ^ bit) for i in range(lax.axis_size(axis))])


def bits_of(axis):
    return [1 << n for n in range(lax.axis_size(axis).bit_length() - 1)]


def gather_ring(x, axis):
    blocks = {0: x}
    for bit in bits_of(axis)[1:]:
        blocks.update({j ^ bit: swap(b, axis, bit) for j, b in list(blocks.items())})
    return [blocks[j] for j in sorted(blocks) if j]


def gather_chip(blocks, axis):
    return [x for b in blocks for x in (b, swap(b, axis, 1))]


def sum_chip(parts, axis):
    return [
        (parts[j].astype(F32) + swap(parts[j + 1], axis, 1).astype(F32)).astype(BF16)
        for j in range(0, len(parts), 2)
    ]


def sum_ring(parts, axis):
    parts = {2 * (n + 1): x for n, x in enumerate(parts)}
    for bit in bits_of(axis)[1:]:
        kept = {}
        for j in sorted({j & ~bit for j in parts}):
            got = swap(parts[j | bit].astype(BF16), axis, bit)
            kept[j] = got.astype(F32) + parts[j].astype(F32) if j in parts else got
        parts = kept
    return parts[0]


def total_of(x, axis):
    for bit in bits_of(axis):
        x = x + swap(x, axis, bit)
    return x


def gate(*values):
    return lax.optimization_barrier(values)


def half_of(x, upper):
    rows = x.shape[0] // 2
    return lax.dynamic_slice_in_dim(x, jnp.where(upper, rows, 0), rows, 0)


class DpSum:
    def __init__(self, x, order, place):
        self.value, self.got, self.later = x, None, [(True, b) for b in order] + [(False, b) for b in order[::-1]]
        self.send(place)

    def send(self, place):
        halving, bit = self.later[0]
        send = half_of(self.value, (place & bit) == 0).astype(BF16) if halving else self.value
        self.got = swap(send, "dp", bit)

    def take(self, place):
        halving, bit = self.later.pop(0)
        upper = (place & bit) != 0
        x, got = self.value, self.got
        if halving:
            x = half_of(x, upper).astype(F32) + got.astype(F32)
            if not self.later[0][0]:
                x = x.astype(BF16)
        else:
            x = jnp.concatenate([jnp.where(upper, got, x), jnp.where(upper, x, got)], axis=0)
        self.value = x

    def result(self, place):
        while len(self.later) > 1:
            self.take(place)
            self.send(place)
        self.take(place)
        return self.value.astype(F32)


def step(items, place, critical):
    for item in items:
        item.take(place)
        item.send(place)
    critical, *values = gate(critical, *[item.value for item in items])
    for item, value in zip(items, values):
        item.value = value
    return critical


def body(
    layer_in,
    cotangent,
    lengths,
    languages,
    lang_weight,
    ln1_gain,
    ln1_bias,
    w_qkv,
    b_qv,
    w_out,
    b_out,
    ln2_gain,
    ln2_bias,
    w_up,
    b_up,
    w_down,
    b_down,
):
    groups = lax.axis_size("tensor")
    place = lax.axis_index("tensor")
    place_one = place.astype(jnp.int32).reshape(1)
    own_rows = layer_in.shape[0]
    local_heads = w_out.shape[0] // HD
    dp_place = lax.axis_index("dp")
    order_a = bits_of("dp")
    order_b = order_a[1:] + order_a[:1]

    width = layer_in.shape[1]

    def row(x):
        return x.reshape(1, -1)

    (n1_own,) = rows_call(norm_in_kernel, [], [layer_in], [row(ln1_gain), row(ln1_bias)], [BF16], 0, "norm_in")
    n1_far = gather_ring(n1_own, "tensor")
    n1 = gather_chip([n1_own], "tensor")
    near = len(n1)

    positions = place * own_rows + jnp.arange(own_rows, dtype=jnp.int32)
    weight = jnp.sum(jnp.where(jnp.arange(lang_weight.shape[0]) == languages[0], lang_weight, 0.0))
    live = jnp.where(positions < lengths[0], weight, 0.0)
    top_own = (cotangent.astype(F32) * live[:, None]).astype(BF16)

    pairs = b_qv.reshape(local_heads, 2, HD)
    bias_three = jnp.stack([pairs[:, 0], jnp.zeros_like(pairs[:, 0]), pairs[:, 1]], axis=1).reshape(1, -1)

    def project(x):
        return (nn(x, w_qkv) + bias_three).astype(BF16)

    mixed = [project(x) for x in n1]
    top_own, *rest = gate(top_own, *mixed, *n1_far)
    mixed, n1_far = rest[:near], rest[near:]
    top_far = gather_ring(top_own, "tensor")
    n1 += gather_chip(n1_far, "tensor")
    mixed += [project(x) for x in n1[near:]]
    slope_parts = slope_table(place * local_heads, local_heads, HEADS)
    heads_b, saved = attend_forward(mixed, place_one, lengths, slope_parts)
    rest = gate(*heads_b, *top_far)
    heads_b, top_far = list(rest[:groups]), list(rest[groups:])

    parts = [nn(x, w_out).astype(BF16) for x in heads_b[near:]]
    far_sum = sum_chip(parts, "tensor")
    rest = gate(*heads_b[:near], *far_sum)
    heads_b[:near], far_sum = rest[:near], rest[near:]
    attn_far = sum_ring(far_sum, "tensor")
    attn_near = [nn(x, w_out).astype(BF16) for x in heads_b[:near]]
    attn_near[1] = swap(attn_near[1], "tensor", 1)
    top = gather_chip([top_own] + top_far, "tensor")
    middle, n2_own = rows_call(
        norm_mid_kernel,
        [],
        [layer_in, *attn_near, attn_far],
        [row(b_out), row(ln2_gain), row(ln2_bias)],
        [F32, BF16],
        0,
        "norm_mid",
    )
    n2_far = gather_ring(n2_own, "tensor")
    n2 = gather_chip([n2_own], "tensor")

    active, grad_pre, back, up_sums = mlp_both(n2, top[:near], w_up, w_down, b_up)
    square = w_up.shape[0] == w_up.shape[1]

    def mlp_weight_grads(lows, highs, **more):
        if square:
            return [weight_grads(lows, highs, stack=True, **more)]
        return [weight_grads(lows, **more), weight_grads(highs, **more)]

    near_sums = mlp_weight_grads((active, top[:near]), (n2, grad_pre), kind=F32)
    rest = gate(*back, *n2_far, *near_sums)
    back, n2_far, near_sums = list(rest[:near]), list(rest[near : -len(near_sums)]), rest[-len(near_sums) :]
    n2 += gather_chip(n2_far, "tensor")
    far_active, far_pre, far_back, far_sums = mlp_both(n2[near:], top[near:], w_up, w_down, b_up)
    g_b_up = up_sums + far_sums
    far_sum = sum_chip(far_back, "tensor")
    rest = gate(*far_sum, *far_active, *far_pre, *back, *active)
    far_sum, rest = list(rest[: len(far_sum)]), list(rest[len(far_sum) :])
    count = groups - near
    far_active, far_pre, back, active = rest[:count], rest[count : 2 * count], rest[2 * count : -near], rest[-near:]
    norm2_far = sum_ring(far_sum, "tensor")
    groups_of_far = (far_active, top[near:]), (n2[near:], far_pre)
    if square:
        mlp_grads = [weight_grads(*groups_of_far, base=near_sums[0], stack=True)]
    else:
        mlp_grads = [weight_grads(g, base=base) for g, base in zip(groups_of_far, near_sums)]
    *mlp_grads, back[0] = gate(*mlp_grads, back[0])
    mlp_grads = [lax.psum_scatter(x, "dp", scatter_dimension=0, tiled=True) for x in mlp_grads]
    active += far_active
    back[1] = swap(back[1], "tensor", 1)
    grad_middle, gm_own, mid_sums = rows_call(
        norm_mid_back_kernel,
        [(place * own_rows).astype(jnp.int32).reshape(1), lengths, weight.reshape(1)],
        [middle, *back, norm2_far, cotangent],
        [row(ln2_gain)],
        [F32, BF16],
        4,
        "norm_mid_back",
    )
    *active, gm_own, dp_place = gate(*active, gm_own, dp_place)
    gm_far = gather_ring(gm_own, "tensor")
    gm = gather_chip([gm_own], "tensor")

    mlp_parts = [nn(x, w_down).astype(BF16) for x in active]
    pairs = [mlp_parts[j] if j % 2 == 0 else swap(mlp_parts[j], "tensor", 1) for j in range(groups)]
    mlp_sums = rows_call(pair_sums_kernel, [], pairs, [], [BF16] * (groups // 2), 0, "pair_sums")
    grad_heads = through([[x] for x in gm], w_out)
    rest = gate(*gm_far, *grad_heads, *mlp_sums, dp_place)
    dp_place = rest[-1]
    count = len(gm_far)
    gm_far, grad_heads, mlp_sums = list(rest[:count]), list(rest[count : count + near]), rest[count + near : -1]
    gm += gather_chip(gm_far, "tensor")
    grad_heads += through([[x] for x in gm[near:]], w_out)
    mlp_far = sum_ring(mlp_sums[1:], "tensor")

    parts = 2 if local_heads % 4 == 0 else 1
    grad_mixed, w_sums, columns, w_cols = [], [], [], w_qkv.shape[1] // parts
    for part in range(parts):
        *piece, sums = attend_backward(saved, heads_b, grad_heads, place_one, part, parts)
        *grad_heads, piece[0], dp_place = gate(*grad_heads, piece[0], dp_place)
        columns.append(sums[0])
        if w_sums:
            w_sums[-1].take(dp_place)
            w_sums[-1].send(dp_place)
            w_sums[-1].value, mlp_far, piece[near] = gate(w_sums[-1].value, mlp_far, piece[near])
        grad_mixed.append(piece)
        if part == 0:
            dp_place, *mlp_grads = gate(dp_place, *mlp_grads)
            mlp_grads = [lax.all_gather(x, "dp", axis=0, tiled=True) for x in mlp_grads]
        if part < parts - 1:
            w_part = weight_grads((n1, piece), (gm, heads_b))
            *grad_heads, w_part, dp_place = gate(*grad_heads, w_part, dp_place)
            w_sums.append(DpSum(w_part, order_a, dp_place))
    blocks = [[piece[j] for piece in grad_mixed] for j in range(groups)]
    far_sum = sum_chip(through(blocks[near:], w_qkv), "tensor")
    *far_sum, n1[0], blocks[0][0], dp_place = gate(*far_sum, n1[0], blocks[0][0], dp_place)
    norm1_far = sum_ring(far_sum, "tensor")
    last = [(n1, grad_mixed[-1])] + ([(gm, heads_b)] if parts == 1 else [])
    w_part = weight_grads(*last)
    blocks[0][0], w_part = gate(blocks[0][0], w_part)
    w_sums.append(DpSum(w_part, order_a, dp_place))
    norm1_near = through(blocks[:near], w_qkv)
    norm1_near[1] = swap(norm1_near[1], "tensor", 1)
    output = (middle + (mlp_sums[0].astype(F32) + mlp_far.astype(F32)) + b_down).astype(BF16)
    norm1_near[0], output, dp_place = gate(norm1_near[0], output, dp_place)
    if parts > 1:
        norm1_near[0] = step(w_sums[:1], dp_place, norm1_near[0])
    grad_input, in_sums = rows_call(
        norm_in_back_kernel,
        [],
        [layer_in, *norm1_near, norm1_far, grad_middle],
        [row(ln1_gain)],
        [BF16],
        2,
        "norm_in_back",
    )
    in_sums, dp_place, *mlp_grads = gate(in_sums, dp_place, *mlp_grads)
    down, up = (mlp_grads[0][: w_down.shape[0]], mlp_grads[0][w_down.shape[0] :]) if square else mlp_grads
    down, up = down.astype(F32), up.astype(F32)
    in_sums = step(w_sums, dp_place, in_sums)
    down, up, w_sums[0].value = gate(down, up, w_sums[0].value)
    while max(len(item.later) for item in w_sums) > 1:
        for item in w_sums:
            if len(item.later) > 1:
                item.take(dp_place)
                item.send(dp_place)
    uppers = jnp.stack([(dp_place & item.later[0][1]).astype(jnp.int32) for item in w_sums])
    qkv, out = whole_call(
        functools.partial(unpack_kernel, w_cols, w_out.shape[0]),
        [(w_qkv.shape, F32), (w_out.shape, F32)],
        [uppers] + [x for item in w_sums for x in (item.value, item.got)],
        "unpack",
        smem=1,
    )
    column_sums = jnp.concatenate(columns).reshape(local_heads, 3, HD)
    g_b_qv = jnp.stack([column_sums[:, 0], column_sums[:, 2]], axis=1).reshape(-1)
    total = total_of(jnp.concatenate([mid_sums.reshape(-1), in_sums.reshape(-1)]), "tensor")
    total = total_of(jnp.concatenate([total, g_b_up, g_b_qv]), "dp")
    shared = [total[n * width : (n + 1) * width] for n in range(6)]
    hidden = b_up.shape[0]
    g_b_up, g_b_qv = total[6 * width : 6 * width + hidden], total[6 * width + hidden :]
    return (
        output,
        grad_input,
        shared[4],
        shared[5],
        qkv,
        g_b_qv,
        out,
        shared[1],
        shared[2],
        shared[3],
        up,
        g_b_up,
        down,
        shared[0],
    )


def solution(mesh):
    rows, columns, flat = P("tensor", None), P(None, "tensor"), P("tensor")
    tokens = P(("dp", "tensor"), None)
    in_specs = (tokens, tokens, P("dp"), P("dp"), P(), P(), P(), columns, flat, rows, P(), P(), P(), columns, flat, rows, P())
    out_specs = (tokens, tokens, P(), P(), columns, flat, rows, P(), P(), P(), columns, flat, rows, P())
    return jax.shard_map(body, mesh=mesh, in_specs=in_specs, out_specs=out_specs, check_vma=False)
```

```python
import functools
import math
import jax
import jax.numpy as jnp
from jax import lax
from jax.sharding import PartitionSpec as P
from jax.experimental import pallas as pl
from jax.experimental.pallas import tpu as pltpu

HEADS = 16
HD = 64
LANES = 128
F32 = jnp.float32
BF16 = jnp.bfloat16
COST = pl.CostEstimate(flops=1000, transcendentals=0, bytes_accessed=1000)


def split3(x):
    hi = x.astype(BF16)
    rest = x - hi.astype(F32)
    mid = rest.astype(BF16)
    low = (rest - mid.astype(F32)).astype(BF16)
    return hi.astype(F32), mid.astype(F32), low.astype(F32)


def nt(a, b):
    return lax.dot_general(a, b, (((1,), (1,)), ((), ())), preferred_element_type=F32)


def nn(a, b):
    return jnp.dot(a, b, preferred_element_type=F32)


def at_lanes(lane, base, pairs):
    out = base
    for where, value in pairs:
        out = jnp.where(lane == where, value, out)
    return out


def key_side(span, first, length):
    pos = first + lax.broadcasted_iota(jnp.int32, (span, HD), 0)
    lane = lax.broadcasted_iota(jnp.int32, (span, HD), 1)
    low = (pos & 255).astype(F32)
    high = (pos - (pos & 255)).astype(F32)
    out = jnp.where((lane == 1) | (lane == 3) | (lane == 5), low, 0.0)
    out = jnp.where((lane == 0) | (lane == 2) | (lane == 4), high, out)
    out = jnp.where(lane == 6, jnp.where(pos < length, 0.0, -1e30), out)
    return jnp.where((lane >= 7) & (lane <= 9), 1.0, out).astype(BF16)


def slope_side(rows, slope_parts):
    lane = lax.broadcasted_iota(jnp.int32, (rows, HD), 1)
    s1, s2, s3 = slope_parts
    out = jnp.where(lane < 2, s1, jnp.where(lane < 4, s2, s3))
    return jnp.where(lane < 6, out, jnp.where(lane == 6, 1.0, 0.0)).astype(BF16)


def beside(x, extra):
    return jnp.concatenate([x, extra], axis=1)


def fwd_kernel(count, bq, place_ref, length_ref, slope_ref, *refs):
    mixed_refs, heads_refs = refs[:count], refs[count : 2 * count]
    qa_ref, ka_ref, va_ref, o_ref, keys_ref = refs[2 * count :]
    own = mixed_refs[0].shape[0]
    heads, span, _ = o_ref.shape
    lane = lax.broadcasted_iota(jnp.int32, (1, LANES), 1)
    h = pl.program_id(0)

    def rows_of(j):
        return pl.ds(pl.multiple_of((place_ref[0] ^ j) * own, own), own)

    @pl.when(h == 0)
    def _():
        for j in range(count):
            keys_ref[rows_of(j), :] = key_side(own, (place_ref[0] ^ j) * own, length_ref[0])

    ones = (lax.broadcasted_iota(jnp.int32, (own, HD), 1) < 3).astype(F32).astype(BF16)
    slopes = slope_side(own, [slope_ref[h, n] for n in range(3)])
    for head in range(heads):

        @pl.when(h == head)
        def _(base=head * 3 * HD):
            for j in range(count):
                rows = rows_of(j)
                q = mixed_refs[j][:, base : base + HD] * jnp.asarray(HD ** -0.5, BF16)
                qa_ref[0, rows, :] = beside(q, slopes)
                ka_ref[0, rows, :] = beside(mixed_refs[j][:, base + HD : base + 2 * HD], keys_ref[rows, :])
                va_ref[0, rows, :] = beside(mixed_refs[j][:, base + 2 * HD : base + 3 * HD], ones)

    for i in range(span // bq):
        rows = slice(i * bq, (i + 1) * bq)
        ext = (i + 1) * bq
        q = qa_ref[0, rows, :]
        s = nt(q, ka_ref[0, :ext, :])
        tq = lax.broadcasted_iota(jnp.int32, (bq, bq), 0)
        tk = lax.broadcasted_iota(jnp.int32, (bq, bq), 1)
        diag = jnp.where(tk <= tq, s[:, i * bq :], -3e38)
        s = jnp.concatenate([s[:, : i * bq], diag], axis=1) if i else diag
        m = jnp.max(s, axis=1, keepdims=True)
        p = jnp.exp(s - m).astype(BF16)
        o = nn(p, va_ref[0, :ext, :])
        total = o[:, HD : HD + 1]
        out = o / total
        l1, l2, l3 = split3(-(m + jnp.log(total)))
        o_ref[h, rows, :] = out.astype(BF16)
        logs = at_lanes(lane, q.astype(F32), ((71, l1), (72, l2), (73, l3)))
        qa_ref[0, rows, :] = logs.astype(BF16)

    @pl.when(h == heads - 1)
    def _():
        for j in range(count):
            heads_refs[j][...] = jnp.concatenate([o_ref[n, rows_of(j), :][:, :HD] for n in range(heads)], axis=1)


def attend_forward(mixed, place, length, slope_parts, bq=256):
    count = len(mixed)
    own = mixed[0].shape[0]
    span = own * count
    heads = mixed[0].shape[1] // (3 * HD)
    vm = pl.BlockSpec(memory_space=pltpu.VMEM)
    sm = pl.BlockSpec(memory_space=pltpu.SMEM)
    aug = jax.ShapeDtypeStruct((heads, span, LANES), BF16)
    one = pl.BlockSpec((1, span, LANES), lambda i: (i, 0, 0))
    res = pl.pallas_call(
        functools.partial(fwd_kernel, count, bq),
        grid=(heads,),
        out_shape=(jax.ShapeDtypeStruct((own, heads * HD), BF16),) * count + (aug, aug, aug),
        in_specs=[sm, sm, sm] + [vm] * count,
        out_specs=(vm,) * count + (one, one, one),
        scratch_shapes=[pltpu.VMEM((heads, span, LANES), BF16), pltpu.VMEM((span, HD), BF16)],
        compiler_params=pltpu.CompilerParams(vmem_limit_bytes=60 << 20),
        cost_estimate=COST,
        name="attend_forward",
    )(place, length, slope_parts, *mixed)
    return res[:count], res[count:]


def bwd_kernel(count, bk, bq, place_ref, qa_ref, ka_ref, va_ref, *refs):
    heads_refs, grad_refs, out_refs = refs[:count], refs[count : 2 * count], refs[2 * count : 3 * count]
    sums_ref, da_ref, dqt_ref, dk_ref, dv_ref = refs[3 * count :]
    own = heads_refs[0].shape[0]
    heads, span, _ = da_ref.shape
    h = pl.program_id(0)

    def rows_of(j):
        return pl.ds(pl.multiple_of((place_ref[0] ^ j) * own, own), own)

    @pl.when(h == 0)
    def _():
        lane = lax.broadcasted_iota(jnp.int32, (1, HD), 1)
        for j in range(count):
            for n in range(heads):
                g = grad_refs[j][:, n * HD : (n + 1) * HD]
                o = heads_refs[j][:, n * HD : (n + 1) * HD].astype(F32)
                d1, d2, d3 = split3(-jnp.sum(o * g.astype(F32), axis=1, keepdims=True))
                extra = at_lanes(lane, jnp.zeros((own, HD), F32), ((0, d1), (1, d2), (2, d3)))
                da_ref[n, rows_of(j), :] = beside(g, extra.astype(BF16))

    for j in range(span // bk):
        cols = slice(j * bk, (j + 1) * bk)
        k = ka_ref[0, cols, :]
        v = va_ref[0, cols, :]
        kt = k[:, :HD].T
        start = j * bk
        dk = jnp.zeros((bk, LANES), F32)
        dv = jnp.zeros((bk, LANES), F32)
        while start < span:
            stop = min(span, (start // bq + 1) * bq)
            q = qa_ref[0, start:stop, :]
            d = da_ref[h, start:stop, :]
            p = jnp.exp(nt(k, q))
            if start == j * bk:
                tk = lax.broadcasted_iota(jnp.int32, (bk, stop - start), 0)
                tq = lax.broadcasted_iota(jnp.int32, (bk, stop - start), 1)
                p = jnp.where(tk <= tq, p, 0.0)
            dp = nt(v, d)
            ds = (p * dp).astype(BF16)
            dv = dv + nn(p.astype(BF16), d)
            dk = dk + nn(ds, q)
            part = nn(kt, ds)
            if j == 0:
                dqt_ref[h, :, start:stop] = part
            else:
                dqt_ref[h, :, start:stop] += part
            start = stop
        dk_ref[h, cols, :] = dk
        dv_ref[h, cols, :] = dv

    @pl.when(h == heads - 1)
    def _():
        for j in range(count):
            rows = rows_of(j)
            pieces = []
            for n in range(heads):
                pieces += [dqt_ref[n, :, rows].T * (HD ** -0.5), dk_ref[n, rows, :HD], dv_ref[n, rows, :HD]]
            rounded = jnp.concatenate(pieces, axis=1).astype(BF16)
            out_refs[j][...] = rounded
            sums = jnp.sum(rounded.astype(F32), axis=0, keepdims=True)
            sums_ref[...] = sums if j == 0 else sums_ref[...] + sums


def attend_backward(saved, heads_b, grad_heads, place, part, parts, bk=256, bq=2048):
    heads, span, _ = saved[0].shape
    heads = heads // parts
    count = len(heads_b)
    own = span // count
    vm = pl.BlockSpec(memory_space=pltpu.VMEM)
    sm = pl.BlockSpec(memory_space=pltpu.SMEM)
    aug = pl.BlockSpec((1, span, LANES), lambda i: (part * heads + i, 0, 0))
    flat = pl.BlockSpec((own, heads * HD), lambda i: (0, part))
    out = pl.BlockSpec((own, heads * 3 * HD), lambda i: (0, 0))
    return pl.pallas_call(
        functools.partial(bwd_kernel, count, bk, bq),
        grid=(heads,),
        out_shape=(jax.ShapeDtypeStruct((own, heads * 3 * HD), BF16),) * count
        + (jax.ShapeDtypeStruct((1, heads * 3 * HD), F32),),
        in_specs=[sm] + [aug] * 3 + [flat] * (2 * count),
        out_specs=(out,) * count + (pl.BlockSpec((1, heads * 3 * HD), lambda i: (0, 0)),),
        scratch_shapes=[
            pltpu.VMEM((heads, span, LANES), BF16),
            pltpu.VMEM((heads, HD, span), F32),
            pltpu.VMEM((heads, span, LANES), F32),
            pltpu.VMEM((heads, span, LANES), F32),
        ],
        compiler_params=pltpu.CompilerParams(vmem_limit_bytes=60 << 20),
        cost_estimate=COST,
        name="attend_backward",
    )(place, *saved, *heads_b, *grad_heads)


def slope_table(first, count, total):
    ids = (first + jnp.arange(count, dtype=jnp.int32)).astype(F32)
    slopes = jnp.exp2(-8.0 * (ids + 1.0) / total)
    return jnp.stack(split3(slopes), axis=1)


eps = 1e-05


def whole_call(kernel, outs, ins, name, smem=0):
    vm = pl.BlockSpec(memory_space=pltpu.VMEM)
    sm = pl.BlockSpec(memory_space=pltpu.SMEM)
    return pl.pallas_call(
        kernel,
        out_shape=tuple(jax.ShapeDtypeStruct(shape, kind) for shape, kind in outs),
        in_specs=[sm] * smem + [vm] * (len(ins) - smem),
        out_specs=(vm,) * len(outs),
        compiler_params=pltpu.CompilerParams(vmem_limit_bytes=60 << 20),
        cost_estimate=COST,
        name=name,
    )(*ins)


def tn(a, b):
    return lax.dot_general(a, b, (((0,), (0,)), ((), ())), preferred_element_type=F32)


def weight_kernel(count, spots, based, *refs):
    out_ref = refs[-1]
    for n, (row, column) in enumerate(spots):
        lefts, rights = [refs[m * count : (m + 1) * count] for m in (2 * n, 2 * n + 1)]
        rows, width = lefts[0].shape[1], rights[0].shape[1]
        for top in range(0, rows, 256):
            size = min(256, rows - top)
            total = tn(lefts[0][:, top : top + size], rights[0][...])
            for left, right in zip(lefts[1:], rights[1:]):
                total = total + tn(left[:, top : top + size], right[...])
            spot = (slice(row + top, row + top + size), slice(column, column + width))
            if based:
                total = total + refs[-2][spot]
            out_ref[spot] = total.astype(out_ref.dtype)


def weight_grads(*groups, base=None, kind=BF16, stack=False):
    count = len(groups[0][0])
    ins = [x for lefts, rights in groups for x in list(lefts) + list(rights)]
    spots, row, column = [], 0, 0
    for lefts, rights in groups:
        spots.append((row, column))
        row, column = (row + lefts[0].shape[1], 0) if stack else (0, column + rights[0].shape[1])
    last = groups[-1]
    shape = (spots[-1][0] + last[0][0].shape[1], spots[-1][1] + last[1][0].shape[1])
    if base is not None:
        ins.append(base)
    kernel = functools.partial(weight_kernel, count, spots, base is not None)
    return whole_call(kernel, [(shape, kind)], ins, "weight_grads")[0]


def through_kernel(count, parts, w_ref, *refs):
    outs = refs[count * parts :]
    width = w_ref.shape[1] // parts
    for j in range(count):
        total = nt(refs[j * parts][...], w_ref[:, :width])
        for p in range(1, parts):
            total = total + nt(refs[j * parts + p][...], w_ref[:, p * width : (p + 1) * width])
        outs[j][...] = total.astype(BF16)


def through(blocks, w):
    count, parts = len(blocks), len(blocks[0])
    shape = (blocks[0][0].shape[0], w.shape[0])
    ins = [w] + [x for block in blocks for x in block]
    return list(whole_call(functools.partial(through_kernel, count, parts), [(shape, BF16)] * count, ins, "through"))


def unit_of(values):
    centre = jnp.mean(values, axis=-1, keepdims=True)
    shifted = values - centre
    factor = lax.rsqrt(jnp.mean(shifted * shifted, axis=-1, keepdims=True) + eps)
    return shifted * factor, factor


def rows_call(kernel, scalars, rows_in, whole_in, kinds, sums, name, tile=256):
    own, width = rows_in[0].shape
    tile = min(tile, own)

    def spec(x):
        return pl.BlockSpec((tile, x.shape[1]), lambda i: (i, 0))

    whole = [pl.BlockSpec(x.shape, lambda i: (0, 0)) for x in whole_in]
    outs = [jax.ShapeDtypeStruct((own, width), kind) for kind in kinds]
    out_specs = [pl.BlockSpec((tile, width), lambda i: (i, 0)) for _ in kinds]
    if sums:
        outs.append(jax.ShapeDtypeStruct((sums, width), F32))
        out_specs.append(pl.BlockSpec((sums, width), lambda i: (0, 0)))
    return pl.pallas_call(
        kernel,
        grid=(own // tile,),
        out_shape=tuple(outs),
        in_specs=[pl.BlockSpec(memory_space=pltpu.SMEM)] * len(scalars) + [spec(x) for x in rows_in] + whole,
        out_specs=tuple(out_specs),
        compiler_params=pltpu.CompilerParams(vmem_limit_bytes=60 << 20),
        cost_estimate=COST,
        name=name,
    )(*scalars, *rows_in, *whole_in)


def add_rows(sums_ref, rows):
    new = jnp.concatenate(rows, axis=0)
    first = pl.program_id(0) == 0
    sums_ref[...] = jnp.where(first, new, sums_ref[...] + new)


def norm_in_kernel(x_ref, gain_ref, bias_ref, out_ref):
    unit, _ = unit_of(x_ref[...].astype(F32))
    out_ref[...] = (unit * gain_ref[...] + bias_ref[...]).astype(BF16)


def three(a_ref, b_ref, far_ref):
    return (a_ref[...].astype(F32) + b_ref[...].astype(F32)) + far_ref[...].astype(F32)


def norm_mid_kernel(x_ref, a_ref, b_ref, far_ref, bo_ref, gain_ref, bias_ref, mid_ref, out_ref):
    mid = x_ref[...].astype(F32) + three(a_ref, b_ref, far_ref) + bo_ref[...]
    mid_ref[...] = mid
    unit, _ = unit_of(mid)
    out_ref[...] = (unit * gain_ref[...] + bias_ref[...]).astype(BF16)


def back_of(grad, values, gain):
    unit, factor = unit_of(values)
    d = grad * gain
    inner = jnp.mean(d * unit, axis=-1, keepdims=True)
    sums = [jnp.sum(grad * unit, axis=0, keepdims=True), jnp.sum(grad, axis=0, keepdims=True)]
    return factor * (d - jnp.mean(d, axis=-1, keepdims=True) - unit * inner), sums


def norm_mid_back_kernel(
    first_ref, length_ref, weight_ref, mid_ref, a_ref, b_ref, far_ref, top_ref, gain_ref, grad_ref, rounded_ref, sums_ref
):
    back, sums = back_of(three(a_ref, b_ref, far_ref), mid_ref[...], gain_ref[...])
    rows = top_ref.shape[0]
    pos = first_ref[0] + pl.program_id(0) * rows + lax.broadcasted_iota(jnp.int32, (rows, 1), 0)
    top = top_ref[...].astype(F32) * jnp.where(pos < length_ref[0], weight_ref[0], 0.0)
    grad_mid = top + back
    grad_ref[...] = grad_mid
    rounded_ref[...] = grad_mid.astype(BF16)
    add_rows(sums_ref, [jnp.sum(top, axis=0, keepdims=True), jnp.sum(grad_mid, axis=0, keepdims=True)] + sums)


def norm_in_back_kernel(x_ref, a_ref, b_ref, far_ref, mid_ref, gain_ref, grad_ref, sums_ref):
    back, sums = back_of(three(a_ref, b_ref, far_ref), x_ref[...].astype(F32), gain_ref[...])
    grad_ref[...] = (mid_ref[...] + back).astype(BF16)
    add_rows(sums_ref, sums)


def unpack_kernel(cols, heads_cols, upper_ref, *refs):
    qkv_ref, out_ref = refs[-2:]
    for p in range(len(refs) // 2 - 1):
        sent, got = refs[2 * p][...].astype(F32), refs[2 * p + 1][...].astype(F32)
        rows = sent.shape[0]
        upper = upper_ref[p] != 0
        for n, x in enumerate((jnp.where(upper, got, sent), jnp.where(upper, sent, got))):
            spot = slice(n * rows, (n + 1) * rows)
            qkv_ref[spot, p * cols : (p + 1) * cols] = x[:, :cols]
            if p == 0:
                out_ref[:, spot] = x[:, cols : cols + heads_cols].T


def mlp_kernel(count, tile, w_up_ref, w_down_ref, b_up_ref, *refs):
    n2_refs, top_refs, act_refs, pre_refs, back_refs = [refs[n * count : (n + 1) * count] for n in range(5)]
    sums_ref = refs[-1]
    sums_ref[...] = jnp.zeros_like(sums_ref)
    root = (2.0 / math.pi) ** 0.5

    for j in range(count):

        def step(i, carry):
            rows = pl.ds(pl.multiple_of(i * tile, tile), tile)
            pre = nn(n2_refs[j][rows, :], w_up_ref[...]) + b_up_ref[...]
            grad = nt(top_refs[j][rows, :], w_down_ref[...])
            square = pre * pre
            tanh = jnp.tanh(pre * (root + (root * 0.044715) * square))
            half = 0.5 + 0.5 * tanh
            act_refs[j][rows, :] = (pre * half).astype(BF16)
            slope = half + (0.5 * pre) * (1.0 - tanh * tanh) * (root + (root * 0.134145) * square)
            inner = (grad * slope).astype(BF16)
            pre_refs[j][rows, :] = inner
            sums_ref[...] += jnp.sum(inner.astype(F32), axis=0, keepdims=True)
            back_refs[j][rows, :] = nt(inner, w_up_ref[...]).astype(BF16)
            return carry

        lax.fori_loop(0, n2_refs[j].shape[0] // tile, step, 0)


def mlp_both(n2, top, w_up, w_down, b_up):
    count = len(n2)
    own, width = n2[0].shape
    hidden = w_up.shape[1]
    vm = pl.BlockSpec(memory_space=pltpu.VMEM)
    inner = jax.ShapeDtypeStruct((own, hidden), BF16)
    outer = jax.ShapeDtypeStruct((own, width), BF16)
    res = pl.pallas_call(
        functools.partial(mlp_kernel, count, min(own, 256)),
        out_shape=(inner,) * (2 * count) + (outer,) * count + (jax.ShapeDtypeStruct((1, hidden), F32),),
        in_specs=[vm] * (3 + 2 * count),
        out_specs=(vm,) * (3 * count + 1),
        compiler_params=pltpu.CompilerParams(vmem_limit_bytes=60 << 20),
        cost_estimate=COST,
        name="mlp_both",
    )(w_up, w_down, b_up.reshape(1, -1), *n2, *top)
    return list(res[:count]), list(res[count : 2 * count]), list(res[2 * count : -1]), res[-1][0]


def swap(x, axis, bit):
    return lax.ppermute(x, axis, [(i, i ^ bit) for i in range(lax.axis_size(axis))])


def bits_of(axis):
    return [1 << n for n in range(lax.axis_size(axis).bit_length() - 1)]


def gather_ring(x, axis):
    blocks = {0: x}
    for bit in bits_of(axis)[1:]:
        blocks.update({j ^ bit: swap(b, axis, bit) for j, b in list(blocks.items())})
    return [blocks[j] for j in sorted(blocks) if j]


def gather_chip(blocks, axis):
    return [x for b in blocks for x in (b, swap(b, axis, 1))]


def sum_chip(parts, axis):
    return [
        (parts[j].astype(F32) + swap(parts[j + 1], axis, 1).astype(F32)).astype(BF16)
        for j in range(0, len(parts), 2)
    ]


def sum_ring(parts, axis):
    parts = {2 * (n + 1): x for n, x in enumerate(parts)}
    for bit in bits_of(axis)[1:]:
        kept = {}
        for j in sorted({j & ~bit for j in parts}):
            got = swap(parts[j | bit].astype(BF16), axis, bit)
            kept[j] = got.astype(F32) + parts[j].astype(F32) if j in parts else got
        parts = kept
    return parts[0]


def total_of(x, axis):
    for bit in bits_of(axis):
        x = x + swap(x, axis, bit)
    return x


def gate(*values):
    return lax.optimization_barrier(values)


def half_of(x, upper):
    rows = x.shape[0] // 2
    return lax.dynamic_slice_in_dim(x, jnp.where(upper, rows, 0), rows, 0)


class DpSum:
    def __init__(self, x, order, place):
        self.value, self.got, self.later = x, None, [(True, b) for b in order] + [(False, b) for b in order[::-1]]
        self.send(place)

    def send(self, place):
        halving, bit = self.later[0]
        send = half_of(self.value, (place & bit) == 0).astype(BF16) if halving else self.value
        self.got = swap(send, "dp", bit)

    def take(self, place):
        halving, bit = self.later.pop(0)
        upper = (place & bit) != 0
        x, got = self.value, self.got
        if halving:
            x = half_of(x, upper).astype(F32) + got.astype(F32)
            if not self.later[0][0]:
                x = x.astype(BF16)
        else:
            x = jnp.concatenate([jnp.where(upper, got, x), jnp.where(upper, x, got)], axis=0)
        self.value = x

    def result(self, place):
        while len(self.later) > 1:
            self.take(place)
            self.send(place)
        self.take(place)
        return self.value.astype(F32)


def step(items, place, critical):
    for item in items:
        item.take(place)
        item.send(place)
    critical, *values = gate(critical, *[item.value for item in items])
    for item, value in zip(items, values):
        item.value = value
    return critical


def body(
    layer_in,
    cotangent,
    lengths,
    languages,
    lang_weight,
    ln1_gain,
    ln1_bias,
    w_qkv,
    b_qv,
    w_out,
    b_out,
    ln2_gain,
    ln2_bias,
    w_up,
    b_up,
    w_down,
    b_down,
):
    groups = lax.axis_size("tensor")
    place = lax.axis_index("tensor")
    place_one = place.astype(jnp.int32).reshape(1)
    own_rows = layer_in.shape[0]
    local_heads = w_out.shape[0] // HD
    dp_place = lax.axis_index("dp")
    order_a = bits_of("dp")
    order_b = order_a[1:] + order_a[:1]

    width = layer_in.shape[1]

    def row(x):
        return x.reshape(1, -1)

    (n1_own,) = rows_call(norm_in_kernel, [], [layer_in], [row(ln1_gain), row(ln1_bias)], [BF16], 0, "norm_in")
    n1_far = gather_ring(n1_own, "tensor")
    n1 = gather_chip([n1_own], "tensor")
    near = len(n1)

    positions = place * own_rows + jnp.arange(own_rows, dtype=jnp.int32)
    weight = jnp.sum(jnp.where(jnp.arange(lang_weight.shape[0]) == languages[0], lang_weight, 0.0))
    live = jnp.where(positions < lengths[0], weight, 0.0)
    top_own = (cotangent.astype(F32) * live[:, None]).astype(BF16)

    pairs = b_qv.reshape(local_heads, 2, HD)
    bias_three = jnp.stack([pairs[:, 0], jnp.zeros_like(pairs[:, 0]), pairs[:, 1]], axis=1).reshape(1, -1)

    def project(x):
        return (nn(x, w_qkv) + bias_three).astype(BF16)

    mixed = [project(x) for x in n1]
    top_own, *rest = gate(top_own, *mixed, *n1_far)
    mixed, n1_far = rest[:near], rest[near:]
    top_far = gather_ring(top_own, "tensor")
    n1 += gather_chip(n1_far, "tensor")
    mixed += [project(x) for x in n1[near:]]
    slope_parts = slope_table(place * local_heads, local_heads, HEADS)
    heads_b, saved = attend_forward(mixed, place_one, lengths, slope_parts)
    rest = gate(*heads_b, *top_far)
    heads_b, top_far = list(rest[:groups]), list(rest[groups:])

    parts = [nn(x, w_out).astype(BF16) for x in heads_b[near:]]
    far_sum = sum_chip(parts, "tensor")
    rest = gate(*heads_b[:near], *far_sum)
    heads_b[:near], far_sum = rest[:near], rest[near:]
    attn_far = sum_ring(far_sum, "tensor")
    attn_near = [nn(x, w_out).astype(BF16) for x in heads_b[:near]]
    attn_near[1] = swap(attn_near[1], "tensor", 1)
    top = gather_chip([top_own] + top_far, "tensor")
    middle, n2_own = rows_call(
        norm_mid_kernel,
        [],
        [layer_in, *attn_near, attn_far],
        [row(b_out), row(ln2_gain), row(ln2_bias)],
        [F32, BF16],
        0,
        "norm_mid",
    )
    n2_far = gather_ring(n2_own, "tensor")
    n2 = gather_chip([n2_own], "tensor")

    active, grad_pre, back, up_sums = mlp_both(n2, top[:near], w_up, w_down, b_up)
    square = w_up.shape[0] == w_up.shape[1]

    def mlp_weight_grads(lows, highs, **more):
        if square:
            return [weight_grads(lows, highs, stack=True, **more)]
        return [weight_grads(lows, **more), weight_grads(highs, **more)]

    near_sums = mlp_weight_grads((active, top[:near]), (n2, grad_pre), kind=F32)
    rest = gate(*back, *n2_far, *near_sums)
    back, n2_far, near_sums = list(rest[:near]), list(rest[near : -len(near_sums)]), rest[-len(near_sums) :]
    n2 += gather_chip(n2_far, "tensor")
    far_active, far_pre, far_back, far_sums = mlp_both(n2[near:], top[near:], w_up, w_down, b_up)
    g_b_up = up_sums + far_sums
    far_sum = sum_chip(far_back, "tensor")
    rest = gate(*far_sum, *far_active, *far_pre, *back, *active)
    far_sum, rest = list(rest[: len(far_sum)]), list(rest[len(far_sum) :])
    count = groups - near
    far_active, far_pre, back, active = rest[:count], rest[count : 2 * count], rest[2 * count : -near], rest[-near:]
    norm2_far = sum_ring(far_sum, "tensor")
    groups_of_far = (far_active, top[near:]), (n2[near:], far_pre)
    if square:
        mlp_grads = [weight_grads(*groups_of_far, base=near_sums[0], stack=True)]
    else:
        mlp_grads = [weight_grads(g, base=base) for g, base in zip(groups_of_far, near_sums)]
    *mlp_grads, back[0] = gate(*mlp_grads, back[0])
    mlp_grads = [lax.psum_scatter(x, "dp", scatter_dimension=0, tiled=True) for x in mlp_grads]
    active += far_active
    back[1] = swap(back[1], "tensor", 1)
    grad_middle, gm_own, mid_sums = rows_call(
        norm_mid_back_kernel,
        [(place * own_rows).astype(jnp.int32).reshape(1), lengths, weight.reshape(1)],
        [middle, *back, norm2_far, cotangent],
        [row(ln2_gain)],
        [F32, BF16],
        4,
        "norm_mid_back",
    )
    *active, gm_own, dp_place = gate(*active, gm_own, dp_place)
    gm_far = gather_ring(gm_own, "tensor")
    gm = gather_chip([gm_own], "tensor")

    mlp_sums = sum_chip([nn(x, w_down).astype(BF16) for x in active], "tensor")
    grad_heads = through([[x] for x in gm], w_out)
    rest = gate(*gm_far, *grad_heads, *mlp_sums, dp_place)
    dp_place = rest[-1]
    count = len(gm_far)
    gm_far, grad_heads, mlp_sums = list(rest[:count]), list(rest[count : count + near]), rest[count + near : -1]
    gm += gather_chip(gm_far, "tensor")
    grad_heads += through([[x] for x in gm[near:]], w_out)
    mlp_far = sum_ring(mlp_sums[1:], "tensor")

    parts = 2 if local_heads % 4 == 0 else 1
    grad_mixed, w_sums, columns, w_cols = [], [], [], w_qkv.shape[1] // parts
    for part in range(parts):
        *piece, sums = attend_backward(saved, heads_b, grad_heads, place_one, part, parts)
        *grad_heads, piece[0], dp_place = gate(*grad_heads, piece[0], dp_place)
        columns.append(sums[0])
        if w_sums:
            w_sums[-1].take(dp_place)
            w_sums[-1].send(dp_place)
            w_sums[-1].value, mlp_far, piece[near] = gate(w_sums[-1].value, mlp_far, piece[near])
        grad_mixed.append(piece)
        if part == 0:
            dp_place, *mlp_grads = gate(dp_place, *mlp_grads)
            mlp_grads = [lax.all_gather(x, "dp", axis=0, tiled=True) for x in mlp_grads]
        if part < parts - 1:
            w_part = weight_grads((n1, piece), (gm, heads_b))
            *grad_heads, w_part, dp_place = gate(*grad_heads, w_part, dp_place)
            w_sums.append(DpSum(w_part, order_a, dp_place))
    blocks = [[piece[j] for piece in grad_mixed] for j in range(groups)]
    far_sum = sum_chip(through(blocks[near:], w_qkv), "tensor")
    *far_sum, n1[0], blocks[0][0], dp_place = gate(*far_sum, n1[0], blocks[0][0], dp_place)
    norm1_far = sum_ring(far_sum, "tensor")
    last = [(n1, grad_mixed[-1])] + ([(gm, heads_b)] if parts == 1 else [])
    w_part = weight_grads(*last)
    blocks[0][0], w_part = gate(blocks[0][0], w_part)
    w_sums.append(DpSum(w_part, order_a, dp_place))
    norm1_near = through(blocks[:near], w_qkv)
    norm1_near[1] = swap(norm1_near[1], "tensor", 1)
    norm1_far, norm1_near[0], dp_place = gate(norm1_far, norm1_near[0], dp_place)
    grad_input, in_sums = rows_call(
        norm_in_back_kernel,
        [],
        [layer_in, *norm1_near, norm1_far, grad_middle],
        [row(ln1_gain)],
        [BF16],
        2,
        "norm_in_back",
    )
    in_sums, dp_place, mlp_far, *mlp_grads = gate(in_sums, dp_place, mlp_far, *mlp_grads)
    output = (middle + (mlp_sums[0].astype(F32) + mlp_far.astype(F32)) + b_down).astype(BF16)
    down, up = (mlp_grads[0][: w_down.shape[0]], mlp_grads[0][w_down.shape[0] :]) if square else mlp_grads
    down, up = down.astype(F32), up.astype(F32)
    in_sums = step(w_sums, dp_place, in_sums)
    down, up, w_sums[0].value = gate(down, up, w_sums[0].value)
    while max(len(item.later) for item in w_sums) > 1:
        for item in w_sums:
            if len(item.later) > 1:
                item.take(dp_place)
                item.send(dp_place)
    uppers = jnp.stack([(dp_place & item.later[0][1]).astype(jnp.int32) for item in w_sums])
    qkv, out = whole_call(
        functools.partial(unpack_kernel, w_cols, w_out.shape[0]),
        [(w_qkv.shape, F32), (w_out.shape, F32)],
        [uppers] + [x for item in w_sums for x in (item.value, item.got)],
        "unpack",
        smem=1,
    )
    column_sums = jnp.concatenate(columns).reshape(local_heads, 3, HD)
    g_b_qv = jnp.stack([column_sums[:, 0], column_sums[:, 2]], axis=1).reshape(-1)
    total = total_of(jnp.concatenate([mid_sums.reshape(-1), in_sums.reshape(-1)]), "tensor")
    total = total_of(jnp.concatenate([total, g_b_up, g_b_qv]), "dp")
    shared = [total[n * width : (n + 1) * width] for n in range(6)]
    hidden = b_up.shape[0]
    g_b_up, g_b_qv = total[6 * width : 6 * width + hidden], total[6 * width + hidden :]
    return (
        output,
        grad_input,
        shared[4],
        shared[5],
        qkv,
        g_b_qv,
        out,
        shared[1],
        shared[2],
        shared[3],
        up,
        g_b_up,
        down,
        shared[0],
    )


def solution(mesh):
    rows, columns, flat = P("tensor", None), P(None, "tensor"), P("tensor")
    tokens = P(("dp", "tensor"), None)
    in_specs = (tokens, tokens, P("dp"), P("dp"), P(), P(), P(), columns, flat, rows, P(), P(), P(), columns, flat, rows, P())
    out_specs = (tokens, tokens, P(), P(), columns, flat, rows, P(), P(), P(), columns, flat, rows, P())
    return jax.shard_map(body, mesh=mesh, in_specs=in_specs, out_specs=out_specs, check_vma=False)
```
